256 devices in a mesh: dp: 4 (over x), expert: 64 (over y, z, core).
Axes of the slice: x: 4, y: 4, z: 8, core: 2. Of those that a mesh axis runs over, the one named last changes fastest.
Arguments:
- frames: bfloat16 [32768, 1024], P(('dp', 'expert')), may hold values from -6 to 6
- lengths: int32 [256], P(('dp', 'expert')), may hold values from 64 to 128
- expert_ids: int32 [32768, 2], P(('dp', 'expert')), may hold values from 0 to 63, all different within a row
- conv_in: bfloat16 [1024, 2048], P(('dp', 'expert')), may hold values from -0.1875 to 0.1875
- depthwise: bfloat16 [1024, 31], P(('dp', 'expert')), may hold values from -1 to 1
- router: bfloat16 [1024, 64], P(('dp', 'expert')), may hold values from -0.1875 to 0.1875
- w_in: bfloat16 [64, 1024, 4096], P('expert', None, 'dp'), may hold values from -0.1875 to 0.1875
- w_out: bfloat16 [64, 4096, 1024], P('expert', 'dp'), may hold values from -0.09375 to 0.09375
- out_grad: bfloat16 [32768, 1024], P(('dp', 'expert')), may hold values from -6 to 6
Outputs:
- layer_out: bfloat16 [32768, 1024], P(('dp', 'expert'))
- frames_grad: bfloat16 [32768, 1024], P(('dp', 'expert'))
- conv_in_grad: float32 [1024, 2048], P(('dp', 'expert'))
- depthwise_grad: float32 [1024, 31], P(('dp', 'expert'))
- router_grad: float32 [1024, 64], P(('dp', 'expert'))
- w_in_grad: bfloat16 [64, 1024, 4096], P('expert', None, 'dp')
- w_out_grad: bfloat16 [64, 4096, 1024], P('expert', 'dp')
The draws below stay inside these ranges and needn't reach their ends.
Inputs may be any that keep to these rules, and one draw needn't show every extreme that they name: `expert_ids`: each frame names 2 different experts, and every expert is named by some frame.
All inputs are finite; a program needn't handle non-finite values.
Results may differ from the reference program's by a relative error of at most 0.019.
Values may be sent and summed in bfloat16 or wider, within the bound.
A program may use at most 128 MiB of HBM per device.

```python
from functools import partial
import jax
import jax.numpy as jnp
from jax import lax

D = 1024
FF = 4096
TOP = 2
KERNEL = 31
TOK_DEV = 128
EXPERTS = 64
CAP = 4
UTTS = 256
FRAMES = 32768
N_DP = 4
N_EXPERT = 64


def touch_ends(values, key, low, largest):
    dims = values.shape
    spot = [jax.random.randint(jax.random.fold_in(key, axis), (), 0, dims[axis]) for axis in range(len(dims))]
    values = values.at[tuple(spot)].set(low)
    longest = dims.index(max(dims))
    spot[longest] = (spot[longest] + 1) % dims[longest]
    return values.at[tuple(spot)].set(largest)


def block_levels(own_key, extent, shards, least, largest):
    factor_of, own = 1.0, jax.random.fold_in(own_key, 6)
    for dim, parts in shards:
        steps = jnp.exp(jax.random.uniform(jax.random.fold_in(own, dim), (parts,), jnp.float32, least / len(shards), largest / len(shards)))
        factor_of = factor_of * jnp.repeat(steps, extent[dim] // parts).reshape([-1 if axis == dim else 1 for axis in range(len(extent))])
    return factor_of


def distinct(stream_key, rows, amount, top, lift):
    order = jax.random.permutation(jax.random.fold_in(stream_key, 1), amount)
    favour = order
    for power in range(3):
        favour = favour * favour // amount
    favour = favour * lift // amount
    tickets = jax.random.randint(jax.random.fold_in(stream_key, 2), (rows, amount), 0, 4096) + favour
    fixed_rows = jax.random.permutation(jax.random.fold_in(stream_key, 3), rows)[jnp.arange(amount) % rows]
    tickets = jnp.where(jnp.arange(rows)[:, None] == fixed_rows[None, :], 1 << 14, tickets)
    score = tickets * amount + jnp.arange(amount)
    return lax.top_k(score.astype(jnp.int32), top)[1].astype(jnp.int32)


def normal_values(rng, dims, spread, reach, cuts=(), kind=jnp.bfloat16):
    result = jax.random.normal(rng, dims, jnp.float32) * spread
    if len(cuts) > 0:
        result = block_levels(rng, dims, cuts, -0.22, 0.18) * result
    return jnp.clip(result, min=-reach, max=reach).astype(kind)


def setup_inputs(seed: int = 0) -> dict:
    seeds = jax.random.split(jax.random.key(seed), 10)
    frames = normal_values(seeds[0], (FRAMES, D), 1.0, 6.0, ((0, 256),))
    lengths = touch_ends(jax.random.randint(seeds[1], (UTTS,), TOK_DEV // 2, TOK_DEV + 1), jax.random.fold_in(seeds[1], 1), TOK_DEV // 2, TOK_DEV).astype(jnp.int32)
    expert_ids = distinct(seeds[2], FRAMES, EXPERTS, TOP, 512)
    conv_in = normal_values(seeds[3], (D, 2 * D), D ** -0.5, 0.1875, ((0, 256),))
    depthwise = normal_values(seeds[4], (D, KERNEL), KERNEL ** -0.5, 1.0, ((0, 256),))
    router = normal_values(seeds[5], (D, EXPERTS), D ** -0.5, 0.1875, ((0, 256),))
    w_in = normal_values(seeds[6], (EXPERTS, D, FF), D ** -0.5, 0.1875, ((0, 64), (2, 4)))
    w_out = normal_values(seeds[7], (EXPERTS, FF, D), FF ** -0.5, 0.09375, ((0, 64), (1, 4)))
    out_grad = normal_values(seeds[8], (FRAMES, D), 1.0, 6.0, ((0, 256),))
    return dict(frames=frames, lengths=lengths, expert_ids=expert_ids, conv_in=conv_in, depthwise=depthwise, router=router, w_in=w_in, w_out=w_out, out_grad=out_grad)


EPSILON = 1e-05

def swish_of(values):
    return values * jax.nn.sigmoid(values)

def swish_slope(values):
    sigmoid_v = jax.nn.sigmoid(values)
    return sigmoid_v * (1.0 + values * (1.0 - sigmoid_v))

def normalize(values):
    center = values - lax.optimization_barrier(jnp.mean(values, axis=-1, keepdims=True))
    inv_scale = lax.rsqrt(lax.optimization_barrier(jnp.mean(center * center, axis=-1, keepdims=True)) + EPSILON)
    return (center * inv_scale, inv_scale)

def norm_backward(upstream, centred, inv_scale):
    first_mean = lax.optimization_barrier(jnp.mean(upstream, axis=-1, keepdims=True))
    second_mean = lax.optimization_barrier(jnp.mean(upstream * centred, axis=-1, keepdims=True))
    return inv_scale * (upstream - first_mean - centred * second_mean)

def pad_time(signal, half_width):
    widths = ((0, 0),) * (signal.ndim - 2) + ((half_width, half_width), (0, 0))
    return jnp.pad(signal, widths)

def depth_apply(signal, tap_rows, half_width):
    length = signal.shape[-2]
    padded = pad_time(signal, half_width)
    summed = jnp.zeros(signal.shape, jnp.float32)
    for tap_index in range(tap_rows.shape[0]):
        piece = lax.slice_in_dim(padded, tap_index, tap_index + length, axis=signal.ndim - 2)
        summed = summed + tap_rows[tap_index] * piece
    return summed

def depth_transpose(upstream, tap_rows, half_width):
    length = upstream.shape[-2]
    padded = pad_time(upstream, half_width)
    summed = jnp.zeros(upstream.shape, jnp.float32)
    for tap_index in range(tap_rows.shape[0]):
        begin = 2 * half_width - tap_index
        piece = lax.slice_in_dim(padded, begin, begin + length, axis=upstream.ndim - 2)
        summed = summed + tap_rows[tap_index] * piece
    return summed

def depth_taps_grad(upstream, signal, half_width):
    length = signal.shape[-2]
    padded = pad_time(signal, half_width)
    reduce_axes = tuple(range(signal.ndim - 1))
    rows_list = []
    for tap_index in range(2 * half_width + 1):
        piece = lax.slice_in_dim(padded, tap_index, tap_index + length, axis=signal.ndim - 2)
        rows_list.append(lax.optimization_barrier(jnp.sum(upstream * piece, axis=reduce_axes)))
    return jnp.stack(rows_list, axis=0)

def routing(choices, length, experts, capacity):
    tokens, top_count = choices.shape
    usable = jnp.arange(tokens, dtype=jnp.int32) < length
    flat_ids = choices.reshape(-1)
    live = jnp.repeat(usable, top_count)
    onehot = (flat_ids[:, None] == jnp.arange(experts, dtype=jnp.int32)[None, :]) & live[:, None]
    onehot_int = onehot.astype(jnp.int32)
    before = (jnp.cumsum(onehot_int, axis=0) - onehot_int).astype(jnp.int32)
    position = lax.optimization_barrier(jnp.sum(jnp.where(onehot, before, 0), axis=1)).astype(jnp.int32)
    kept_rows = live & (position < capacity)
    slot_total = experts * capacity
    slot_index = jnp.where(kept_rows, flat_ids * capacity + position, slot_total).astype(jnp.int32)
    match = slot_index[None, :] == jnp.arange(slot_total, dtype=jnp.int32)[:, None]
    filled = jnp.any(match, axis=1)
    source = lax.optimization_barrier(jnp.sum(jnp.where(match, jnp.arange(tokens * top_count, dtype=jnp.int32)[None, :], 0), axis=1)).astype(jnp.int32)
    return (usable, kept_rows, jnp.minimum(slot_index, slot_total - 1).astype(jnp.int32), filled, source)

def forward_expert(operands):
    slot_rows, inner, outer = operands
    hidden = jnp.dot(slot_rows, inner, preferred_element_type=jnp.float32)
    active = swish_of(hidden).astype(jnp.bfloat16)
    block_width = FF // N_DP
    summed = jnp.zeros((slot_rows.shape[0], outer.shape[1]), jnp.float32)
    for block_index in range(N_DP):
        lower = block_index * block_width
        partial_rows = jnp.dot(active[:, lower:lower + block_width], outer[lower:lower + block_width], preferred_element_type=jnp.float32).astype(jnp.bfloat16)
        partial_rows = lax.optimization_barrier(partial_rows)
        summed = summed + partial_rows.astype(jnp.float32)
    return summed.astype(jnp.bfloat16)

def backward_expert(operands):
    slot_rows, slot_cot, inner, outer = operands
    hidden = jnp.dot(slot_rows, inner, preferred_element_type=jnp.float32)
    active = swish_of(hidden).astype(jnp.bfloat16)
    act_grad = jnp.dot(slot_cot, outer.T, preferred_element_type=jnp.float32)
    pre_grad = (act_grad * swish_slope(hidden)).astype(jnp.bfloat16)
    outer_grad = jnp.dot(active.T, slot_cot, preferred_element_type=jnp.float32).astype(jnp.bfloat16)
    inner_grad = jnp.dot(slot_rows.T, pre_grad, preferred_element_type=jnp.float32).astype(jnp.bfloat16)
    block_width = FF // N_DP
    summed = jnp.zeros(slot_rows.shape, jnp.float32)
    for block_index in range(N_DP):
        lower = block_index * block_width
        partial_rows = jnp.dot(pre_grad[:, lower:lower + block_width], inner[:, lower:lower + block_width].T, preferred_element_type=jnp.float32).astype(jnp.bfloat16)
        partial_rows = lax.optimization_barrier(partial_rows)
        summed = summed + partial_rows.astype(jnp.float32)
    return (inner_grad, outer_grad, summed.astype(jnp.bfloat16))

def to_experts(buffers, utterances):
    grouped = buffers.reshape(utterances, EXPERTS, CAP, D)
    return jnp.transpose(grouped, (1, 0, 2, 3)).reshape(EXPERTS, utterances * CAP, D)

def from_experts(rows_all, utterances):
    grouped = rows_all.reshape(EXPERTS, utterances, CAP, D)
    return jnp.transpose(grouped, (1, 0, 2, 3)).reshape(utterances, EXPERTS * CAP, D)

def reference(frames, lengths, expert_ids, conv_in, depthwise, router, w_in, w_out, out_grad):
    utterances = N_DP * N_EXPERT
    half_width = (KERNEL - 1) // 2
    choices = expert_ids.reshape(utterances, TOK_DEV, TOP)
    usable, kept_rows, slot_index, filled, source = jax.vmap(partial(routing, experts=EXPERTS, capacity=CAP))(choices, lengths)
    frame_mask = usable.astype(jnp.float32)[..., None]
    frame_wide = frames.astype(jnp.float32).reshape(utterances, TOK_DEV, D)
    centred, inv_scale = normalize(frame_wide)
    normed = centred.astype(jnp.bfloat16)
    pointwise = jnp.dot(normed.reshape(-1, D), conv_in, preferred_element_type=jnp.float32).reshape(utterances, TOK_DEV, 2 * D)
    value_half = pointwise[..., :D]
    gate_sig = jax.nn.sigmoid(pointwise[..., D:])
    gated = value_half * gate_sig * frame_mask
    tap_rows = depthwise.astype(jnp.float32).T
    conv_sum = depth_apply(gated, tap_rows, half_width)
    mixed_rows = (frame_wide + swish_of(conv_sum) * frame_mask).astype(jnp.bfloat16)
    logits = jnp.dot(mixed_rows.reshape(-1, D), router, preferred_element_type=jnp.float32).reshape(utterances, TOK_DEV, EXPERTS)
    onehots = (choices[..., None] == jnp.arange(EXPERTS, dtype=jnp.int32)).astype(jnp.float32)
    chosen = lax.optimization_barrier(jnp.sum(logits[:, :, None, :] * onehots, axis=-1))
    scores = jax.nn.sigmoid(chosen)
    score_sum = lax.optimization_barrier(jnp.sum(scores, axis=-1, keepdims=True))
    weights = scores / score_sum
    kept_wide = kept_rows.reshape(utterances, TOK_DEV, TOP).astype(jnp.float32)
    frame_of = (source // TOP).astype(jnp.int32)
    send_rows = jnp.take_along_axis(mixed_rows, frame_of[..., None], axis=1)
    send_rows = jnp.where(filled[..., None], send_rows, jnp.zeros((), jnp.bfloat16))
    slots_all = to_experts(send_rows, utterances)
    expert_out = lax.map(forward_expert, (slots_all, w_in, w_out))
    returned = from_experts(expert_out, utterances)
    picked = jnp.take_along_axis(returned, slot_index[..., None], axis=1).reshape(utterances, TOK_DEV, TOP, D)
    picked_wide = picked.astype(jnp.float32) * kept_wide[..., None]
    layer_out = (mixed_rows.astype(jnp.float32) + lax.optimization_barrier(jnp.sum(weights[..., None] * picked_wide, axis=2))).astype(jnp.bfloat16)
    grad_wide = out_grad.astype(jnp.float32).reshape(utterances, TOK_DEV, D)
    weight_grad = lax.optimization_barrier(jnp.sum(grad_wide[:, :, None, :] * picked_wide, axis=-1))
    mean_term = lax.optimization_barrier(jnp.sum(weight_grad * weights, axis=-1, keepdims=True))
    chosen_grad = (weight_grad - mean_term) / score_sum * scores * (1.0 - scores)
    logit_grad = lax.optimization_barrier(jnp.sum(chosen_grad[..., None] * onehots, axis=2)).astype(jnp.bfloat16)
    router_grad = jnp.dot(mixed_rows.reshape(-1, D).T, logit_grad.reshape(-1, EXPERTS), preferred_element_type=jnp.float32)
    router_back = jnp.dot(logit_grad.reshape(-1, EXPERTS), router.T, preferred_element_type=jnp.float32).reshape(utterances, TOK_DEV, D)
    slot_cot = ((weights * kept_wide)[..., None] * grad_wide[:, :, None, :]).astype(jnp.bfloat16).reshape(utterances, TOK_DEV * TOP, D)
    cot_send = jnp.take_along_axis(slot_cot, source[..., None], axis=1)
    cot_send = jnp.where(filled[..., None], cot_send, jnp.zeros((), jnp.bfloat16))
    w_in_grad, w_out_grad, slot_back = lax.map(backward_expert, (slots_all, to_experts(cot_send, utterances), w_in, w_out))
    back_rows = from_experts(slot_back, utterances)
    slot_grad = jnp.take_along_axis(back_rows, slot_index[..., None], axis=1).reshape(utterances, TOK_DEV, TOP, D)
    slot_grad = slot_grad.astype(jnp.float32) * kept_wide[..., None]
    mixed_grad = grad_wide + lax.optimization_barrier(jnp.sum(slot_grad, axis=2)) + router_back
    conv_grad = mixed_grad * frame_mask * swish_slope(conv_sum)
    glu_grad = depth_transpose(conv_grad, tap_rows, half_width) * frame_mask
    depthwise_grad = depth_taps_grad(conv_grad, gated, half_width).T
    value_grad = glu_grad * gate_sig
    gate_grad = glu_grad * value_half * gate_sig * (1.0 - gate_sig)
    pre_cot = jnp.concatenate([value_grad, gate_grad], axis=-1).astype(jnp.bfloat16)
    conv_in_grad = jnp.dot(normed.reshape(-1, D).T, pre_cot.reshape(-1, 2 * D), preferred_element_type=jnp.float32)
    normed_grad = jnp.dot(pre_cot.reshape(-1, 2 * D), conv_in.T, preferred_element_type=jnp.float32).reshape(utterances, TOK_DEV, D)
    frames_grad = (mixed_grad + norm_backward(normed_grad, centred, inv_scale)).astype(jnp.bfloat16)
    return (layer_out.reshape(-1, D), frames_grad.reshape(-1, D), conv_in_grad, depthwise_grad, router_grad, w_in_grad, w_out_grad)
```

```python
import jax
import jax.numpy as jnp
from jax import lax
from jax.experimental import pallas as pl
from jax.experimental.pallas import tpu as pltpu
from jax.sharding import PartitionSpec as P

TOP = 2
KERNEL = 31


EPSILON = 1e-05


def swish_of(values):
    return values * jax.nn.sigmoid(values)


def swish_slope(values):
    sigmoid_v = jax.nn.sigmoid(values)
    return sigmoid_v * (1.0 + values * (1.0 - sigmoid_v))


def normalize(values):
    center = values - jnp.mean(values, axis=-1, keepdims=True)
    inv_scale = lax.rsqrt(jnp.mean(center * center, axis=-1, keepdims=True) + EPSILON)
    return (center * inv_scale, inv_scale)


def norm_backward(upstream, centred, inv_scale):
    first_mean = jnp.mean(upstream, axis=-1, keepdims=True)
    second_mean = jnp.mean(upstream * centred, axis=-1, keepdims=True)
    return inv_scale * (upstream - first_mean - centred * second_mean)


def pad_time(signal, half_width):
    return jnp.pad(signal, ((half_width, half_width), (0, 0)))


def depth_apply(signal, tap_rows, half_width):
    length = signal.shape[0]
    padded = pad_time(signal, half_width)
    summed = jnp.zeros(signal.shape, jnp.float32)
    for tap_index in range(tap_rows.shape[0]):
        summed = summed + tap_rows[tap_index] * lax.slice_in_dim(
            padded, tap_index, tap_index + length, axis=0
        )
    return summed


def depth_transpose(upstream, tap_rows, half_width):
    length = upstream.shape[0]
    padded = pad_time(upstream, half_width)
    summed = jnp.zeros(upstream.shape, jnp.float32)
    for tap_index in range(tap_rows.shape[0]):
        begin = 2 * half_width - tap_index
        summed = summed + tap_rows[tap_index] * lax.slice_in_dim(
            padded, begin, begin + length, axis=0
        )
    return summed


def depth_taps_grad(upstream, signal, half_width):
    length = signal.shape[0]
    padded = pad_time(signal, half_width)
    rows_list = []
    for tap_index in range(2 * half_width + 1):
        piece = lax.slice_in_dim(padded, tap_index, tap_index + length, axis=0)
        rows_list.append(jnp.sum(upstream * piece, axis=0))
    return jnp.stack(rows_list, axis=0)


def routing(choices, length, experts, capacity):
    tokens, top_count = choices.shape
    usable = jnp.arange(tokens, dtype=jnp.int32) < length
    flat_ids = choices.reshape(-1)
    live = jnp.repeat(usable, top_count)
    onehot = (flat_ids[:, None] == jnp.arange(experts, dtype=jnp.int32)[None, :]) & live[:, None]
    onehot_int = onehot.astype(jnp.int32)
    before = jnp.cumsum(onehot_int, axis=0) - onehot_int
    position = jnp.sum(jnp.where(onehot, before, 0), axis=1)
    kept_rows = live & (position < capacity)
    slot_total = experts * capacity
    slot_index = jnp.where(kept_rows, flat_ids * capacity + position, slot_total)
    match = slot_index[None, :] == jnp.arange(slot_total, dtype=jnp.int32)[:, None]
    filled = jnp.any(match, axis=1)
    source = jnp.sum(
        jnp.where(match, jnp.arange(tokens * top_count, dtype=jnp.int32)[None, :], 0), axis=1
    )
    return (usable, kept_rows, jnp.minimum(slot_index, slot_total - 1), filled, source)


def dispatch(send_rows):
    arrived_cols = lax.all_to_all(send_rows, "expert", split_axis=0, concat_axis=0, tiled=True)
    arrived = lax.all_gather(arrived_cols[None], "dp", axis=0, tiled=True)
    return arrived.reshape(-1, send_rows.shape[-1])


def collect(term_maker, rows_here, columns, capacity, width):
    summed = lax.psum_scatter(
        term_maker(jnp.int32(0), rows_here * lax.axis_size("dp")).astype(jnp.bfloat16),
        "dp",
        scatter_dimension=0,
        tiled=True,
    )
    returned = lax.all_to_all(
        summed.reshape(columns, capacity, width), "expert", split_axis=0, concat_axis=0, tiled=True
    )
    return returned.reshape(columns * capacity, width)


MESH = pl.DeviceIdType.MESH
HALF = 1152
WIDE = 2 * HALF
SPLIT = 640
VMEM_LIMIT = 60 * 1024 * 1024


def place():
    x = lax.axis_index("dp")
    e = lax.axis_index("expert")
    return x, e // 16, (e // 2) % 8, e % 2


def spot(x, y, z, c):
    return (x, y * 16 + z * 2 + c)


def remote(src, dst, send, recv, where):
    return pltpu.make_async_remote_copy(
        src_ref=src, dst_ref=dst, send_sem=send, recv_sem=recv, device_id=where, device_id_type=MESH
    )


def greet(targets):
    barrier = pltpu.get_barrier_semaphore()
    for where in targets:
        pl.semaphore_signal(barrier, inc=1, device_id=where, device_id_type=MESH)
    pl.semaphore_wait(barrier, len(targets))


def axis_peers(x, y, z, c):
    peers = [spot(x, y, z, 1 - c)]
    peers += [spot(x, y, (z + dz) % 8, c) for dz in range(1, 8)]
    peers += [spot(x, (y + dy) % 4, z, c) for dy in (1, 3)]
    peers += [spot((x + dx) % 4, y, z, c) for dx in (1, 3)]
    return peers


def gather_kernel(own_ref, out_ref, core_s, core_r, own_sem, z_s, z_r, ring_s, ring_r, tail_s, tail_r):
    x, y, z, c = place()
    greet(axis_peers(x, y, z, c))
    partner = spot(x, y, z, 1 - c)
    mine = pl.multiple_of(c * HALF, 128)
    other = pl.multiple_of((1 - c) * HALF, 128)
    row = pl.multiple_of(y * 64 + z * 8, 8)
    row4 = pl.multiple_of(row + 4 * c, 4)
    swap = remote(
        own_ref.at[:, pl.ds(other, HALF)],
        out_ref.at[x, pl.ds(row4, 4), pl.ds(other, HALF)],
        core_s,
        core_r,
        partner,
    )
    swap.start()
    keep = pltpu.make_async_copy(
        own_ref.at[:, pl.ds(mine, HALF)], out_ref.at[x, pl.ds(row4, 4), pl.ds(mine, HALF)], own_sem
    )
    keep.start()
    keep.wait()
    swap.wait()
    copies = []
    for dz in (4, 3, 5, 2, 6, 1, 7):
        block = out_ref.at[x, pl.ds(row, 8), pl.ds(mine, HALF)]
        copy = remote(block, block, z_s.at[dz - 1], z_r.at[dz - 1], spot(x, y, (z + dz) % 8, c))
        copy.start()
        copies.append(copy)
    for copy in copies:
        copy.wait()

    first = pl.multiple_of(mine, 128)
    second = pl.multiple_of(mine + SPLIT, 128)
    yrow = pl.multiple_of(y * 64, 64)

    def block_of(colour, level, index, part):
        cols = pl.ds(first, SPLIT) if colour == 0 else pl.ds(second, HALF - SPLIT)
        if level == 0:
            height = 64 if part is None else 32
            offset = 0 if part is None else part * 32
            if colour == 0:
                return out_ref.at[x, pl.ds(pl.multiple_of(index * 64 + offset, 32), height), cols]
            return out_ref.at[index, pl.ds(pl.multiple_of(yrow + offset, 32), height), cols]
        if colour == 0:
            height = 256 if part is None else 128
            offset = 0 if part is None else part * 128
            return out_ref.at[index, pl.ds(offset, height), cols]
        height = 64 if part is None else 32
        offset = 0 if part is None else part * 32
        return out_ref.at[:, pl.ds(pl.multiple_of(index * 64 + offset, 32), height), cols]

    def whereto(colour, level, step):
        if (colour + level) % 2 == 0:
            return spot(x, (y + step) % 4, z, c)
        return spot((x + step) % 4, y, z, c)

    def position(colour, level):
        return y if (colour + level) % 2 == 0 else x

    def opened(colour, level):
        at = position(colour, level)
        block = block_of(colour, level, at, None)
        base = (colour * 2 + level) * 4
        right = remote(block, block, ring_s.at[base], ring_r.at[base], whereto(colour, level, 1))
        left = remote(block, block, ring_s.at[base + 1], ring_r.at[base + 1], whereto(colour, level, 3))
        right.start()
        left.start()
        return right, left

    def passed(colour, level, pair, tell):
        at = position(colour, level)
        base = (colour * 2 + level) * 4
        right, left = pair
        right.wait_recv()
        block = block_of(colour, level, (at + 3) % 4, 0)
        on_right = remote(block, block, ring_s.at[base + 2], ring_r.at[base + 2], whereto(colour, level, 1))
        on_right.start()
        tell((at + 3) % 4, 1)
        left.wait_recv()
        block = block_of(colour, level, (at + 1) % 4, 1)
        on_left = remote(block, block, ring_s.at[base + 3], ring_r.at[base + 3], whereto(colour, level, 3))
        on_left.start()
        tell((at + 1) % 4, 2)
        return on_right, on_left

    def closed(colour, level, pair, onward, tell):
        at = position(colour, level)
        for copy in onward:
            copy.wait_recv()
        tell((at + 2) % 4, 3)
        for copy in pair + onward:
            copy.wait_send()

    silent = lambda index, slot: None
    low = [opened(colour, 0) for colour in (0, 1)]
    low_on = [passed(colour, 0, low[colour], silent) for colour in (0, 1)]
    for colour in (0, 1):
        closed(colour, 0, low[colour], low_on[colour], silent)
    tails = []

    def teller(colour):
        def tell(index, slot):
            block = block_of(colour, 1, index, None)
            at = colour * 4 + slot
            copy = remote(block, block, tail_s.at[at], tail_r.at[at], partner)
            copy.start()
            tails.append(copy)

        return tell

    high = [opened(colour, 1) for colour in (0, 1)]
    for colour in (0, 1):
        teller(colour)(position(colour, 1), 0)
    high_on = [passed(colour, 1, high[colour], teller(colour)) for colour in (0, 1)]
    for colour in (0, 1):
        closed(colour, 1, high[colour], high_on[colour], teller(colour))
    for copy in tails:
        copy.wait()


def gather_weights(packed):
    dma = pltpu.SemaphoreType.DMA
    return pl.pallas_call(
        gather_kernel,
        out_shape=jax.ShapeDtypeStruct((4, 256, WIDE), jnp.bfloat16),
        in_specs=[pl.BlockSpec(memory_space=pltpu.VMEM)],
        out_specs=pl.BlockSpec(memory_space=pltpu.VMEM),
        scratch_shapes=[dma, dma, dma, dma((7,)), dma((7,)), dma((16,)), dma((16,)), dma((8,)), dma((8,))],
        compiler_params=pltpu.CompilerParams(
            collective_id=0, has_side_effects=True, vmem_limit_bytes=VMEM_LIMIT
        ),
        name="gather_weights",
    )(packed)


def reduce_kernel(
    part_ref, out_ref, swap_buf, half_buf, far_buf, near_buf, mid_buf, mid_far, mid_near, z_src, z_buf, last_src,
    last_buf, swap_s, swap_r, ring_s, ring_r, z_s, z_r, last_s, last_r
):
    x, y, z, c = place()
    greet(axis_peers(x, y, z, c))
    partner = spot(x, y, z, 1 - c)
    mine = pl.multiple_of(c * HALF, 128)
    other = pl.multiple_of((1 - c) * HALF, 128)
    colours = ((0, SPLIT), (SPLIT, HALF - SPLIT))
    order = (2, 1, 3, 0)

    def rows_of(colour, index):
        if colour == 0:
            return index, pl.ds(0, 256)
        return slice(None), pl.ds(pl.multiple_of(index * 64, 64), 64)

    swaps = {}
    for step in order:
        for colour, (begin, width) in enumerate(colours):
            at = ((x if colour == 0 else y) + step) % 4
            lead, rows = rows_of(colour, at)
            slot = colour * 4 + step
            copy = remote(
                part_ref.at[lead, rows, pl.ds(pl.multiple_of(other + begin, 128), width)],
                swap_buf.at[lead, rows, pl.ds(begin, width)],
                swap_s.at[slot],
                swap_r.at[slot],
                partner,
            )
            copy.start()
            swaps[colour, step] = copy

    def first_to(colour, step):
        if colour == 0:
            return spot((x + step) % 4, y, z, c)
        return spot(x, (y + step) % 4, z, c)

    def second_to(colour, step):
        return first_to(1 - colour, step)

    def fold(colour, step, extra):
        begin, width = colours[colour]
        at = ((x if colour == 0 else y) + step) % 4
        swaps[colour, step].wait_recv()

        def body(t, carry):
            if colour == 0:
                lead, row = at, pl.multiple_of(t * 32, 32)
            else:
                lead, row = t // 2, pl.multiple_of(at * 64 + (t % 2) * 32, 32)
            value = part_ref[lead, pl.ds(row, 32), pl.ds(pl.multiple_of(mine + begin, 128), width)].astype(jnp.float32)
            value = value + swap_buf[lead, pl.ds(row, 32), pl.ds(begin, width)].astype(jnp.float32)
            value = extra(t, value)
            half_buf[colour, step, pl.ds(pl.multiple_of(t * 32, 32), 32), pl.ds(0, width)] = value.astype(jnp.bfloat16)
            return carry

        return body

    plain = lambda t, value: value
    sent = []
    pend = {}
    for colour, (begin, width) in enumerate(colours):
        lax.fori_loop(0, 8, fold(colour, 2, plain), 0)
        for side, step in ((0, 1), (1, 3)):
            slot = colour * 8 + side
            copy = remote(
                half_buf.at[colour, 2, pl.ds(side * 128, 128), pl.ds(0, width)],
                far_buf.at[colour, side, :, pl.ds(0, width)],
                ring_s.at[slot],
                ring_r.at[slot],
                first_to(colour, step),
            )
            copy.start()
            pend[colour, side] = copy
            sent.append(copy)
    for colour, (begin, width) in enumerate(colours):
        for side, step in ((0, 1), (1, 3)):
            lo = side * 4

            lax.fori_loop(4 - lo, 8 - lo, fold(colour, step, plain), 0)
            pend[colour, side].wait_recv()

            def extra(t, value, colour=colour, side=side, lo=lo, width=width):
                row = pl.multiple_of((t - lo) * 32, 32)
                return value + far_buf[colour, side, pl.ds(row, 32), pl.ds(0, width)].astype(jnp.float32)

            def again(t, carry, colour=colour, step=step, extra=extra, begin=begin, width=width):
                at = ((x if colour == 0 else y) + step) % 4
                if colour == 0:
                    lead, row = at, pl.multiple_of(t * 32, 32)
                else:
                    lead, row = t // 2, pl.multiple_of(at * 64 + (t % 2) * 32, 32)
                value = part_ref[lead, pl.ds(row, 32), pl.ds(pl.multiple_of(mine + begin, 128), width)].astype(jnp.float32)
                value = value + swap_buf[lead, pl.ds(row, 32), pl.ds(begin, width)].astype(jnp.float32)
                value = extra(t, value)
                half_buf[colour, step, pl.ds(pl.multiple_of(t * 32, 32), 32), pl.ds(0, width)] = value.astype(jnp.bfloat16)
                return carry

            lax.fori_loop(lo, lo + 4, again, 0)
            slot = colour * 8 + 2 + side
            copy = remote(
                half_buf.at[colour, step, :, pl.ds(0, width)],
                near_buf.at[colour, side, :, pl.ds(0, width)],
                ring_s.at[slot],
                ring_r.at[slot],
                first_to(colour, step),
            )
            copy.start()
            pend[colour, 2 + side] = copy
            sent.append(copy)
    for colour, (begin, width) in enumerate(colours):
        pend[colour, 2].wait_recv()
        pend[colour, 3].wait_recv()

        def extra(t, value, colour=colour, width=width):
            row = pl.multiple_of(t * 32, 32)
            for side in (0, 1):
                value = value + near_buf[colour, side, pl.ds(row, 32), pl.ds(0, width)].astype(jnp.float32)
            return value

        body = fold(colour, 0, extra)
        lax.fori_loop(0, 8, body, 0)
        at = y if colour == 0 else x
        for side, step in ((0, 1), (1, 3)):
            row = pl.multiple_of(((at + 2) % 4) * 64 + side * 32, 32)
            slot = colour * 8 + 4 + side
            copy = remote(
                half_buf.at[colour, 0, pl.ds(row, 32), pl.ds(0, width)],
                mid_far.at[colour, side, :, pl.ds(0, width)],
                ring_s.at[slot],
                ring_r.at[slot],
                second_to(colour, step),
            )
            copy.start()
            pend[colour, 4 + side] = copy
            sent.append(copy)
    for colour, (begin, width) in enumerate(colours):
        at = y if colour == 0 else x
        for side, step in ((0, 1), (1, 3)):
            row = pl.multiple_of(((at + step) % 4) * 64, 32)
            pend[colour, 4 + side].wait_recv()
            for piece in (0, 1):
                value = half_buf[colour, 0, pl.ds(pl.multiple_of(row + piece * 32, 32), 32), pl.ds(0, width)]
                if piece == side:
                    value = value.astype(jnp.float32) + mid_far[colour, side, :, pl.ds(0, width)].astype(jnp.float32)
                    value = value.astype(jnp.bfloat16)
                mid_buf[colour, side, pl.ds(piece * 32, 32), pl.ds(0, width)] = value
            slot = colour * 8 + 6 + side
            copy = remote(
                mid_buf.at[colour, side, :, pl.ds(0, width)],
                mid_near.at[colour, side, :, pl.ds(0, width)],
                ring_s.at[slot],
                ring_r.at[slot],
                second_to(colour, step),
            )
            copy.start()
            pend[colour, 6 + side] = copy
            sent.append(copy)
    for colour, (begin, width) in enumerate(colours):
        at = y if colour == 0 else x
        pend[colour, 6].wait_recv()
        pend[colour, 7].wait_recv()
        for piece in range(2):
            rows = pl.ds(piece * 32, 32)
            value = half_buf[colour, 0, pl.ds(pl.multiple_of(at * 64 + piece * 32, 32), 32), pl.ds(0, width)].astype(jnp.float32)
            for side in (0, 1):
                value = value + mid_near[colour, side, rows, pl.ds(0, width)].astype(jnp.float32)
            z_src[pl.ds(piece * 4, 4), :, pl.ds(begin, width)] = value.astype(jnp.bfloat16).reshape(4, 8, width)
    z_copies = []
    for dz in (4, 3, 5, 2, 6, 1, 7):
        to = (z + dz) % 8
        copy = remote(z_src.at[to], z_buf.at[dz - 1], z_s.at[dz - 1], z_r.at[dz - 1], spot(x, y, to, c))
        copy.start()
        z_copies.append(copy)
    total = z_src[z].astype(jnp.float32)
    for copy in z_copies:
        copy.wait_recv()
    for k in range(7):
        total = total + z_buf[k].astype(jnp.float32)
    last_src[...] = total
    last = remote(last_src, last_buf, last_s, last_r, partner)
    last.start()
    for copy in sent + z_copies:
        copy.wait_send()
    for copy in swaps.values():
        copy.wait_send()
    out_ref[:, pl.ds(mine, HALF)] = jnp.where(c == 0, last_src[0:4, :], last_src[4:8, :])
    last.wait()
    out_ref[:, pl.ds(other, HALF)] = jnp.where(c == 0, last_buf[0:4, :], last_buf[4:8, :])


def reduce_grads(part):
    dma = pltpu.SemaphoreType.DMA
    bf, wide = jnp.bfloat16, SPLIT
    return pl.pallas_call(
        reduce_kernel,
        out_shape=jax.ShapeDtypeStruct((4, WIDE), jnp.float32),
        in_specs=[pl.BlockSpec(memory_space=pltpu.VMEM)],
        out_specs=pl.BlockSpec(memory_space=pltpu.VMEM),
        scratch_shapes=[
            pltpu.VMEM((4, 256, HALF), bf),
            pltpu.VMEM((2, 4, 256, wide), bf),
            pltpu.VMEM((2, 2, 128, wide), bf),
            pltpu.VMEM((2, 2, 256, wide), bf),
            pltpu.VMEM((2, 2, 64, wide), bf),
            pltpu.VMEM((2, 2, 32, wide), bf),
            pltpu.VMEM((2, 2, 64, wide), bf),
            pltpu.VMEM((8, 8, HALF), bf),
            pltpu.VMEM((7, 8, HALF), bf),
            pltpu.VMEM((8, HALF), jnp.float32),
            pltpu.VMEM((8, HALF), jnp.float32),
            dma((8,)),
            dma((8,)),
            dma((16,)),
            dma((16,)),
            dma((7,)),
            dma((7,)),
            dma,
            dma,
        ],
        compiler_params=pltpu.CompilerParams(
            collective_id=1, has_side_effects=True, vmem_limit_bytes=VMEM_LIMIT
        ),
        name="reduce_grads",
    )(part)


def per_device(frames, lengths, expert_ids, conv_in, depthwise, router, w_in, w_out, out_grad):
    tokens, width = frames.shape
    experts = router.shape[1]
    capacity = TOP * tokens // experts
    columns = lax.axis_size("expert")
    rows_here = columns * capacity
    half_width = (KERNEL - 1) // 2
    packed = jnp.concatenate(
        [conv_in, router, jnp.pad(depthwise, ((0, 0), (0, WIDE - 2 * width - experts - KERNEL)))], axis=1
    )
    everything = gather_weights(packed).reshape(width, WIDE)
    conv_full = everything[:, : 2 * width]
    router_full = everything[:, 2 * width : 2 * width + experts]
    depth_full = everything[:, 2 * width + experts : 2 * width + experts + KERNEL]
    usable, kept_rows, slot_index, filled, source = routing(
        expert_ids, lengths[0], experts, capacity
    )
    frame_mask = usable.astype(jnp.float32)[:, None]
    frame_wide = frames.astype(jnp.float32)
    centred, inv_scale = normalize(frame_wide)
    normed = centred.astype(jnp.bfloat16)
    pointwise = jnp.dot(normed, conv_full, preferred_element_type=jnp.float32)
    value_half = pointwise[:, :width]
    gate_sig = jax.nn.sigmoid(pointwise[:, width:])
    gated = value_half * gate_sig * frame_mask
    tap_rows = depth_full.astype(jnp.float32).T
    conv_sum = depth_apply(gated, tap_rows, half_width)
    mixed_rows = (frame_wide + swish_of(conv_sum) * frame_mask).astype(jnp.bfloat16)
    logits = jnp.dot(mixed_rows, router_full, preferred_element_type=jnp.float32)
    onehots = (expert_ids[:, :, None] == jnp.arange(experts, dtype=jnp.int32)).astype(jnp.float32)
    chosen = jnp.sum(logits[:, None, :] * onehots, axis=-1)
    scores = jax.nn.sigmoid(chosen)
    score_sum = jnp.sum(scores, axis=-1, keepdims=True)
    weights = scores / score_sum
    kept_wide = kept_rows.reshape(tokens, TOP).astype(jnp.float32)
    send_rows = jnp.take(mixed_rows, source // TOP, axis=0)
    send_rows = jnp.where(filled[:, None], send_rows, jnp.zeros((), jnp.bfloat16)).reshape(
        experts, capacity, width
    )
    slot_rows = dispatch(send_rows)
    hidden = jnp.dot(slot_rows, w_in[0], preferred_element_type=jnp.float32)
    active = swish_of(hidden).astype(jnp.bfloat16)

    def forward_term(start, count):
        partial_rows = jnp.dot(active, w_out[0], preferred_element_type=jnp.float32).astype(
            jnp.bfloat16
        )
        return lax.optimization_barrier(partial_rows).astype(jnp.float32)

    expert_rows = collect(forward_term, rows_here, columns, capacity, width)
    picked = jnp.take(expert_rows, slot_index, axis=0).reshape(tokens, TOP, width)
    picked_wide = picked.astype(jnp.float32) * kept_wide[..., None]
    layer_out = (
        mixed_rows.astype(jnp.float32) + jnp.sum(weights[..., None] * picked_wide, axis=1)
    ).astype(jnp.bfloat16)
    conv_back, depth_back, router_back = conv_full, depth_full, router_full
    grad_wide = out_grad.astype(jnp.float32)
    weight_grad = jnp.sum(grad_wide[:, None, :] * picked_wide, axis=-1)
    mean_term = jnp.sum(weight_grad * weights, axis=-1, keepdims=True)
    chosen_grad = (weight_grad - mean_term) / score_sum * scores * (1.0 - scores)
    logit_grad = jnp.sum(chosen_grad[..., None] * onehots, axis=1).astype(jnp.bfloat16)
    router_part = lax.dot_general(
        mixed_rows, logit_grad, (((0,), (0,)), ((), ())), preferred_element_type=jnp.float32
    )
    router_term = lax.dot_general(
        logit_grad, router_back, (((1,), (1,)), ((), ())), preferred_element_type=jnp.float32
    )
    slot_cot = (
        ((weights * kept_wide)[..., None] * grad_wide[:, None, :])
        .astype(jnp.bfloat16)
        .reshape(tokens * TOP, width)
    )
    cot_send = jnp.take(slot_cot, source, axis=0)
    cot_send = jnp.where(filled[:, None], cot_send, jnp.zeros((), jnp.bfloat16)).reshape(
        experts, capacity, width
    )
    cot_rows = dispatch(cot_send)
    act_grad = lax.dot_general(
        cot_rows, w_out[0], (((1,), (1,)), ((), ())), preferred_element_type=jnp.float32
    )
    pre_grad = (act_grad * swish_slope(hidden)).astype(jnp.bfloat16)
    w_out_grad = lax.dot_general(
        active, cot_rows, (((0,), (0,)), ((), ())), preferred_element_type=jnp.float32
    ).astype(jnp.bfloat16)[None]
    w_in_grad = lax.dot_general(
        slot_rows, pre_grad, (((0,), (0,)), ((), ())), preferred_element_type=jnp.float32
    ).astype(jnp.bfloat16)[None]

    def backward_term(start, count):
        partial_rows = lax.dot_general(
            pre_grad, w_in[0], (((1,), (1,)), ((), ())), preferred_element_type=jnp.float32
        ).astype(jnp.bfloat16)
        return lax.optimization_barrier(partial_rows).astype(jnp.float32)

    back_rows = collect(backward_term, rows_here, columns, capacity, width)
    slot_grad = jnp.take(back_rows, slot_index, axis=0).reshape(tokens, TOP, width)
    slot_grad = slot_grad.astype(jnp.float32) * kept_wide[..., None]
    mixed_grad = grad_wide + jnp.sum(slot_grad, axis=1) + router_term
    conv_grad = mixed_grad * frame_mask * swish_slope(conv_sum)
    tap_back = depth_back.astype(jnp.float32).T
    glu_grad = depth_transpose(conv_grad, tap_back, half_width) * frame_mask
    taps_grad = depth_taps_grad(conv_grad, gated, half_width)
    value_grad = glu_grad * gate_sig
    gate_grad = glu_grad * value_half * gate_sig * (1.0 - gate_sig)
    pre_cot = jnp.concatenate([value_grad, gate_grad], axis=-1).astype(jnp.bfloat16)
    conv_part = lax.dot_general(
        normed, pre_cot, (((0,), (0,)), ((), ())), preferred_element_type=jnp.float32
    )
    normed_grad = lax.dot_general(
        pre_cot, conv_back, (((1,), (1,)), ((), ())), preferred_element_type=jnp.float32
    )
    frames_grad = (mixed_grad + norm_backward(normed_grad, centred, inv_scale)).astype(jnp.bfloat16)
    small = jnp.concatenate(
        [router_part, taps_grad.T, jnp.zeros((width, WIDE - 2 * width - experts - KERNEL), jnp.float32)], axis=1
    )
    part = jnp.concatenate([conv_part.astype(jnp.bfloat16), small.astype(jnp.bfloat16)], axis=1)
    summed = reduce_grads(part.reshape(4, width // 4, WIDE))
    conv_in_grad = summed[:, : 2 * width]
    router_grad = summed[:, 2 * width : 2 * width + experts]
    depthwise_grad = summed[:, 2 * width + experts : 2 * width + experts + KERNEL]
    return (
        layer_out,
        frames_grad,
        conv_in_grad,
        depthwise_grad,
        router_grad,
        w_in_grad,
        w_out_grad,
    )


def solution(mesh):
    in_specs = (
        P(("dp", "expert"), None),
        P(("dp", "expert")),
        P(("dp", "expert"), None),
        P(("dp", "expert"), None),
        P(("dp", "expert"), None),
        P(("dp", "expert"), None),
        P("expert", None, "dp"),
        P("expert", "dp", None),
        P(("dp", "expert"), None),
    )
    out_specs = (
        P(("dp", "expert"), None),
        P(("dp", "expert"), None),
        P(("dp", "expert"), None),
        P(("dp", "expert"), None),
        P(("dp", "expert"), None),
        P("expert", None, "dp"),
        P("expert", "dp", None),
    )
    return jax.shard_map(
        per_device, mesh=mesh, in_specs=in_specs, out_specs=out_specs, check_vma=False
    )
```

```python
import jax
import jax.numpy as jnp
from jax import lax
from jax.experimental import pallas as pl
from jax.experimental.pallas import tpu as pltpu
from jax.sharding import PartitionSpec as P

TOP = 2
KERNEL = 31


EPSILON = 1e-05


def swish_of(values):
    return values * jax.nn.sigmoid(values)


def swish_slope(values):
    sigmoid_v = jax.nn.sigmoid(values)
    return sigmoid_v * (1.0 + values * (1.0 - sigmoid_v))


def normalize(values):
    center = values - jnp.mean(values, axis=-1, keepdims=True)
    inv_scale = lax.rsqrt(jnp.mean(center * center, axis=-1, keepdims=True) + EPSILON)
    return (center * inv_scale, inv_scale)


def norm_backward(upstream, centred, inv_scale):
    first_mean = jnp.mean(upstream, axis=-1, keepdims=True)
    second_mean = jnp.mean(upstream * centred, axis=-1, keepdims=True)
    return inv_scale * (upstream - first_mean - centred * second_mean)


def pad_time(signal, half_width):
    return jnp.pad(signal, ((half_width, half_width), (0, 0)))


def depth_apply(signal, tap_rows, half_width):
    length = signal.shape[0]
    padded = pad_time(signal, half_width)
    summed = jnp.zeros(signal.shape, jnp.float32)
    for tap_index in range(tap_rows.shape[0]):
        summed = summed + tap_rows[tap_index] * lax.slice_in_dim(
            padded, tap_index, tap_index + length, axis=0
        )
    return summed


def depth_transpose(upstream, tap_rows, half_width):
    length = upstream.shape[0]
    padded = pad_time(upstream, half_width)
    summed = jnp.zeros(upstream.shape, jnp.float32)
    for tap_index in range(tap_rows.shape[0]):
        begin = 2 * half_width - tap_index
        summed = summed + tap_rows[tap_index] * lax.slice_in_dim(
            padded, begin, begin + length, axis=0
        )
    return summed


def depth_taps_grad(upstream, signal, half_width):
    length = signal.shape[0]
    padded = pad_time(signal, half_width)
    rows_list = []
    for tap_index in range(2 * half_width + 1):
        piece = lax.slice_in_dim(padded, tap_index, tap_index + length, axis=0)
        rows_list.append(jnp.sum(upstream * piece, axis=0))
    return jnp.stack(rows_list, axis=0)


def routing(choices, length, experts, capacity):
    tokens, top_count = choices.shape
    usable = jnp.arange(tokens, dtype=jnp.int32) < length
    flat_ids = choices.reshape(-1)
    live = jnp.repeat(usable, top_count)
    onehot = (flat_ids[:, None] == jnp.arange(experts, dtype=jnp.int32)[None, :]) & live[:, None]
    onehot_int = onehot.astype(jnp.int32)
    before = jnp.cumsum(onehot_int, axis=0) - onehot_int
    position = jnp.sum(jnp.where(onehot, before, 0), axis=1)
    kept_rows = live & (position < capacity)
    slot_total = experts * capacity
    slot_index = jnp.where(kept_rows, flat_ids * capacity + position, slot_total)
    match = slot_index[None, :] == jnp.arange(slot_total, dtype=jnp.int32)[:, None]
    filled = jnp.any(match, axis=1)
    source = jnp.sum(
        jnp.where(match, jnp.arange(tokens * top_count, dtype=jnp.int32)[None, :], 0), axis=1
    )
    return (usable, kept_rows, jnp.minimum(slot_index, slot_total - 1), filled, source)


MESH = pl.DeviceIdType.MESH
HALF = 1152
WIDE = 2 * HALF
SPLIT = 640
VMEM_LIMIT = 60 * 1024 * 1024


def place():
    x = lax.axis_index("dp")
    e = lax.axis_index("expert")
    return x, e // 16, (e // 2) % 8, e % 2


def spot(x, y, z, c):
    return (x, y * 16 + z * 2 + c)


def remote(src, dst, send, recv, where):
    return pltpu.make_async_remote_copy(
        src_ref=src, dst_ref=dst, send_sem=send, recv_sem=recv, device_id=where, device_id_type=MESH
    )


def greet(targets):
    barrier = pltpu.get_barrier_semaphore()
    for where in targets:
        pl.semaphore_signal(barrier, inc=1, device_id=where, device_id_type=MESH)
    pl.semaphore_wait(barrier, len(targets))


def axis_peers(x, y, z, c):
    peers = [spot(x, y, z, 1 - c)]
    peers += [spot(x, y, (z + dz) % 8, c) for dz in range(1, 8)]
    peers += [spot(x, (y + dy) % 4, z, c) for dy in (1, 3)]
    peers += [spot((x + dx) % 4, y, z, c) for dx in (1, 3)]
    return peers


def gather_kernel(own_ref, out_ref, core_s, core_r, own_sem, z_s, z_r, ring_s, ring_r, tail_s, tail_r):
    x, y, z, c = place()
    greet(axis_peers(x, y, z, c))
    partner = spot(x, y, z, 1 - c)
    mine = pl.multiple_of(c * HALF, 128)
    other = pl.multiple_of((1 - c) * HALF, 128)
    row = pl.multiple_of(y * 64 + z * 8, 8)
    row4 = pl.multiple_of(row + 4 * c, 4)
    swap = remote(
        own_ref.at[:, pl.ds(other, HALF)],
        out_ref.at[x, pl.ds(row4, 4), pl.ds(other, HALF)],
        core_s,
        core_r,
        partner,
    )
    swap.start()
    keep = pltpu.make_async_copy(
        own_ref.at[:, pl.ds(mine, HALF)], out_ref.at[x, pl.ds(row4, 4), pl.ds(mine, HALF)], own_sem
    )
    keep.start()
    keep.wait()
    swap.wait()
    copies = []
    for dz in (4, 3, 5, 2, 6, 1, 7):
        block = out_ref.at[x, pl.ds(row, 8), pl.ds(mine, HALF)]
        copy = remote(block, block, z_s.at[dz - 1], z_r.at[dz - 1], spot(x, y, (z + dz) % 8, c))
        copy.start()
        copies.append(copy)
    for copy in copies:
        copy.wait()

    first = pl.multiple_of(mine, 128)
    second = pl.multiple_of(mine + SPLIT, 128)
    yrow = pl.multiple_of(y * 64, 64)

    def block_of(colour, level, index, part):
        cols = pl.ds(first, SPLIT) if colour == 0 else pl.ds(second, HALF - SPLIT)
        if level == 0:
            height = 64 if part is None else 32
            offset = 0 if part is None else part * 32
            if colour == 0:
                return out_ref.at[x, pl.ds(pl.multiple_of(index * 64 + offset, 32), height), cols]
            return out_ref.at[index, pl.ds(pl.multiple_of(yrow + offset, 32), height), cols]
        if colour == 0:
            height = 256 if part is None else 128
            offset = 0 if part is None else part * 128
            return out_ref.at[index, pl.ds(offset, height), cols]
        height = 64 if part is None else 32
        offset = 0 if part is None else part * 32
        return out_ref.at[:, pl.ds(pl.multiple_of(index * 64 + offset, 32), height), cols]

    def whereto(colour, level, step):
        if (colour + level) % 2 == 0:
            return spot(x, (y + step) % 4, z, c)
        return spot((x + step) % 4, y, z, c)

    def position(colour, level):
        return y if (colour + level) % 2 == 0 else x

    def opened(colour, level):
        at = position(colour, level)
        block = block_of(colour, level, at, None)
        base = (colour * 2 + level) * 4
        right = remote(block, block, ring_s.at[base], ring_r.at[base], whereto(colour, level, 1))
        left = remote(block, block, ring_s.at[base + 1], ring_r.at[base + 1], whereto(colour, level, 3))
        right.start()
        left.start()
        return right, left

    def passed(colour, level, pair, tell):
        at = position(colour, level)
        base = (colour * 2 + level) * 4
        right, left = pair
        right.wait_recv()
        block = block_of(colour, level, (at + 3) % 4, 0)
        on_right = remote(block, block, ring_s.at[base + 2], ring_r.at[base + 2], whereto(colour, level, 1))
        on_right.start()
        tell((at + 3) % 4, 1)
        left.wait_recv()
        block = block_of(colour, level, (at + 1) % 4, 1)
        on_left = remote(block, block, ring_s.at[base + 3], ring_r.at[base + 3], whereto(colour, level, 3))
        on_left.start()
        tell((at + 1) % 4, 2)
        return on_right, on_left

    def closed(colour, level, pair, onward, tell):
        at = position(colour, level)
        for copy in onward:
            copy.wait_recv()
        tell((at + 2) % 4, 3)
        for copy in pair + onward:
            copy.wait_send()

    silent = lambda index, slot: None
    low = [opened(colour, 0) for colour in (0, 1)]
    low_on = [passed(colour, 0, low[colour], silent) for colour in (0, 1)]
    for colour in (0, 1):
        closed(colour, 0, low[colour], low_on[colour], silent)
    tails = []

    def teller(colour):
        def tell(index, slot):
            block = block_of(colour, 1, index, None)
            at = colour * 4 + slot
            copy = remote(block, block, tail_s.at[at], tail_r.at[at], partner)
            copy.start()
            tails.append(copy)

        return tell

    high = [opened(colour, 1) for colour in (0, 1)]
    for colour in (0, 1):
        teller(colour)(position(colour, 1), 0)
    high_on = [passed(colour, 1, high[colour], teller(colour)) for colour in (0, 1)]
    for colour in (0, 1):
        closed(colour, 1, high[colour], high_on[colour], teller(colour))
    for copy in tails:
        copy.wait()


def gather_weights(packed):
    dma = pltpu.SemaphoreType.DMA
    return pl.pallas_call(
        gather_kernel,
        out_shape=jax.ShapeDtypeStruct((4, 256, WIDE), jnp.bfloat16),
        in_specs=[pl.BlockSpec(memory_space=pltpu.VMEM)],
        out_specs=pl.BlockSpec(memory_space=pltpu.VMEM),
        scratch_shapes=[dma, dma, dma, dma((7,)), dma((7,)), dma((16,)), dma((16,)), dma((8,)), dma((8,))],
        compiler_params=pltpu.CompilerParams(
            collective_id=0, has_side_effects=True, vmem_limit_bytes=VMEM_LIMIT
        ),
        name="gather_weights",
    )(packed)


def reduce_kernel(
    part_ref, out_ref, swap_buf, half_buf, far_buf, near_buf, mid_buf, mid_far, mid_near, z_src, z_buf, last_src,
    last_buf, swap_s, swap_r, ring_s, ring_r, z_s, z_r, last_s, last_r
):
    x, y, z, c = place()
    greet(axis_peers(x, y, z, c))
    partner = spot(x, y, z, 1 - c)
    mine = pl.multiple_of(c * HALF, 128)
    other = pl.multiple_of((1 - c) * HALF, 128)
    colours = ((0, SPLIT), (SPLIT, HALF - SPLIT))
    order = (2, 1, 3, 0)

    def rows_of(colour, index):
        if colour == 0:
            return index, pl.ds(0, 256)
        return slice(None), pl.ds(pl.multiple_of(index * 64, 64), 64)

    swaps = {}
    for step in order:
        for colour, (begin, width) in enumerate(colours):
            at = ((x if colour == 0 else y) + step) % 4
            lead, rows = rows_of(colour, at)
            slot = colour * 4 + step
            copy = remote(
                part_ref.at[lead, rows, pl.ds(pl.multiple_of(other + begin, 128), width)],
                swap_buf.at[lead, rows, pl.ds(begin, width)],
                swap_s.at[slot],
                swap_r.at[slot],
                partner,
            )
            copy.start()
            swaps[colour, step] = copy

    def first_to(colour, step):
        if colour == 0:
            return spot((x + step) % 4, y, z, c)
        return spot(x, (y + step) % 4, z, c)

    def second_to(colour, step):
        return first_to(1 - colour, step)

    def fold(colour, step, extra):
        begin, width = colours[colour]
        at = ((x if colour == 0 else y) + step) % 4
        swaps[colour, step].wait_recv()

        def body(t, carry):
            if colour == 0:
                lead, row = at, pl.multiple_of(t * 32, 32)
            else:
                lead, row = t // 2, pl.multiple_of(at * 64 + (t % 2) * 32, 32)
            value = part_ref[lead, pl.ds(row, 32), pl.ds(pl.multiple_of(mine + begin, 128), width)].astype(jnp.float32)
            value = value + swap_buf[lead, pl.ds(row, 32), pl.ds(begin, width)].astype(jnp.float32)
            value = extra(t, value)
            half_buf[colour, step, pl.ds(pl.multiple_of(t * 32, 32), 32), pl.ds(0, width)] = value.astype(jnp.bfloat16)
            return carry

        return body

    plain = lambda t, value: value
    sent = []
    pend = {}
    for colour, (begin, width) in enumerate(colours):
        lax.fori_loop(0, 8, fold(colour, 2, plain), 0)
        for side, step in ((0, 1), (1, 3)):
            slot = colour * 8 + side
            copy = remote(
                half_buf.at[colour, 2, pl.ds(side * 128, 128), pl.ds(0, width)],
                far_buf.at[colour, side, :, pl.ds(0, width)],
                ring_s.at[slot],
                ring_r.at[slot],
                first_to(colour, step),
            )
            copy.start()
            pend[colour, side] = copy
            sent.append(copy)
    for colour, (begin, width) in enumerate(colours):
        for side, step in ((0, 1), (1, 3)):
            lo = side * 4

            lax.fori_loop(4 - lo, 8 - lo, fold(colour, step, plain), 0)
            pend[colour, side].wait_recv()

            def extra(t, value, colour=colour, side=side, lo=lo, width=width):
                row = pl.multiple_of((t - lo) * 32, 32)
                return value + far_buf[colour, side, pl.ds(row, 32), pl.ds(0, width)].astype(jnp.float32)

            def again(t, carry, colour=colour, step=step, extra=extra, begin=begin, width=width):
                at = ((x if colour == 0 else y) + step) % 4
                if colour == 0:
                    lead, row = at, pl.multiple_of(t * 32, 32)
                else:
                    lead, row = t // 2, pl.multiple_of(at * 64 + (t % 2) * 32, 32)
                value = part_ref[lead, pl.ds(row, 32), pl.ds(pl.multiple_of(mine + begin, 128), width)].astype(jnp.float32)
                value = value + swap_buf[lead, pl.ds(row, 32), pl.ds(begin, width)].astype(jnp.float32)
                value = extra(t, value)
                half_buf[colour, step, pl.ds(pl.multiple_of(t * 32, 32), 32), pl.ds(0, width)] = value.astype(jnp.bfloat16)
                return carry

            lax.fori_loop(lo, lo + 4, again, 0)
            slot = colour * 8 + 2 + side
            copy = remote(
                half_buf.at[colour, step, :, pl.ds(0, width)],
                near_buf.at[colour, side, :, pl.ds(0, width)],
                ring_s.at[slot],
                ring_r.at[slot],
                first_to(colour, step),
            )
            copy.start()
            pend[colour, 2 + side] = copy
            sent.append(copy)
    for colour, (begin, width) in enumerate(colours):
        pend[colour, 2].wait_recv()
        pend[colour, 3].wait_recv()

        def extra(t, value, colour=colour, width=width):
            row = pl.multiple_of(t * 32, 32)
            for side in (0, 1):
                value = value + near_buf[colour, side, pl.ds(row, 32), pl.ds(0, width)].astype(jnp.float32)
            return value

        body = fold(colour, 0, extra)
        lax.fori_loop(0, 8, body, 0)
        at = y if colour == 0 else x
        for side, step in ((0, 1), (1, 3)):
            row = pl.multiple_of(((at + 2) % 4) * 64 + side * 32, 32)
            slot = colour * 8 + 4 + side
            copy = remote(
                half_buf.at[colour, 0, pl.ds(row, 32), pl.ds(0, width)],
                mid_far.at[colour, side, :, pl.ds(0, width)],
                ring_s.at[slot],
                ring_r.at[slot],
                second_to(colour, step),
            )
            copy.start()
            pend[colour, 4 + side] = copy
            sent.append(copy)
    for colour, (begin, width) in enumerate(colours):
        at = y if colour == 0 else x
        for side, step in ((0, 1), (1, 3)):
            row = pl.multiple_of(((at + step) % 4) * 64, 32)
            pend[colour, 4 + side].wait_recv()
            for piece in (0, 1):
                value = half_buf[colour, 0, pl.ds(pl.multiple_of(row + piece * 32, 32), 32), pl.ds(0, width)]
                if piece == side:
                    value = value.astype(jnp.float32) + mid_far[colour, side, :, pl.ds(0, width)].astype(jnp.float32)
                    value = value.astype(jnp.bfloat16)
                mid_buf[colour, side, pl.ds(piece * 32, 32), pl.ds(0, width)] = value
            slot = colour * 8 + 6 + side
            copy = remote(
                mid_buf.at[colour, side, :, pl.ds(0, width)],
                mid_near.at[colour, side, :, pl.ds(0, width)],
                ring_s.at[slot],
                ring_r.at[slot],
                second_to(colour, step),
            )
            copy.start()
            pend[colour, 6 + side] = copy
            sent.append(copy)
    for colour, (begin, width) in enumerate(colours):
        at = y if colour == 0 else x
        pend[colour, 6].wait_recv()
        pend[colour, 7].wait_recv()
        for piece in range(2):
            rows = pl.ds(piece * 32, 32)
            value = half_buf[colour, 0, pl.ds(pl.multiple_of(at * 64 + piece * 32, 32), 32), pl.ds(0, width)].astype(jnp.float32)
            for side in (0, 1):
                value = value + mid_near[colour, side, rows, pl.ds(0, width)].astype(jnp.float32)
            z_src[pl.ds(piece * 4, 4), :, pl.ds(begin, width)] = value.astype(jnp.bfloat16).reshape(4, 8, width)
    z_copies = []
    for dz in (4, 3, 5, 2, 6, 1, 7):
        to = (z + dz) % 8
        copy = remote(z_src.at[to], z_buf.at[dz - 1], z_s.at[dz - 1], z_r.at[dz - 1], spot(x, y, to, c))
        copy.start()
        z_copies.append(copy)
    total = z_src[z].astype(jnp.float32)
    for copy in z_copies:
        copy.wait_recv()
    for k in range(7):
        total = total + z_buf[k].astype(jnp.float32)
    last_src[...] = total
    last = remote(last_src, last_buf, last_s, last_r, partner)
    last.start()
    for copy in sent + z_copies:
        copy.wait_send()
    for copy in swaps.values():
        copy.wait_send()
    out_ref[:, pl.ds(mine, HALF)] = jnp.where(c == 0, last_src[0:4, :], last_src[4:8, :])
    last.wait()
    out_ref[:, pl.ds(other, HALF)] = jnp.where(c == 0, last_buf[0:4, :], last_buf[4:8, :])


def reduce_grads(part):
    dma = pltpu.SemaphoreType.DMA
    bf, wide = jnp.bfloat16, SPLIT
    return pl.pallas_call(
        reduce_kernel,
        out_shape=jax.ShapeDtypeStruct((4, WIDE), jnp.float32),
        in_specs=[pl.BlockSpec(memory_space=pltpu.VMEM)],
        out_specs=pl.BlockSpec(memory_space=pltpu.VMEM),
        scratch_shapes=[
            pltpu.VMEM((4, 256, HALF), bf),
            pltpu.VMEM((2, 4, 256, wide), bf),
            pltpu.VMEM((2, 2, 128, wide), bf),
            pltpu.VMEM((2, 2, 256, wide), bf),
            pltpu.VMEM((2, 2, 64, wide), bf),
            pltpu.VMEM((2, 2, 32, wide), bf),
            pltpu.VMEM((2, 2, 64, wide), bf),
            pltpu.VMEM((8, 8, HALF), bf),
            pltpu.VMEM((7, 8, HALF), bf),
            pltpu.VMEM((8, HALF), jnp.float32),
            pltpu.VMEM((8, HALF), jnp.float32),
            dma((8,)),
            dma((8,)),
            dma((16,)),
            dma((16,)),
            dma((7,)),
            dma((7,)),
            dma,
            dma,
        ],
        compiler_params=pltpu.CompilerParams(
            collective_id=1, has_side_effects=True, vmem_limit_bytes=VMEM_LIMIT
        ),
        name="reduce_grads",
    )(part)


STEPS = (0, 1, 3, 2)


def expert_kernel(
    rows_ref, cot_ref, inner_hbm, outer_hbm, y_ref, z_ref, inner_grad_hbm, outer_grad_hbm,
    slots, cots, active, pre, inner, outer, part_y, part_z, straight_y, straight_z, relay_y, relay_z, joint_y, joint_z,
    grad_buf, sized, load_sem, self_s, there_s, there_r, ring_s, ring_r, fold_s, fold_r, back_s, back_r, store_sem
):
    x, y, z, c = place()
    f32, bf = jnp.float32, jnp.bfloat16
    here = y * 16 + z * 2 + c
    right, left, far = (x + 1) % 4, (x + 3) % 4, (x + 2) % 4
    to_right, to_left = spot(right, y, z, c), spot(left, y, z, c)
    loads = [
        pltpu.make_async_copy(inner_hbm, inner, load_sem.at[0]),
        pltpu.make_async_copy(outer_hbm, outer, load_sem.at[1]),
    ]
    for load in loads:
        load.start()

    barrier = pltpu.get_barrier_semaphore()

    def hail(i, carry):
        pl.semaphore_signal(barrier, inc=1, device_id=(x, (here + i) % 64), device_id_type=MESH)
        return carry

    lax.fori_loop(1, 64, hail, 0)
    for where in (to_right, to_left):
        pl.semaphore_signal(barrier, inc=1, device_id=where, device_id_type=MESH)
    pl.semaphore_wait(barrier, 65)

    own4 = pl.multiple_of(4 * here, 4)
    line4 = pl.multiple_of(8 * z + 4 * c, 4)
    kinds = ((rows_ref, slots), (cot_ref, cots))
    selfs = []
    for kind, (source, target) in enumerate(kinds):
        copy = pltpu.make_async_copy(
            source.at[pl.ds(own4, 4)], target.at[x, y, pl.ds(line4, 4)], self_s.at[kind]
        )
        copy.start()
        selfs.append(copy)
    for q, dy in enumerate(STEPS):
        yt = (y + 4 - dy) % 4

        def there(i, carry, yt=yt, q=q):
            zt, ct = (z + 4 + i // 2) % 8, (c + i) % 2
            et = yt * 16 + zt * 2 + ct
            rows = pl.ds(pl.multiple_of(4 * et, 4), 4)
            for kind, (source, target) in enumerate(kinds):
                remote(
                    source.at[rows], target.at[x, y, pl.ds(line4, 4)], there_s.at[kind, q], there_r.at[kind, q], (x, et)
                ).start()
            return carry

        if dy == 0:
            lax.fori_loop(0, 8, there, 0)
            lax.fori_loop(9, 16, there, 0)
        else:
            lax.fori_loop(0, 16, there, 0)

    def source_y(q):
        return (y + STEPS[q]) % 4

    rings = {}

    def arrive(q):
        ys = source_y(q)
        if STEPS[q] == 0:
            for copy in selfs:
                copy.wait()
        for kind, (_, target) in enumerate(kinds):
            view = sized.at[pl.ds(0, 15 if STEPS[q] == 0 else 16)]
            remote(view, view, there_s.at[kind, q], there_r.at[kind, q], to_right).wait_recv()
            block = target.at[x, ys]
            for side, where in ((0, to_right), (1, to_left)):
                copy = remote(block, block, ring_s.at[kind, side, q], ring_r.at[kind, side, q], where)
                copy.start()
                rings[kind, side, q] = copy

    def forward(q):
        ys = source_y(q)
        for kind, side, at, where in ((0, 0, left, to_right), (1, 1, right, to_left)):
            rings[kind, side, q].wait_recv()
            block = kinds[kind][1].at[at, ys]
            copy = remote(block, block, ring_s.at[kind, 2, q], ring_r.at[kind, 2, q], where)
            copy.start()
            rings[kind, 2, q] = copy

    folds = {}

    def push(name, q, source, target, where):
        copy = remote(source, target, fold_s.at[name, q], fold_r.at[name, q], where)
        copy.start()
        folds[name, q] = copy

    def compute(q):
        ys = source_y(q)
        rings[0, 1, q].wait_recv()
        rings[1, 0, q].wait_recv()
        rings[0, 2, q].wait_recv()
        rings[1, 2, q].wait_recv()

        def first(n, carry):
            cols = pl.ds(pl.multiple_of(n * 256, 256), 256)
            hidden = jnp.dot(slots[:, ys].reshape(256, 1024), inner[:, cols], preferred_element_type=f32)
            act_grad = lax.dot_general(
                cots[:, ys].reshape(256, 1024), outer[cols, :], (((1,), (1,)), ((), ())), preferred_element_type=f32
            )
            sig = jax.nn.sigmoid(hidden)
            active[:, ys, :, cols] = (hidden * sig).astype(bf).reshape(4, 64, 256)
            slope = sig * (1.0 + hidden * (1.0 - sig))
            pre[:, ys, :, cols] = (act_grad * slope).astype(bf).reshape(4, 64, 256)
            return carry

        lax.fori_loop(0, 4, first, 0)

        def second(n, carry):
            cols = pl.ds(pl.multiple_of(n * 256, 256), 256)
            out = jnp.dot(active[:, ys].reshape(256, 1024), outer[:, cols], preferred_element_type=f32)
            part_y[q, :, :, cols] = out.astype(bf).reshape(4, 64, 256)
            out = lax.dot_general(
                pre[:, ys].reshape(256, 1024), inner[cols, :], (((1,), (1,)), ((), ())), preferred_element_type=f32
            )
            part_z[q, :, :, cols] = out.astype(bf).reshape(4, 64, 256)
            return carry

        lax.fori_loop(0, 4, second, 0)
        push(2, q, part_y.at[q, far], relay_y.at[q], to_right)
        push(3, q, part_z.at[q, far], relay_z.at[q], to_left)
        push(0, q, part_z.at[q, right], straight_z.at[q], to_right)
        push(1, q, part_y.at[q, left], straight_y.at[q], to_left)

    def relay(q):
        folds[2, q].wait_recv()
        part_y[q, right] = (part_y[q, right].astype(f32) + relay_y[q].astype(f32)).astype(bf)
        push(4, q, part_y.at[q, right], joint_y.at[q], to_right)
        folds[3, q].wait_recv()
        part_z[q, left] = (part_z[q, left].astype(f32) + relay_z[q].astype(f32)).astype(bf)
        push(5, q, part_z.at[q, left], joint_z.at[q], to_left)

    def deliver(q):
        yt = source_y(q)
        for name in (1, 4, 0, 5):
            folds[name, q].wait_recv()
        part_y[q, x] = (part_y[q, x].astype(f32) + straight_y[q].astype(f32) + joint_y[q].astype(f32)).astype(bf)
        part_z[q, x] = (part_z[q, x].astype(f32) + straight_z[q].astype(f32) + joint_z[q].astype(f32)).astype(bf)

        def back(i, carry):
            zt, ct = (z + 4 + i // 2) % 8, (c + i) % 2
            rows = pl.ds(pl.multiple_of(8 * zt + 4 * ct, 4), 4)
            for kind, (source, target) in enumerate(((part_y, y_ref), (part_z, z_ref))):
                remote(
                    source.at[q, x, rows], target.at[pl.ds(own4, 4)], back_s.at[kind], back_r.at[kind], (x, yt * 16 + zt * 2 + ct)
                ).start()
            return carry

        if STEPS[q] == 0:
            lax.fori_loop(0, 8, back, 0)
            lax.fori_loop(9, 16, back, 0)
            for kind, (source, target) in enumerate(((part_y, y_ref), (part_z, z_ref))):
                copy = pltpu.make_async_copy(
                    source.at[q, x, pl.ds(line4, 4)], target.at[pl.ds(own4, 4)], self_s.at[2 + kind]
                )
                copy.start()
                selfs.append(copy)
        else:
            lax.fori_loop(0, 16, back, 0)

    stores = []

    def weight_grad(which, left_ref, right_ref, target):
        def body(n, carry):
            cols = pl.ds(pl.multiple_of(n * 256, 256), 256)
            out = lax.dot_general(
                left_ref[:, :, :, cols].reshape(1024, 256),
                right_ref[...].reshape(1024, 1024),
                (((0,), (0,)), ((), ())),
                preferred_element_type=f32,
            )
            grad_buf[which, cols, :] = out.astype(bf)
            return carry

        lax.fori_loop(0, 4, body, 0)
        copy = pltpu.make_async_copy(grad_buf.at[which], target, store_sem.at[which])
        copy.start()
        stores.append(copy)

    arrive(0)
    for load in loads:
        load.wait()
    arrive(1)
    forward(0)
    arrive(2)
    forward(1)
    compute(0)
    arrive(3)
    forward(2)
    compute(1)
    relay(0)
    forward(3)
    compute(2)
    relay(1)
    deliver(0)
    compute(3)
    relay(2)
    deliver(1)
    weight_grad(1, active, cots, outer_grad_hbm)
    relay(3)
    deliver(2)
    weight_grad(0, slots, pre, inner_grad_hbm)
    deliver(3)
    for kind in (0, 1):
        for q in range(4):
            view = sized.at[pl.ds(0, 15 if STEPS[q] == 0 else 16)]
            remote(view, view, there_s.at[kind, q], there_r.at[kind, q], to_right).wait_send()
    for copy in rings.values():
        copy.wait_send()
    for copy in folds.values():
        copy.wait_send()
    for kind in (0, 1):
        view = sized.at[pl.ds(0, 63)]
        remote(view, view, back_s.at[kind], back_r.at[kind], to_right).wait()
    for copy in selfs[2:] + stores:
        copy.wait()


def expert_pass(rows, cot, inner, outer):
    dma, bf = pltpu.SemaphoreType.DMA, jnp.bfloat16
    block = lambda *lead: pltpu.VMEM(lead + (64, 1024), bf)
    whole = jax.ShapeDtypeStruct((1024, 1024), bf)
    slot = jax.ShapeDtypeStruct((256, 1024), bf)
    vmem, anywhere = pl.BlockSpec(memory_space=pltpu.VMEM), pl.BlockSpec(memory_space=pl.ANY)
    return pl.pallas_call(
        expert_kernel,
        out_shape=(slot, slot, whole, whole),
        in_specs=[vmem, vmem, anywhere, anywhere],
        out_specs=(vmem, vmem, anywhere, anywhere),
        scratch_shapes=[block(4, 4)] * 4
        + [pltpu.VMEM((1024, 1024), bf)] * 2
        + [block(4, 4)] * 2
        + [block(4)] * 6
        + [pltpu.VMEM((2, 1024, 1024), bf), pltpu.VMEM((63, 4, 1024), bf)]
        + [
            dma((2,)),
            dma((4,)),
            dma((2, 4)),
            dma((2, 4)),
            dma((2, 3, 4)),
            dma((2, 3, 4)),
            dma((6, 4)),
            dma((6, 4)),
            dma((2,)),
            dma((2,)),
            dma((2,)),
        ],
        compiler_params=pltpu.CompilerParams(
            collective_id=2, has_side_effects=True, vmem_limit_bytes=VMEM_LIMIT
        ),
        name="expert_pass",
    )(rows, cot, inner, outer)


def per_device(frames, lengths, expert_ids, conv_in, depthwise, router, w_in, w_out, out_grad):
    tokens, width = frames.shape
    experts = router.shape[1]
    capacity = TOP * tokens // experts
    half_width = (KERNEL - 1) // 2
    packed = jnp.concatenate(
        [conv_in, router, jnp.pad(depthwise, ((0, 0), (0, WIDE - 2 * width - experts - KERNEL)))], axis=1
    )
    everything = gather_weights(packed).reshape(width, WIDE)
    conv_full = everything[:, : 2 * width]
    router_full = everything[:, 2 * width : 2 * width + experts]
    depth_full = everything[:, 2 * width + experts : 2 * width + experts + KERNEL]
    usable, kept_rows, slot_index, filled, source = routing(
        expert_ids, lengths[0], experts, capacity
    )
    frame_mask = usable.astype(jnp.float32)[:, None]
    frame_wide = frames.astype(jnp.float32)
    centred, inv_scale = normalize(frame_wide)
    normed = centred.astype(jnp.bfloat16)
    pointwise = jnp.dot(normed, conv_full, preferred_element_type=jnp.float32)
    value_half = pointwise[:, :width]
    gate_sig = jax.nn.sigmoid(pointwise[:, width:])
    gated = value_half * gate_sig * frame_mask
    tap_rows = depth_full.astype(jnp.float32).T
    conv_sum = depth_apply(gated, tap_rows, half_width)
    mixed_rows = (frame_wide + swish_of(conv_sum) * frame_mask).astype(jnp.bfloat16)
    logits = jnp.dot(mixed_rows, router_full, preferred_element_type=jnp.float32)
    onehots = (expert_ids[:, :, None] == jnp.arange(experts, dtype=jnp.int32)).astype(jnp.float32)
    chosen = jnp.sum(logits[:, None, :] * onehots, axis=-1)
    scores = jax.nn.sigmoid(chosen)
    score_sum = jnp.sum(scores, axis=-1, keepdims=True)
    weights = scores / score_sum
    kept_wide = kept_rows.reshape(tokens, TOP).astype(jnp.float32)
    send_rows = jnp.take(mixed_rows, source // TOP, axis=0)
    send_rows = jnp.where(filled[:, None], send_rows, jnp.zeros((), jnp.bfloat16)).reshape(
        experts, capacity, width
    )
    grad_wide = out_grad.astype(jnp.float32)
    slot_cot = (
        ((weights * kept_wide)[..., None] * grad_wide[:, None, :])
        .astype(jnp.bfloat16)
        .reshape(tokens * TOP, width)
    )
    cot_send = jnp.take(slot_cot, source, axis=0)
    cot_send = jnp.where(filled[:, None], cot_send, jnp.zeros((), jnp.bfloat16)).reshape(
        experts, capacity, width
    )
    expert_rows, back_rows, w_in_grad, w_out_grad = expert_pass(
        send_rows.reshape(-1, width), cot_send.reshape(-1, width), w_in[0], w_out[0]
    )
    picked = jnp.take(expert_rows, slot_index, axis=0).reshape(tokens, TOP, width)
    picked_wide = picked.astype(jnp.float32) * kept_wide[..., None]
    layer_out = (
        mixed_rows.astype(jnp.float32) + jnp.sum(weights[..., None] * picked_wide, axis=1)
    ).astype(jnp.bfloat16)
    conv_back, depth_back, router_back = conv_full, depth_full, router_full
    weight_grad = jnp.sum(grad_wide[:, None, :] * picked_wide, axis=-1)
    mean_term = jnp.sum(weight_grad * weights, axis=-1, keepdims=True)
    chosen_grad = (weight_grad - mean_term) / score_sum * scores * (1.0 - scores)
    logit_grad = jnp.sum(chosen_grad[..., None] * onehots, axis=1).astype(jnp.bfloat16)
    router_part = lax.dot_general(
        mixed_rows, logit_grad, (((0,), (0,)), ((), ())), preferred_element_type=jnp.float32
    )
    router_term = lax.dot_general(
        logit_grad, router_back, (((1,), (1,)), ((), ())), preferred_element_type=jnp.float32
    )
    slot_grad = jnp.take(back_rows, slot_index, axis=0).reshape(tokens, TOP, width)
    slot_grad = slot_grad.astype(jnp.float32) * kept_wide[..., None]
    mixed_grad = grad_wide + jnp.sum(slot_grad, axis=1) + router_term
    conv_grad = mixed_grad * frame_mask * swish_slope(conv_sum)
    tap_back = depth_back.astype(jnp.float32).T
    glu_grad = depth_transpose(conv_grad, tap_back, half_width) * frame_mask
    taps_grad = depth_taps_grad(conv_grad, gated, half_width)
    value_grad = glu_grad * gate_sig
    gate_grad = glu_grad * value_half * gate_sig * (1.0 - gate_sig)
    pre_cot = jnp.concatenate([value_grad, gate_grad], axis=-1).astype(jnp.bfloat16)
    conv_part = lax.dot_general(
        normed, pre_cot, (((0,), (0,)), ((), ())), preferred_element_type=jnp.float32
    )
    normed_grad = lax.dot_general(
        pre_cot, conv_back, (((1,), (1,)), ((), ())), preferred_element_type=jnp.float32
    )
    frames_grad = (mixed_grad + norm_backward(normed_grad, centred, inv_scale)).astype(jnp.bfloat16)
    small = jnp.concatenate(
        [router_part, taps_grad.T, jnp.zeros((width, WIDE - 2 * width - experts - KERNEL), jnp.float32)], axis=1
    )
    part = jnp.concatenate([conv_part.astype(jnp.bfloat16), small.astype(jnp.bfloat16)], axis=1)
    summed = reduce_grads(part.reshape(4, width // 4, WIDE))
    conv_in_grad = summed[:, : 2 * width]
    router_grad = summed[:, 2 * width : 2 * width + experts]
    depthwise_grad = summed[:, 2 * width + experts : 2 * width + experts + KERNEL]
    return (
        layer_out,
        frames_grad,
        conv_in_grad,
        depthwise_grad,
        router_grad,
        w_in_grad[None],
        w_out_grad[None],
    )


def solution(mesh):
    in_specs = (
        P(("dp", "expert"), None),
        P(("dp", "expert")),
        P(("dp", "expert"), None),
        P(("dp", "expert"), None),
        P(("dp", "expert"), None),
        P(("dp", "expert"), None),
        P("expert", None, "dp"),
        P("expert", "dp", None),
        P(("dp", "expert"), None),
    )
    out_specs = (
        P(("dp", "expert"), None),
        P(("dp", "expert"), None),
        P(("dp", "expert"), None),
        P(("dp", "expert"), None),
        P(("dp", "expert"), None),
        P("expert", None, "dp"),
        P("expert", "dp", None),
    )
    return jax.shard_map(
        per_device, mesh=mesh, in_specs=in_specs, out_specs=out_specs, check_vma=False
    )
```

```python
import jax
import jax.numpy as jnp
from jax import lax
from jax.experimental import pallas as pl
from jax.experimental.pallas import tpu as pltpu
from jax.sharding import PartitionSpec as P

KERNEL = 31
EPSILON = 1e-05


def swish_of(values):
    return values * jax.nn.sigmoid(values)


def swish_slope(values):
    sigmoid_v = jax.nn.sigmoid(values)
    return sigmoid_v * (1.0 + values * (1.0 - sigmoid_v))


def normalize(values):
    center = values - jnp.mean(values, axis=-1, keepdims=True)
    inv_scale = lax.rsqrt(jnp.mean(center * center, axis=-1, keepdims=True) + EPSILON)
    return (center * inv_scale, inv_scale)


MESH = pl.DeviceIdType.MESH
HALF = 1152
WIDE = 2 * HALF
SPLIT = 640
VMEM_LIMIT = 60 * 1024 * 1024


def place():
    x = lax.axis_index("dp")
    e = lax.axis_index("expert")
    return x, e // 16, (e // 2) % 8, e % 2


def spot(x, y, z, c):
    return (x, y * 16 + z * 2 + c)


def remote(src, dst, send, recv, where):
    return pltpu.make_async_remote_copy(
        src_ref=src, dst_ref=dst, send_sem=send, recv_sem=recv, device_id=where, device_id_type=MESH
    )


def greet(targets):
    barrier = pltpu.get_barrier_semaphore()
    for where in targets:
        pl.semaphore_signal(barrier, inc=1, device_id=where, device_id_type=MESH)
    pl.semaphore_wait(barrier, len(targets))


def axis_peers(x, y, z, c):
    peers = [spot(x, y, z, 1 - c)]
    peers += [spot(x, y, (z + dz) % 8, c) for dz in range(1, 8)]
    peers += [spot(x, (y + dy) % 4, z, c) for dy in (1, 3)]
    peers += [spot((x + dx) % 4, y, z, c) for dx in (1, 3)]
    return peers


def gather_kernel(own_ref, out_ref, core_s, core_r, own_sem, z_s, z_r, ring_s, ring_r, tail_s, tail_r):
    x, y, z, c = place()
    greet(axis_peers(x, y, z, c))
    partner = spot(x, y, z, 1 - c)
    mine = pl.multiple_of(c * HALF, 128)
    other = pl.multiple_of((1 - c) * HALF, 128)
    row = pl.multiple_of(y * 64 + z * 8, 8)
    row4 = pl.multiple_of(row + 4 * c, 4)
    swap = remote(
        own_ref.at[:, pl.ds(other, HALF)],
        out_ref.at[x, pl.ds(row4, 4), pl.ds(other, HALF)],
        core_s,
        core_r,
        partner,
    )
    swap.start()
    keep = pltpu.make_async_copy(
        own_ref.at[:, pl.ds(mine, HALF)], out_ref.at[x, pl.ds(row4, 4), pl.ds(mine, HALF)], own_sem
    )
    keep.start()
    keep.wait()
    swap.wait()
    copies = []
    for dz in (4, 3, 5, 2, 6, 1, 7):
        block = out_ref.at[x, pl.ds(row, 8), pl.ds(mine, HALF)]
        copy = remote(block, block, z_s.at[dz - 1], z_r.at[dz - 1], spot(x, y, (z + dz) % 8, c))
        copy.start()
        copies.append(copy)
    for copy in copies:
        copy.wait()

    first = pl.multiple_of(mine, 128)
    second = pl.multiple_of(mine + SPLIT, 128)
    yrow = pl.multiple_of(y * 64, 64)

    def block_of(colour, level, index, part):
        cols = pl.ds(first, SPLIT) if colour == 0 else pl.ds(second, HALF - SPLIT)
        if level == 0:
            height = 64 if part is None else 32
            offset = 0 if part is None else part * 32
            if colour == 0:
                return out_ref.at[x, pl.ds(pl.multiple_of(index * 64 + offset, 32), height), cols]
            return out_ref.at[index, pl.ds(pl.multiple_of(yrow + offset, 32), height), cols]
        if colour == 0:
            height = 256 if part is None else 128
            offset = 0 if part is None else part * 128
            return out_ref.at[index, pl.ds(offset, height), cols]
        height = 64 if part is None else 32
        offset = 0 if part is None else part * 32
        return out_ref.at[:, pl.ds(pl.multiple_of(index * 64 + offset, 32), height), cols]

    def whereto(colour, level, step):
        if (colour + level) % 2 == 0:
            return spot(x, (y + step) % 4, z, c)
        return spot((x + step) % 4, y, z, c)

    def position(colour, level):
        return y if (colour + level) % 2 == 0 else x

    def opened(colour, level):
        at = position(colour, level)
        block = block_of(colour, level, at, None)
        base = (colour * 2 + level) * 4
        right = remote(block, block, ring_s.at[base], ring_r.at[base], whereto(colour, level, 1))
        left = remote(block, block, ring_s.at[base + 1], ring_r.at[base + 1], whereto(colour, level, 3))
        right.start()
        left.start()
        return right, left

    def passed(colour, level, pair, tell):
        at = position(colour, level)
        base = (colour * 2 + level) * 4
        right, left = pair
        right.wait_recv()
        block = block_of(colour, level, (at + 3) % 4, 0)
        on_right = remote(block, block, ring_s.at[base + 2], ring_r.at[base + 2], whereto(colour, level, 1))
        on_right.start()
        tell((at + 3) % 4, 1)
        left.wait_recv()
        block = block_of(colour, level, (at + 1) % 4, 1)
        on_left = remote(block, block, ring_s.at[base + 3], ring_r.at[base + 3], whereto(colour, level, 3))
        on_left.start()
        tell((at + 1) % 4, 2)
        return on_right, on_left

    def closed(colour, level, pair, onward, tell):
        at = position(colour, level)
        for copy in onward:
            copy.wait_recv()
        tell((at + 2) % 4, 3)
        for copy in pair + onward:
            copy.wait_send()

    silent = lambda index, slot: None
    low = [opened(colour, 0) for colour in (0, 1)]
    low_on = [passed(colour, 0, low[colour], silent) for colour in (0, 1)]
    for colour in (0, 1):
        closed(colour, 0, low[colour], low_on[colour], silent)
    tails = []

    def teller(colour):
        def tell(index, slot):
            block = block_of(colour, 1, index, None)
            at = colour * 4 + slot
            copy = remote(block, block, tail_s.at[at], tail_r.at[at], partner)
            copy.start()
            tails.append(copy)

        return tell

    high = [opened(colour, 1) for colour in (0, 1)]
    for colour in (0, 1):
        teller(colour)(position(colour, 1), 0)
    high_on = [passed(colour, 1, high[colour], teller(colour)) for colour in (0, 1)]
    for colour in (0, 1):
        closed(colour, 1, high[colour], high_on[colour], teller(colour))
    for copy in tails:
        copy.wait()


def gather_weights(packed):
    dma = pltpu.SemaphoreType.DMA
    return pl.pallas_call(
        gather_kernel,
        out_shape=jax.ShapeDtypeStruct((4, 256, WIDE), jnp.bfloat16),
        in_specs=[pl.BlockSpec(memory_space=pltpu.VMEM)],
        out_specs=pl.BlockSpec(memory_space=pltpu.VMEM),
        scratch_shapes=[dma, dma, dma, dma((7,)), dma((7,)), dma((16,)), dma((16,)), dma((8,)), dma((8,))],
        compiler_params=pltpu.CompilerParams(
            collective_id=0, has_side_effects=True, vmem_limit_bytes=VMEM_LIMIT
        ),
        name="gather_weights",
    )(packed)


def reduce_kernel(
    part_ref, out_ref, depth_ref, router_ref, swap_buf, half_buf, far_buf, near_buf, mid_buf, mid_far, mid_near, z_src, z_buf, last_src,
    last_buf, swap_s, swap_r, ring_s, ring_r, z_s, z_r, last_s, last_r
):
    x, y, z, c = place()
    greet(axis_peers(x, y, z, c))
    partner = spot(x, y, z, 1 - c)
    mine = pl.multiple_of(c * HALF, 128)
    other = pl.multiple_of((1 - c) * HALF, 128)
    colours = ((0, SPLIT), (SPLIT, HALF - SPLIT))
    order = (2, 1, 3, 0)

    def rows_of(colour, index):
        if colour == 0:
            return index, pl.ds(0, 256)
        return slice(None), pl.ds(pl.multiple_of(index * 64, 64), 64)

    swaps = {}
    for step in order:
        for colour, (begin, width) in enumerate(colours):
            at = ((x if colour == 0 else y) + step) % 4
            lead, rows = rows_of(colour, at)
            slot = colour * 4 + step
            copy = remote(
                part_ref.at[lead, rows, pl.ds(pl.multiple_of(other + begin, 128), width)],
                swap_buf.at[lead, rows, pl.ds(begin, width)],
                swap_s.at[slot],
                swap_r.at[slot],
                partner,
            )
            copy.start()
            swaps[colour, step] = copy

    def first_to(colour, step):
        if colour == 0:
            return spot((x + step) % 4, y, z, c)
        return spot(x, (y + step) % 4, z, c)

    def second_to(colour, step):
        return first_to(1 - colour, step)

    def fold(colour, step, extra):
        begin, width = colours[colour]
        at = ((x if colour == 0 else y) + step) % 4
        swaps[colour, step].wait_recv()

        def body(t, carry):
            if colour == 0:
                lead, row = at, pl.multiple_of(t * 32, 32)
            else:
                lead, row = t // 2, pl.multiple_of(at * 64 + (t % 2) * 32, 32)
            value = part_ref[lead, pl.ds(row, 32), pl.ds(pl.multiple_of(mine + begin, 128), width)].astype(jnp.float32)
            value = value + swap_buf[lead, pl.ds(row, 32), pl.ds(begin, width)].astype(jnp.float32)
            value = extra(t, value)
            half_buf[colour, step, pl.ds(pl.multiple_of(t * 32, 32), 32), pl.ds(0, width)] = value.astype(jnp.bfloat16)
            return carry

        return body

    plain = lambda t, value: value
    sent = []
    pend = {}
    for colour, (begin, width) in enumerate(colours):
        lax.fori_loop(0, 8, fold(colour, 2, plain), 0)
        for side, step in ((0, 1), (1, 3)):
            slot = colour * 8 + side
            copy = remote(
                half_buf.at[colour, 2, pl.ds(side * 128, 128), pl.ds(0, width)],
                far_buf.at[colour, side, :, pl.ds(0, width)],
                ring_s.at[slot],
                ring_r.at[slot],
                first_to(colour, step),
            )
            copy.start()
            pend[colour, side] = copy
            sent.append(copy)
    for colour, (begin, width) in enumerate(colours):
        for side, step in ((0, 1), (1, 3)):
            lo = side * 4

            lax.fori_loop(4 - lo, 8 - lo, fold(colour, step, plain), 0)
            pend[colour, side].wait_recv()

            def extra(t, value, colour=colour, side=side, lo=lo, width=width):
                row = pl.multiple_of((t - lo) * 32, 32)
                return value + far_buf[colour, side, pl.ds(row, 32), pl.ds(0, width)].astype(jnp.float32)

            def again(t, carry, colour=colour, step=step, extra=extra, begin=begin, width=width):
                at = ((x if colour == 0 else y) + step) % 4
                if colour == 0:
                    lead, row = at, pl.multiple_of(t * 32, 32)
                else:
                    lead, row = t // 2, pl.multiple_of(at * 64 + (t % 2) * 32, 32)
                value = part_ref[lead, pl.ds(row, 32), pl.ds(pl.multiple_of(mine + begin, 128), width)].astype(jnp.float32)
                value = value + swap_buf[lead, pl.ds(row, 32), pl.ds(begin, width)].astype(jnp.float32)
                value = extra(t, value)
                half_buf[colour, step, pl.ds(pl.multiple_of(t * 32, 32), 32), pl.ds(0, width)] = value.astype(jnp.bfloat16)
                return carry

            lax.fori_loop(lo, lo + 4, again, 0)
            slot = colour * 8 + 2 + side
            copy = remote(
                half_buf.at[colour, step, :, pl.ds(0, width)],
                near_buf.at[colour, side, :, pl.ds(0, width)],
                ring_s.at[slot],
                ring_r.at[slot],
                first_to(colour, step),
            )
            copy.start()
            pend[colour, 2 + side] = copy
            sent.append(copy)
    for colour, (begin, width) in enumerate(colours):
        pend[colour, 2].wait_recv()
        pend[colour, 3].wait_recv()

        def extra(t, value, colour=colour, width=width):
            row = pl.multiple_of(t * 32, 32)
            for side in (0, 1):
                value = value + near_buf[colour, side, pl.ds(row, 32), pl.ds(0, width)].astype(jnp.float32)
            return value

        body = fold(colour, 0, extra)
        lax.fori_loop(0, 8, body, 0)
        at = y if colour == 0 else x
        for side, step in ((0, 1), (1, 3)):
            row = pl.multiple_of(((at + 2) % 4) * 64 + side * 32, 32)
            slot = colour * 8 + 4 + side
            copy = remote(
                half_buf.at[colour, 0, pl.ds(row, 32), pl.ds(0, width)],
                mid_far.at[colour, side, :, pl.ds(0, width)],
                ring_s.at[slot],
                ring_r.at[slot],
                second_to(colour, step),
            )
            copy.start()
            pend[colour, 4 + side] = copy
            sent.append(copy)
    for colour, (begin, width) in enumerate(colours):
        at = y if colour == 0 else x
        for side, step in ((0, 1), (1, 3)):
            row = pl.multiple_of(((at + step) % 4) * 64, 32)
            pend[colour, 4 + side].wait_recv()
            for piece in (0, 1):
                value = half_buf[colour, 0, pl.ds(pl.multiple_of(row + piece * 32, 32), 32), pl.ds(0, width)]
                if piece == side:
                    value = value.astype(jnp.float32) + mid_far[colour, side, :, pl.ds(0, width)].astype(jnp.float32)
                    value = value.astype(jnp.bfloat16)
                mid_buf[colour, side, pl.ds(piece * 32, 32), pl.ds(0, width)] = value
            slot = colour * 8 + 6 + side
            copy = remote(
                mid_buf.at[colour, side, :, pl.ds(0, width)],
                mid_near.at[colour, side, :, pl.ds(0, width)],
                ring_s.at[slot],
                ring_r.at[slot],
                second_to(colour, step),
            )
            copy.start()
            pend[colour, 6 + side] = copy
            sent.append(copy)
    for colour, (begin, width) in enumerate(colours):
        at = y if colour == 0 else x
        pend[colour, 6].wait_recv()
        pend[colour, 7].wait_recv()
        for piece in range(2):
            rows = pl.ds(piece * 32, 32)
            value = half_buf[colour, 0, pl.ds(pl.multiple_of(at * 64 + piece * 32, 32), 32), pl.ds(0, width)].astype(jnp.float32)
            for side in (0, 1):
                value = value + mid_near[colour, side, rows, pl.ds(0, width)].astype(jnp.float32)
            z_src[pl.ds(piece * 4, 4), :, pl.ds(begin, width)] = value.astype(jnp.bfloat16).reshape(4, 8, width)
    z_copies = []
    for dz in (4, 3, 5, 2, 6, 1, 7):
        to = (z + dz) % 8
        copy = remote(z_src.at[to], z_buf.at[dz - 1], z_s.at[dz - 1], z_r.at[dz - 1], spot(x, y, to, c))
        copy.start()
        z_copies.append(copy)
    total = z_src[z].astype(jnp.float32)
    for copy in z_copies:
        copy.wait_recv()
    for k in range(7):
        total = total + z_buf[k].astype(jnp.float32)
    last_src[...] = total
    last = remote(last_src, last_buf, last_s, last_r, partner)
    last.start()
    for copy in sent + z_copies:
        copy.wait_send()
    for copy in swaps.values():
        copy.wait_send()
    kept = jnp.where(c == 0, last_src[0:4, :], last_src[4:8, :])
    last.wait()
    got = jnp.where(c == 0, last_buf[0:4, :], last_buf[4:8, :])
    low, high = jnp.where(c == 0, kept, got), jnp.where(c == 0, got, kept)
    out_ref[:, 0:HALF] = low
    out_ref[:, HALF:2048] = high[:, 0 : 2048 - HALF]
    router_ref[...] = high[:, 2048 - HALF : 2112 - HALF]
    depth_ref[...] = high[:, 2112 - HALF : 2112 + KERNEL - HALF]


def reduce_grads(part):
    dma = pltpu.SemaphoreType.DMA
    bf, wide = jnp.bfloat16, SPLIT
    return pl.pallas_call(
        reduce_kernel,
        out_shape=tuple(jax.ShapeDtypeStruct((4, width), jnp.float32) for width in (2048, KERNEL, 64)),
        in_specs=[pl.BlockSpec(memory_space=pltpu.VMEM)],
        out_specs=(pl.BlockSpec(memory_space=pltpu.VMEM),) * 3,
        scratch_shapes=[
            pltpu.VMEM((4, 256, HALF), bf),
            pltpu.VMEM((2, 4, 256, wide), bf),
            pltpu.VMEM((2, 2, 128, wide), bf),
            pltpu.VMEM((2, 2, 256, wide), bf),
            pltpu.VMEM((2, 2, 64, wide), bf),
            pltpu.VMEM((2, 2, 32, wide), bf),
            pltpu.VMEM((2, 2, 64, wide), bf),
            pltpu.VMEM((8, 8, HALF), bf),
            pltpu.VMEM((7, 8, HALF), bf),
            pltpu.VMEM((8, HALF), jnp.float32),
            pltpu.VMEM((8, HALF), jnp.float32),
            dma((8,)),
            dma((8,)),
            dma((16,)),
            dma((16,)),
            dma((7,)),
            dma((7,)),
            dma,
            dma,
        ],
        compiler_params=pltpu.CompilerParams(
            collective_id=1, has_side_effects=True, vmem_limit_bytes=VMEM_LIMIT
        ),
        name="reduce_grads",
    )(part)


STEPS = (0, 1, 3, 2)


def expert_kernel(
    rows_ref, cot_ref, inner_hbm, outer_hbm, y_ref, z_ref, inner_grad_hbm, outer_grad_hbm,
    slots, cots, active, pre, inner, outer, part_y, part_z, straight_y, straight_z, relay_y, relay_z, joint_y, joint_z,
    grad_buf, sized, load_sem, self_s, there_s, there_r, ring_s, ring_r, fold_s, fold_r, back_s, back_r, store_sem
):
    x, y, z, c = place()
    f32, bf = jnp.float32, jnp.bfloat16
    here = y * 16 + z * 2 + c
    right, left, far = (x + 1) % 4, (x + 3) % 4, (x + 2) % 4
    to_right, to_left = spot(right, y, z, c), spot(left, y, z, c)
    loads = [
        pltpu.make_async_copy(inner_hbm, inner, load_sem.at[0]),
        pltpu.make_async_copy(outer_hbm, outer, load_sem.at[1]),
    ]
    for load in loads:
        load.start()

    barrier = pltpu.get_barrier_semaphore()

    def hail(i, carry):
        pl.semaphore_signal(barrier, inc=1, device_id=(x, (here + i) % 64), device_id_type=MESH)
        return carry

    lax.fori_loop(1, 64, hail, 0)
    for where in (to_right, to_left):
        pl.semaphore_signal(barrier, inc=1, device_id=where, device_id_type=MESH)
    pl.semaphore_wait(barrier, 65)

    own4 = pl.multiple_of(4 * here, 4)
    line4 = pl.multiple_of(8 * z + 4 * c, 4)
    kinds = ((rows_ref, slots), (cot_ref, cots))
    selfs = []
    for kind, (source, target) in enumerate(kinds):
        copy = pltpu.make_async_copy(
            source.at[pl.ds(own4, 4)], target.at[x, y, pl.ds(line4, 4)], self_s.at[kind]
        )
        copy.start()
        selfs.append(copy)
    for q, dy in enumerate(STEPS):
        yt = (y + 4 - dy) % 4

        def there(i, carry, yt=yt, q=q):
            zt, ct = (z + 4 + i // 2) % 8, (c + i) % 2
            et = yt * 16 + zt * 2 + ct
            rows = pl.ds(pl.multiple_of(4 * et, 4), 4)
            for kind, (source, target) in enumerate(kinds):
                remote(
                    source.at[rows], target.at[x, y, pl.ds(line4, 4)], there_s.at[kind, q], there_r.at[kind, q], (x, et)
                ).start()
            return carry

        if dy == 0:
            lax.fori_loop(0, 8, there, 0)
            lax.fori_loop(9, 16, there, 0)
        else:
            lax.fori_loop(0, 16, there, 0)

    def source_y(q):
        return (y + STEPS[q]) % 4

    rings = {}

    def arrive(q):
        ys = source_y(q)
        if STEPS[q] == 0:
            for copy in selfs:
                copy.wait()
        for kind, (_, target) in enumerate(kinds):
            view = sized.at[pl.ds(0, 15 if STEPS[q] == 0 else 16)]
            remote(view, view, there_s.at[kind, q], there_r.at[kind, q], to_right).wait_recv()
            block = target.at[x, ys]
            for side, where in ((0, to_right), (1, to_left)):
                copy = remote(block, block, ring_s.at[kind, side, q], ring_r.at[kind, side, q], where)
                copy.start()
                rings[kind, side, q] = copy

    def forward(q):
        ys = source_y(q)
        for kind, side, at, where in ((0, 0, left, to_right), (1, 1, right, to_left)):
            rings[kind, side, q].wait_recv()
            block = kinds[kind][1].at[at, ys]
            copy = remote(block, block, ring_s.at[kind, 2, q], ring_r.at[kind, 2, q], where)
            copy.start()
            rings[kind, 2, q] = copy

    folds = {}

    def push(name, q, source, target, where):
        copy = remote(source, target, fold_s.at[name, q], fold_r.at[name, q], where)
        copy.start()
        folds[name, q] = copy

    def compute(q):
        ys = source_y(q)
        rings[0, 1, q].wait_recv()
        rings[1, 0, q].wait_recv()
        rings[0, 2, q].wait_recv()
        rings[1, 2, q].wait_recv()

        def first(n, carry):
            cols = pl.ds(pl.multiple_of(n * 256, 256), 256)
            hidden = jnp.dot(slots[:, ys].reshape(256, 1024), inner[:, cols], preferred_element_type=f32)
            act_grad = lax.dot_general(
                cots[:, ys].reshape(256, 1024), outer[cols, :], (((1,), (1,)), ((), ())), preferred_element_type=f32
            )
            sig = jax.nn.sigmoid(hidden)
            active[:, ys, :, cols] = (hidden * sig).astype(bf).reshape(4, 64, 256)
            slope = sig * (1.0 + hidden * (1.0 - sig))
            pre[:, ys, :, cols] = (act_grad * slope).astype(bf).reshape(4, 64, 256)
            return carry

        lax.fori_loop(0, 4, first, 0)

        def second(n, carry):
            cols = pl.ds(pl.multiple_of(n * 256, 256), 256)
            out = jnp.dot(active[:, ys].reshape(256, 1024), outer[:, cols], preferred_element_type=f32)
            part_y[q, :, :, cols] = out.astype(bf).reshape(4, 64, 256)
            out = lax.dot_general(
                pre[:, ys].reshape(256, 1024), inner[cols, :], (((1,), (1,)), ((), ())), preferred_element_type=f32
            )
            part_z[q, :, :, cols] = out.astype(bf).reshape(4, 64, 256)
            return carry

        lax.fori_loop(0, 4, second, 0)
        push(2, q, part_y.at[q, far], relay_y.at[q], to_right)
        push(3, q, part_z.at[q, far], relay_z.at[q], to_left)
        push(0, q, part_z.at[q, right], straight_z.at[q], to_right)
        push(1, q, part_y.at[q, left], straight_y.at[q], to_left)

    def relay(q):
        folds[2, q].wait_recv()
        part_y[q, right] = (part_y[q, right].astype(f32) + relay_y[q].astype(f32)).astype(bf)
        push(4, q, part_y.at[q, right], joint_y.at[q], to_right)
        folds[3, q].wait_recv()
        part_z[q, left] = (part_z[q, left].astype(f32) + relay_z[q].astype(f32)).astype(bf)
        push(5, q, part_z.at[q, left], joint_z.at[q], to_left)

    def deliver(q):
        yt = source_y(q)
        for name in (1, 4, 0, 5):
            folds[name, q].wait_recv()
        part_y[q, x] = (part_y[q, x].astype(f32) + straight_y[q].astype(f32) + joint_y[q].astype(f32)).astype(bf)
        part_z[q, x] = (part_z[q, x].astype(f32) + straight_z[q].astype(f32) + joint_z[q].astype(f32)).astype(bf)

        def back(i, carry):
            zt, ct = (z + 4 + i // 2) % 8, (c + i) % 2
            rows = pl.ds(pl.multiple_of(8 * zt + 4 * ct, 4), 4)
            for kind, (source, target) in enumerate(((part_y, y_ref), (part_z, z_ref))):
                remote(
                    source.at[q, x, rows], target.at[pl.ds(own4, 4)], back_s.at[kind], back_r.at[kind], (x, yt * 16 + zt * 2 + ct)
                ).start()
            return carry

        if STEPS[q] == 0:
            lax.fori_loop(0, 8, back, 0)
            lax.fori_loop(9, 16, back, 0)
            for kind, (source, target) in enumerate(((part_y, y_ref), (part_z, z_ref))):
                copy = pltpu.make_async_copy(
                    source.at[q, x, pl.ds(line4, 4)], target.at[pl.ds(own4, 4)], self_s.at[2 + kind]
                )
                copy.start()
                selfs.append(copy)
        else:
            lax.fori_loop(0, 16, back, 0)

    stores = []

    def weight_grad(which, left_ref, right_ref, target):
        def body(n, carry):
            cols = pl.ds(pl.multiple_of(n * 256, 256), 256)
            out = lax.dot_general(
                left_ref[:, :, :, cols].reshape(1024, 256),
                right_ref[...].reshape(1024, 1024),
                (((0,), (0,)), ((), ())),
                preferred_element_type=f32,
            )
            grad_buf[which, cols, :] = out.astype(bf)
            return carry

        lax.fori_loop(0, 4, body, 0)
        copy = pltpu.make_async_copy(grad_buf.at[which], target, store_sem.at[which])
        copy.start()
        stores.append(copy)

    arrive(0)
    for load in loads:
        load.wait()
    arrive(1)
    forward(0)
    arrive(2)
    forward(1)
    compute(0)
    arrive(3)
    forward(2)
    compute(1)
    relay(0)
    forward(3)
    compute(2)
    relay(1)
    deliver(0)
    compute(3)
    relay(2)
    deliver(1)
    weight_grad(1, active, cots, outer_grad_hbm)
    relay(3)
    deliver(2)
    weight_grad(0, slots, pre, inner_grad_hbm)
    deliver(3)
    for kind in (0, 1):
        for q in range(4):
            view = sized.at[pl.ds(0, 15 if STEPS[q] == 0 else 16)]
            remote(view, view, there_s.at[kind, q], there_r.at[kind, q], to_right).wait_send()
    for copy in rings.values():
        copy.wait_send()
    for copy in folds.values():
        copy.wait_send()
    for kind in (0, 1):
        view = sized.at[pl.ds(0, 63)]
        remote(view, view, back_s.at[kind], back_r.at[kind], to_right).wait()
    for copy in selfs[2:] + stores:
        copy.wait()


def expert_pass(rows, cot, inner, outer):
    dma, bf = pltpu.SemaphoreType.DMA, jnp.bfloat16
    block = lambda *lead: pltpu.VMEM(lead + (64, 1024), bf)
    whole = jax.ShapeDtypeStruct((1024, 1024), bf)
    slot = jax.ShapeDtypeStruct((256, 1024), bf)
    vmem, anywhere = pl.BlockSpec(memory_space=pltpu.VMEM), pl.BlockSpec(memory_space=pl.ANY)
    return pl.pallas_call(
        expert_kernel,
        out_shape=(slot, slot, whole, whole),
        in_specs=[vmem, vmem, anywhere, anywhere],
        out_specs=(vmem, vmem, anywhere, anywhere),
        scratch_shapes=[block(4, 4)] * 4
        + [pltpu.VMEM((1024, 1024), bf)] * 2
        + [block(4, 4)] * 2
        + [block(4)] * 6
        + [pltpu.VMEM((2, 1024, 1024), bf), pltpu.VMEM((63, 4, 1024), bf)]
        + [
            dma((2,)),
            dma((4,)),
            dma((2, 4)),
            dma((2, 4)),
            dma((2, 3, 4)),
            dma((2, 3, 4)),
            dma((6, 4)),
            dma((6, 4)),
            dma((2,)),
            dma((2,)),
            dma((2,)),
        ],
        compiler_params=pltpu.CompilerParams(
            collective_id=2, has_side_effects=True, vmem_limit_bytes=VMEM_LIMIT
        ),
        name="expert_pass",
    )(rows, cot, inner, outer)


def columns_of(n, width):
    return pl.ds(pl.multiple_of(n * width, width), width)


def mask_of(length_ref):
    return (lax.broadcasted_iota(jnp.int32, (128, 1), 0) < length_ref[0]).astype(jnp.float32)


def chosen_of(ids_ref):
    lane = lax.broadcasted_iota(jnp.int32, (128, 128), 1)
    return [lane == ids_ref[:, k : k + 1] for k in (0, 1)]


def identity():
    shape = (128, 128)
    return (lax.broadcasted_iota(jnp.int32, shape, 0) == lax.broadcasted_iota(jnp.int32, shape, 1)).astype(jnp.bfloat16)


def front_kernel(
    frames_ref, length_ref, ids_ref, og_ref, full_ref, rows_ref, cot_ref, mixed_ref, value_ref, sig_ref, conv_ref,
    xhat_ref, notes_ref, gated_ref, taps_ref
):
    f32, bf = jnp.float32, jnp.bfloat16
    mask = mask_of(length_ref)
    xhat, inv_scale = normalize(frames_ref[...].astype(f32))
    xhat_ref[...] = xhat
    normed = xhat.astype(bf)
    zeros = jnp.zeros((16, 1024), f32)
    gated_ref[0:16, :] = zeros
    gated_ref[144:160, :] = zeros

    def point(n, carry):
        cols = columns_of(n, 256)
        value = jnp.dot(normed, full_ref[:, :, cols].reshape(1024, 256), preferred_element_type=f32)
        gate = jnp.dot(normed, full_ref[:, :, columns_of(n + 4, 256)].reshape(1024, 256), preferred_element_type=f32)
        sig = jax.nn.sigmoid(gate)
        value_ref[:, cols] = value
        sig_ref[:, cols] = sig
        gated_ref[16:144, cols] = value * sig * mask
        return carry

    lax.fori_loop(0, 4, point, 0)
    small = full_ref[:, :, 2048:2176].reshape(1024, 128)
    taps_ref[...] = lax.dot_general(identity(), small, (((1,), (1,)), ((), ())), preferred_element_type=f32)

    def depth(n, carry):
        cols = columns_of(n, 128)
        total = jnp.zeros((128, 128), f32)
        for k in range(KERNEL):
            total = total + taps_ref[64 + k : 65 + k, cols] * gated_ref[k + 1 : k + 129, cols]
        conv_ref[:, cols] = total
        mixed_ref[:, cols] = (frames_ref[:, cols].astype(f32) + swish_of(total) * mask).astype(bf)
        return carry

    lax.fori_loop(0, 8, depth, 0)
    mixed = mixed_ref[...]
    logits = jnp.dot(mixed, small, preferred_element_type=f32)
    picks = chosen_of(ids_ref)
    scores = [jax.nn.sigmoid(jnp.sum(jnp.where(pick, logits, 0.0), axis=1, keepdims=True)) for pick in picks]
    score_sum = scores[0] + scores[1]
    weights = [score / score_sum for score in scores]
    count = (jnp.where(picks[0] | picks[1], 1.0, 0.0) * mask).astype(bf)
    shape = (128, 128)
    below = (lax.broadcasted_iota(jnp.int32, shape, 1) < lax.broadcasted_iota(jnp.int32, shape, 0)).astype(bf)
    before = jnp.dot(below, count, preferred_element_type=f32)
    wide = lax.broadcasted_iota(jnp.int32, (128, 256), 1).astype(f32)
    slots, spots = [], []
    for k, pick in enumerate(picks):
        position = jnp.sum(jnp.where(pick, before, 0.0), axis=1, keepdims=True)
        kept = (position < 4.0) & (mask > 0.0)
        slot = jnp.where(kept, ids_ref[:, k : k + 1].astype(f32) * 4.0 + position, -1.0)
        slots.append(slot)
        spots.append((wide == slot).astype(bf))
    lane = lax.broadcasted_iota(jnp.int32, shape, 1)
    notes = jnp.zeros(shape, f32)
    for i, column in enumerate(weights + scores + [score_sum] + slots + [inv_scale]):
        notes = jnp.where(lane == i, column, notes)
    notes_ref[...] = notes
    both = spots[0] + spots[1]

    def fill(n, carry):
        cols = columns_of(n, 256)
        down = (((0,), (0,)), ((), ()))
        rows_ref[:, cols] = lax.dot_general(both, mixed_ref[:, cols], down, preferred_element_type=f32).astype(bf)
        og = og_ref[:, cols].astype(f32)
        total = jnp.zeros((256, 256), f32)
        for k in (0, 1):
            total = total + lax.dot_general(
                spots[k], (weights[k] * og).astype(bf), down, preferred_element_type=f32
            )
        cot_ref[:, cols] = total.astype(bf)
        return carry

    lax.fori_loop(0, 4, fill, 0)


def front(frames, lengths, ids, og, full):
    bf, f32 = jnp.bfloat16, jnp.float32
    vmem = pl.BlockSpec(memory_space=pltpu.VMEM)
    shape = lambda *args: jax.ShapeDtypeStruct(*args)
    return pl.pallas_call(
        front_kernel,
        out_shape=(
            shape((256, 1024), bf), shape((256, 1024), bf), shape((128, 1024), bf), shape((128, 1024), f32),
            shape((128, 1024), f32), shape((128, 1024), f32), shape((128, 1024), f32), shape((128, 128), f32),
            shape((160, 1024), f32), shape((128, 1024), f32),
        ),
        in_specs=[vmem, pl.BlockSpec(memory_space=pltpu.SMEM), vmem, vmem, vmem],
        out_specs=(vmem,) * 10,
        compiler_params=pltpu.CompilerParams(vmem_limit_bytes=VMEM_LIMIT),
        name="front",
    )(frames, lengths, ids, og, full)


def back_kernel(
    y_ref, z_ref, og_ref, mixed_ref, value_ref, sig_ref, conv_ref, xhat_ref, notes_ref, gated_ref, taps_ref, length_ref,
    ids_ref, full_ref, inner_ref, outer_ref, layer_ref, frames_ref, part_ref, inner_out, outer_out, pass_buf, pass_s,
    mg_buf, cg_buf, tg_buf, pc_buf, turned, ng_buf
):
    f32, bf = jnp.float32, jnp.bfloat16
    takes = [pltpu.make_async_copy(src, pass_buf.at[i], pass_s.at[i]) for i, src in enumerate((inner_ref, outer_ref))]
    gives = [pltpu.make_async_copy(pass_buf.at[i], dst, pass_s.at[2 + i]) for i, dst in enumerate((inner_out, outer_out))]
    for take in takes:
        take.start()
    mask = mask_of(length_ref)
    picks = chosen_of(ids_ref)
    notes = notes_ref[...]
    column = lambda i: notes[:, i : i + 1]
    weights, scores, score_sum, inv_scale = (column(0), column(1)), (column(2), column(3)), column(4), column(7)
    wide = lax.broadcasted_iota(jnp.int32, (128, 256), 1).astype(f32)
    spots = [(wide == column(5 + k)).astype(bf) for k in (0, 1)]
    both = spots[0] + spots[1]

    def output(n, carry):
        cols = columns_of(n, 256)
        og = og_ref[:, cols].astype(f32)
        total = jnp.zeros((128, 256), f32)
        sums = []
        for k in (0, 1):
            picked = jnp.dot(spots[k], y_ref[:, cols], preferred_element_type=f32)
            total = total + weights[k] * picked
            sums.append(carry[k] + jnp.sum(og * picked, axis=1, keepdims=True))
        layer_ref[:, cols] = (mixed_ref[:, cols].astype(f32) + total).astype(bf)
        return tuple(sums)

    start = jnp.zeros((128, 1), f32)
    weight_grad = lax.fori_loop(0, 4, output, (start, start))
    mean_term = weight_grad[0] * weights[0] + weight_grad[1] * weights[1]
    logit_grad = jnp.zeros((128, 128), f32)
    for k in (0, 1):
        chosen = (weight_grad[k] - mean_term) / score_sum * scores[k] * (1.0 - scores[k])
        logit_grad = jnp.where(picks[k], chosen, logit_grad)
    logit_grad = logit_grad.astype(bf)
    zeros = jnp.zeros((16, 1024), f32)
    cg_buf[0:16, :] = zeros
    cg_buf[144:160, :] = zeros
    across = (((1,), (1,)), ((), ()))

    def mix(n, carry):
        cols = columns_of(n, 256)
        grad = og_ref[:, cols].astype(f32) + jnp.dot(both, z_ref[:, cols], preferred_element_type=f32)
        grad = grad + lax.dot_general(logit_grad, full_ref[n, :, 2048:2176], across, preferred_element_type=f32)
        mg_buf[:, cols] = grad
        cg_buf[16:144, cols] = grad * mask * swish_slope(conv_ref[:, cols])
        return carry

    lax.fori_loop(0, 4, mix, 0)
    tg_buf[...] = jnp.zeros((128, 1024), f32)

    def depth(n, carry):
        cols = columns_of(n, 128)
        grad = cg_buf[16:144, cols]
        total = jnp.zeros((128, 128), f32)
        for k in range(KERNEL):
            total = total + taps_ref[64 + k : 65 + k, cols] * cg_buf[31 - k : 159 - k, cols]
            tg_buf[64 + k : 65 + k, cols] = jnp.sum(grad * gated_ref[k + 1 : k + 129, cols], axis=0, keepdims=True)
        total = total * mask
        sig = sig_ref[:, cols]
        pc_buf[:, cols] = (total * sig).astype(bf)
        pc_buf[:, columns_of(n + 8, 128)] = (total * value_ref[:, cols] * sig * (1.0 - sig)).astype(bf)
        return carry

    lax.fori_loop(0, 8, depth, 0)
    for take in takes:
        take.wait()
    for give in gives:
        give.start()
    turned[...] = jnp.transpose(xhat_ref[...]).astype(bf)

    def outer_product(n, carry):
        cols = columns_of(n, 256)
        out = jnp.dot(turned[...], pc_buf[:, cols], preferred_element_type=f32)
        part_ref[:, :, cols] = out.astype(bf).reshape(4, 256, 256)
        return carry

    lax.fori_loop(0, 8, outer_product, 0)
    down = (((0,), (0,)), ((), ()))
    out = lax.dot_general(mixed_ref[...], logit_grad, down, preferred_element_type=f32)
    out = out + lax.dot_general(tg_buf[...].astype(bf), identity(), down, preferred_element_type=f32)
    part_ref[:, :, 2048:2176] = out.astype(bf).reshape(4, 256, 128)
    part_ref[:, :, 2176:2304] = jnp.zeros((4, 256, 128), bf)

    def inward(n, carry):
        cols = columns_of(n, 256)
        out = lax.dot_general(pc_buf[...], full_ref[n, :, 0:2048], across, preferred_element_type=f32)
        ng_buf[:, cols] = out
        first = carry[0] + jnp.sum(out, axis=1, keepdims=True)
        second = carry[1] + jnp.sum(out * xhat_ref[:, cols], axis=1, keepdims=True)
        return first, second

    first, second = lax.fori_loop(0, 4, inward, (start, start))
    first, second = first * (1.0 / 1024), second * (1.0 / 1024)

    def finish(n, carry):
        cols = columns_of(n, 256)
        grad = inv_scale * (ng_buf[:, cols] - first - xhat_ref[:, cols] * second)
        frames_ref[:, cols] = (mg_buf[:, cols] + grad).astype(bf)
        return carry

    lax.fori_loop(0, 4, finish, 0)
    for give in gives:
        give.wait()


def backward(y, z, og, saved, lengths, ids, full, inner, outer):
    bf, f32 = jnp.bfloat16, jnp.float32
    vmem, anywhere = pl.BlockSpec(memory_space=pltpu.VMEM), pl.BlockSpec(memory_space=pl.ANY)
    shape = lambda *args: jax.ShapeDtypeStruct(*args)
    whole = shape((1024, 1024), bf)
    return pl.pallas_call(
        back_kernel,
        out_shape=(shape((128, 1024), bf), shape((128, 1024), bf), shape((4, 256, WIDE), bf), whole, whole),
        in_specs=[vmem] * 11 + [pl.BlockSpec(memory_space=pltpu.SMEM), vmem, vmem, anywhere, anywhere],
        out_specs=(vmem, vmem, vmem, anywhere, anywhere),
        scratch_shapes=[
            pltpu.VMEM((2, 1024, 1024), bf),
            pltpu.SemaphoreType.DMA((4,)),
            pltpu.VMEM((128, 1024), f32),
            pltpu.VMEM((160, 1024), f32),
            pltpu.VMEM((128, 1024), f32),
            pltpu.VMEM((128, 2048), bf),
            pltpu.VMEM((1024, 128), bf),
            pltpu.VMEM((128, 1024), f32),
        ],
        compiler_params=pltpu.CompilerParams(vmem_limit_bytes=VMEM_LIMIT),
        name="backward",
    )(y, z, og, *saved, lengths, ids, full, inner, outer)


def per_device(frames, lengths, expert_ids, conv_in, depthwise, router, w_in, w_out, out_grad):
    width = frames.shape[1]
    experts = router.shape[1]
    packed = jnp.concatenate(
        [conv_in, router, jnp.pad(depthwise, ((0, 0), (0, WIDE - 2 * width - experts - KERNEL)))], axis=1
    )
    full = gather_weights(packed)
    rows, cot, *saved = front(frames, lengths, expert_ids, out_grad, full)
    expert_rows, back_rows, inner, outer = expert_pass(rows, cot, w_in[0], w_out[0])
    layer_out, frames_grad, part, w_in_grad, w_out_grad = backward(
        expert_rows, back_rows, out_grad, saved, lengths, expert_ids, full, inner, outer
    )
    conv_in_grad, depthwise_grad, router_grad = reduce_grads(part)
    return (
        layer_out,
        frames_grad,
        conv_in_grad,
        depthwise_grad,
        router_grad,
        w_in_grad[None],
        w_out_grad[None],
    )


def solution(mesh):
    in_specs = (
        P(("dp", "expert"), None),
        P(("dp", "expert")),
        P(("dp", "expert"), None),
        P(("dp", "expert"), None),
        P(("dp", "expert"), None),
        P(("dp", "expert"), None),
        P("expert", None, "dp"),
        P("expert", "dp", None),
        P(("dp", "expert"), None),
    )
    out_specs = (
        P(("dp", "expert"), None),
        P(("dp", "expert"), None),
        P(("dp", "expert"), None),
        P(("dp", "expert"), None),
        P(("dp", "expert"), None),
        P("expert", None, "dp"),
        P("expert", "dp", None),
    )
    return jax.shard_map(
        per_device, mesh=mesh, in_specs=in_specs, out_specs=out_specs, check_vma=False
    )
```

```python
import jax
import jax.numpy as jnp
from jax import lax
from jax.experimental import pallas as pl
from jax.experimental.pallas import tpu as pltpu
from jax.sharding import PartitionSpec as P

KERNEL = 31
EPSILON = 1e-05


def swish_of(values):
    return values * jax.nn.sigmoid(values)


def swish_slope(values):
    sigmoid_v = jax.nn.sigmoid(values)
    return sigmoid_v * (1.0 + values * (1.0 - sigmoid_v))


def normalize(values):
    center = values - jnp.mean(values, axis=-1, keepdims=True)
    inv_scale = lax.rsqrt(jnp.mean(center * center, axis=-1, keepdims=True) + EPSILON)
    return (center * inv_scale, inv_scale)


MESH = pl.DeviceIdType.MESH
HALF = 1152
WIDE = 2 * HALF
SPLIT = 640
VMEM_LIMIT = 60 * 1024 * 1024


def place():
    x = lax.axis_index("dp")
    e = lax.axis_index("expert")
    return x, e // 16, (e // 2) % 8, e % 2


def spot(x, y, z, c):
    return (x, y * 16 + z * 2 + c)


def remote(src, dst, send, recv, where):
    return pltpu.make_async_remote_copy(
        src_ref=src, dst_ref=dst, send_sem=send, recv_sem=recv, device_id=where, device_id_type=MESH
    )


def greet(targets):
    barrier = pltpu.get_barrier_semaphore()
    for where in targets:
        pl.semaphore_signal(barrier, inc=1, device_id=where, device_id_type=MESH)
    pl.semaphore_wait(barrier, len(targets))


def axis_peers(x, y, z, c):
    peers = [spot(x, y, z, 1 - c)]
    peers += [spot(x, y, (z + dz) % 8, c) for dz in range(1, 8)]
    peers += [spot(x, (y + dy) % 4, z, c) for dy in (1, 3)]
    peers += [spot((x + dx) % 4, y, z, c) for dx in (1, 3)]
    return peers


def reduce_kernel(
    part_ref, out_ref, depth_ref, router_ref, swap_buf, half_buf, far_buf, near_buf, mid_buf, mid_far, mid_near, z_src, z_buf, last_src,
    last_buf, swap_s, swap_r, ring_s, ring_r, z_s, z_r, last_s, last_r
):
    x, y, z, c = place()
    greet(axis_peers(x, y, z, c))
    partner = spot(x, y, z, 1 - c)
    mine = pl.multiple_of(c * HALF, 128)
    other = pl.multiple_of((1 - c) * HALF, 128)
    colours = ((0, SPLIT), (SPLIT, HALF - SPLIT))
    order = (2, 1, 3, 0)

    def rows_of(colour, index):
        if colour == 0:
            return index, pl.ds(0, 256)
        return slice(None), pl.ds(pl.multiple_of(index * 64, 64), 64)

    swaps = {}
    for step in order:
        for colour, (begin, width) in enumerate(colours):
            at = ((x if colour == 0 else y) + step) % 4
            lead, rows = rows_of(colour, at)
            slot = colour * 4 + step
            copy = remote(
                part_ref.at[lead, rows, pl.ds(pl.multiple_of(other + begin, 128), width)],
                swap_buf.at[lead, rows, pl.ds(begin, width)],
                swap_s.at[slot],
                swap_r.at[slot],
                partner,
            )
            copy.start()
            swaps[colour, step] = copy

    def first_to(colour, step):
        if colour == 0:
            return spot((x + step) % 4, y, z, c)
        return spot(x, (y + step) % 4, z, c)

    def second_to(colour, step):
        return first_to(1 - colour, step)

    def fold(colour, step, extra):
        begin, width = colours[colour]
        at = ((x if colour == 0 else y) + step) % 4
        swaps[colour, step].wait_recv()

        def body(t, carry):
            if colour == 0:
                lead, row = at, pl.multiple_of(t * 32, 32)
            else:
                lead, row = t // 2, pl.multiple_of(at * 64 + (t % 2) * 32, 32)
            value = part_ref[lead, pl.ds(row, 32), pl.ds(pl.multiple_of(mine + begin, 128), width)].astype(jnp.float32)
            value = value + swap_buf[lead, pl.ds(row, 32), pl.ds(begin, width)].astype(jnp.float32)
            value = extra(t, value)
            half_buf[colour, step, pl.ds(pl.multiple_of(t * 32, 32), 32), pl.ds(0, width)] = value.astype(jnp.bfloat16)
            return carry

        return body

    plain = lambda t, value: value
    sent = []
    pend = {}
    for colour, (begin, width) in enumerate(colours):
        lax.fori_loop(0, 8, fold(colour, 2, plain), 0)
        for side, step in ((0, 1), (1, 3)):
            slot = colour * 8 + side
            copy = remote(
                half_buf.at[colour, 2, pl.ds(side * 128, 128), pl.ds(0, width)],
                far_buf.at[colour, side, :, pl.ds(0, width)],
                ring_s.at[slot],
                ring_r.at[slot],
                first_to(colour, step),
            )
            copy.start()
            pend[colour, side] = copy
            sent.append(copy)
    for colour, (begin, width) in enumerate(colours):
        for side, step in ((0, 1), (1, 3)):
            lo = side * 4

            lax.fori_loop(4 - lo, 8 - lo, fold(colour, step, plain), 0)
            pend[colour, side].wait_recv()

            def extra(t, value, colour=colour, side=side, lo=lo, width=width):
                row = pl.multiple_of((t - lo) * 32, 32)
                return value + far_buf[colour, side, pl.ds(row, 32), pl.ds(0, width)].astype(jnp.float32)

            def again(t, carry, colour=colour, step=step, extra=extra, begin=begin, width=width):
                at = ((x if colour == 0 else y) + step) % 4
                if colour == 0:
                    lead, row = at, pl.multiple_of(t * 32, 32)
                else:
                    lead, row = t // 2, pl.multiple_of(at * 64 + (t % 2) * 32, 32)
                value = part_ref[lead, pl.ds(row, 32), pl.ds(pl.multiple_of(mine + begin, 128), width)].astype(jnp.float32)
                value = value + swap_buf[lead, pl.ds(row, 32), pl.ds(begin, width)].astype(jnp.float32)
                value = extra(t, value)
                half_buf[colour, step, pl.ds(pl.multiple_of(t * 32, 32), 32), pl.ds(0, width)] = value.astype(jnp.bfloat16)
                return carry

            lax.fori_loop(lo, lo + 4, again, 0)
            slot = colour * 8 + 2 + side
            copy = remote(
                half_buf.at[colour, step, :, pl.ds(0, width)],
                near_buf.at[colour, side, :, pl.ds(0, width)],
                ring_s.at[slot],
                ring_r.at[slot],
                first_to(colour, step),
            )
            copy.start()
            pend[colour, 2 + side] = copy
            sent.append(copy)
    for colour, (begin, width) in enumerate(colours):
        pend[colour, 2].wait_recv()
        pend[colour, 3].wait_recv()

        def extra(t, value, colour=colour, width=width):
            row = pl.multiple_of(t * 32, 32)
            for side in (0, 1):
                value = value + near_buf[colour, side, pl.ds(row, 32), pl.ds(0, width)].astype(jnp.float32)
            return value

        body = fold(colour, 0, extra)
        lax.fori_loop(0, 8, body, 0)
        at = y if colour == 0 else x
        for side, step in ((0, 1), (1, 3)):
            row = pl.multiple_of(((at + 2) % 4) * 64 + side * 32, 32)
            slot = colour * 8 + 4 + side
            copy = remote(
                half_buf.at[colour, 0, pl.ds(row, 32), pl.ds(0, width)],
                mid_far.at[colour, side, :, pl.ds(0, width)],
                ring_s.at[slot],
                ring_r.at[slot],
                second_to(colour, step),
            )
            copy.start()
            pend[colour, 4 + side] = copy
            sent.append(copy)
    for colour, (begin, width) in enumerate(colours):
        at = y if colour == 0 else x
        for side, step in ((0, 1), (1, 3)):
            row = pl.multiple_of(((at + step) % 4) * 64, 32)
            pend[colour, 4 + side].wait_recv()
            for piece in (0, 1):
                value = half_buf[colour, 0, pl.ds(pl.multiple_of(row + piece * 32, 32), 32), pl.ds(0, width)]
                if piece == side:
                    value = value.astype(jnp.float32) + mid_far[colour, side, :, pl.ds(0, width)].astype(jnp.float32)
                    value = value.astype(jnp.bfloat16)
                mid_buf[colour, side, pl.ds(piece * 32, 32), pl.ds(0, width)] = value
            slot = colour * 8 + 6 + side
            copy = remote(
                mid_buf.at[colour, side, :, pl.ds(0, width)],
                mid_near.at[colour, side, :, pl.ds(0, width)],
                ring_s.at[slot],
                ring_r.at[slot],
                second_to(colour, step),
            )
            copy.start()
            pend[colour, 6 + side] = copy
            sent.append(copy)
    for colour, (begin, width) in enumerate(colours):
        at = y if colour == 0 else x
        pend[colour, 6].wait_recv()
        pend[colour, 7].wait_recv()
        for piece in range(2):
            rows = pl.ds(piece * 32, 32)
            value = half_buf[colour, 0, pl.ds(pl.multiple_of(at * 64 + piece * 32, 32), 32), pl.ds(0, width)].astype(jnp.float32)
            for side in (0, 1):
                value = value + mid_near[colour, side, rows, pl.ds(0, width)].astype(jnp.float32)
            z_src[pl.ds(piece * 4, 4), :, pl.ds(begin, width)] = value.astype(jnp.bfloat16).reshape(4, 8, width)
    z_copies = []
    for dz in (4, 3, 5, 2, 6, 1, 7):
        to = (z + dz) % 8
        copy = remote(z_src.at[to], z_buf.at[dz - 1], z_s.at[dz - 1], z_r.at[dz - 1], spot(x, y, to, c))
        copy.start()
        z_copies.append(copy)
    total = z_src[z].astype(jnp.float32)
    for copy in z_copies:
        copy.wait_recv()
    for k in range(7):
        total = total + z_buf[k].astype(jnp.float32)
    last_src[...] = total
    last = remote(last_src, last_buf, last_s, last_r, partner)
    last.start()
    for copy in sent + z_copies:
        copy.wait_send()
    for copy in swaps.values():
        copy.wait_send()
    kept = jnp.where(c == 0, last_src[0:4, :], last_src[4:8, :])
    last.wait()
    got = jnp.where(c == 0, last_buf[0:4, :], last_buf[4:8, :])
    low, high = jnp.where(c == 0, kept, got), jnp.where(c == 0, got, kept)
    out_ref[:, 0:HALF] = low
    out_ref[:, HALF:2048] = high[:, 0 : 2048 - HALF]
    router_ref[...] = high[:, 2048 - HALF : 2112 - HALF]
    depth_ref[...] = high[:, 2112 - HALF : 2112 + KERNEL - HALF]


def reduce_grads(part):
    dma = pltpu.SemaphoreType.DMA
    bf, wide = jnp.bfloat16, SPLIT
    return pl.pallas_call(
        reduce_kernel,
        out_shape=tuple(jax.ShapeDtypeStruct((4, width), jnp.float32) for width in (2048, KERNEL, 64)),
        in_specs=[pl.BlockSpec(memory_space=pltpu.VMEM)],
        out_specs=(pl.BlockSpec(memory_space=pltpu.VMEM),) * 3,
        scratch_shapes=[
            pltpu.VMEM((4, 256, HALF), bf),
            pltpu.VMEM((2, 4, 256, wide), bf),
            pltpu.VMEM((2, 2, 128, wide), bf),
            pltpu.VMEM((2, 2, 256, wide), bf),
            pltpu.VMEM((2, 2, 64, wide), bf),
            pltpu.VMEM((2, 2, 32, wide), bf),
            pltpu.VMEM((2, 2, 64, wide), bf),
            pltpu.VMEM((8, 8, HALF), bf),
            pltpu.VMEM((7, 8, HALF), bf),
            pltpu.VMEM((8, HALF), jnp.float32),
            pltpu.VMEM((8, HALF), jnp.float32),
            dma((8,)),
            dma((8,)),
            dma((16,)),
            dma((16,)),
            dma((7,)),
            dma((7,)),
            dma,
            dma,
        ],
        compiler_params=pltpu.CompilerParams(
            collective_id=1, has_side_effects=True, vmem_limit_bytes=VMEM_LIMIT
        ),
        name="reduce_grads",
    )(part)


STEPS = (0, 1, 3, 2)
TALL = 1152


def columns_of(n, width):
    return pl.ds(pl.multiple_of(n * width, width), width)


def mask_of(length_ref):
    return (lax.broadcasted_iota(jnp.int32, (128, 1), 0) < length_ref[0]).astype(jnp.float32)


def chosen_of(ids_ref):
    lane = lax.broadcasted_iota(jnp.int32, (128, 128), 1)
    return [lane == ids_ref[:, k : k + 1] for k in (0, 1)]


def identity():
    shape = (128, 128)
    return (lax.broadcasted_iota(jnp.int32, shape, 0) == lax.broadcasted_iota(jnp.int32, shape, 1)).astype(jnp.bfloat16)


def main_kernel(
    frames_ref, length_ref, ids_ref, og_ref, conv_in_ref, router_ref, depthwise_ref, inner_hbm, outer_hbm,
    out_ref, mixed_ref, value_ref, sig_ref, conv_ref, xhat_ref, notes_ref, gated_ref, taps_ref,
    y_ref, z_ref, inner_grad_hbm, outer_grad_hbm,
    own_ref, rows_buf, og_rows, slots, cots, scaled, active, pre, inner, outer, part_y, part_z, straight_y, straight_z,
    relay_y, relay_z, joint_y, joint_z, grad_buf, sized, load_sem, core_s, core_r, own_sem, z_s, z_r, gring_s, gring_r,
    tail_s, tail_r, self_s, there_s, there_r, ring_s, ring_r, fold_s, fold_r, back_s, back_r, store_sem
):
    x, y, z, c = place()
    f32, bf = jnp.float32, jnp.bfloat16
    here = y * 16 + z * 2 + c
    right, left, far = (x + 1) % 4, (x + 3) % 4, (x + 2) % 4
    to_right, to_left = spot(right, y, z, c), spot(left, y, z, c)
    loads = [
        pltpu.make_async_copy(inner_hbm, inner, load_sem.at[0]),
        pltpu.make_async_copy(outer_hbm, outer, load_sem.at[1]),
    ]
    for load in loads:
        load.start()

    barrier = pltpu.get_barrier_semaphore()

    def hail(i, carry):
        pl.semaphore_signal(barrier, inc=1, device_id=(x, (here + i) % 64), device_id_type=MESH)
        return carry

    lax.fori_loop(1, 64, hail, 0)
    for where in (to_right, to_left):
        pl.semaphore_signal(barrier, inc=1, device_id=where, device_id_type=MESH)

    own_ref[:, 0:2048] = conv_in_ref[...]
    own_ref[:, 2048:WIDE] = jnp.concatenate(
        [router_ref[...].astype(f32), depthwise_ref[...].astype(f32), jnp.zeros((4, WIDE - 2112 - KERNEL), f32)], axis=1
    ).astype(bf)
    mask = mask_of(length_ref)
    picks = chosen_of(ids_ref)
    count = (jnp.where(picks[0] | picks[1], 1.0, 0.0) * mask).astype(bf)
    shape = (128, 128)
    below = (lax.broadcasted_iota(jnp.int32, shape, 1) < lax.broadcasted_iota(jnp.int32, shape, 0)).astype(bf)
    before = jnp.dot(below, count, preferred_element_type=f32)
    wide = lax.broadcasted_iota(jnp.int32, (128, 256), 1).astype(f32)
    slot_of, spots = [], []
    for k, pick in enumerate(picks):
        position = jnp.sum(jnp.where(pick, before, 0.0), axis=1, keepdims=True)
        kept = (position < 4.0) & (mask > 0.0)
        slot = jnp.where(kept, ids_ref[:, k : k + 1].astype(f32) * 4.0 + position, -1.0)
        slot_of.append(slot)
        spots.append((wide == slot).astype(bf))
    both = spots[0] + spots[1]
    down = (((0,), (0,)), ((), ()))

    def fill_og(n, carry):
        cols = columns_of(n, 256)
        og_rows[:, cols] = lax.dot_general(both, og_ref[:, cols], down, preferred_element_type=f32).astype(bf)
        return carry

    lax.fori_loop(0, 4, fill_og, 0)
    pl.semaphore_wait(barrier, 65)

    own4 = pl.multiple_of(4 * here, 4)
    line4 = pl.multiple_of(8 * z + 4 * c, 4)
    kinds = ((rows_buf, slots, TALL), (og_rows, cots, 1024))
    selfs = {}
    rings = {}

    def source_y(q):
        return (y + STEPS[q]) % 4

    def depart(kind, q):
        source, target, _ = kinds[kind]
        dy = STEPS[q]
        yt = (y + 4 - dy) % 4

        def there(i, carry):
            zt, ct = (z + 4 + i // 2) % 8, (c + i) % 2
            et = yt * 16 + zt * 2 + ct
            rows = pl.ds(pl.multiple_of(4 * et, 4), 4)
            remote(
                source.at[rows], target.at[x, y, pl.ds(line4, 4)], there_s.at[kind, q], there_r.at[kind, q], (x, et)
            ).start()
            return carry

        if dy == 0:
            lax.fori_loop(0, 8, there, 0)
            lax.fori_loop(9, 16, there, 0)
            selfs[kind] = pltpu.make_async_copy(
                source.at[pl.ds(own4, 4)], target.at[x, y, pl.ds(line4, 4)], self_s.at[kind]
            )
            selfs[kind].start()
        else:
            lax.fori_loop(0, 16, there, 0)

    def bulk(kind, q):
        return sized.at[pl.ds(0, 15 if STEPS[q] == 0 else 16), :, pl.ds(0, kinds[kind][2])]

    def arrive(kind, q):
        if STEPS[q] == 0:
            selfs[kind].wait()
        view = bulk(kind, q)
        remote(view, view, there_s.at[kind, q], there_r.at[kind, q], to_right).wait_recv()
        block = kinds[kind][1].at[x, source_y(q)]
        for side, where in ((0, to_right), (1, to_left)):
            copy = remote(block, block, ring_s.at[kind, side, q], ring_r.at[kind, side, q], where)
            copy.start()
            rings[kind, side, q] = copy

    def forward(kind, q):
        for side, at, where in ((0, left, to_right), (1, right, to_left)):
            rings[kind, side, q].wait_recv()
            block = kinds[kind][1].at[at, source_y(q), pl.ds(32 * side, 32)]
            copy = remote(block, block, ring_s.at[kind, 2 + side, q], ring_r.at[kind, 2 + side, q], where)
            copy.start()
            rings[kind, 2 + side, q] = copy

    partner = spot(x, y, z, 1 - c)
    mine = pl.multiple_of(c * HALF, 128)
    other = pl.multiple_of((1 - c) * HALF, 128)
    row = pl.multiple_of(y * 64 + z * 8, 8)
    row4 = pl.multiple_of(row + 4 * c, 4)
    swap = remote(
        own_ref.at[:, pl.ds(other, HALF)],
        out_ref.at[x, pl.ds(row4, 4), pl.ds(other, HALF)],
        core_s,
        core_r,
        partner,
    )
    swap.start()
    keep = pltpu.make_async_copy(
        own_ref.at[:, pl.ds(mine, HALF)], out_ref.at[x, pl.ds(row4, 4), pl.ds(mine, HALF)], own_sem
    )
    keep.start()
    depart(1, 0)
    keep.wait()
    swap.wait()
    copies = []
    for dz in (4, 3, 5, 2, 6, 1, 7):
        block = out_ref.at[x, pl.ds(row, 8), pl.ds(mine, HALF)]
        copy = remote(block, block, z_s.at[dz - 1], z_r.at[dz - 1], spot(x, y, (z + dz) % 8, c))
        copy.start()
        copies.append(copy)
    depart(1, 1)
    xhat, inv_scale = normalize(frames_ref[...].astype(f32))
    xhat_ref[...] = xhat
    zeros = jnp.zeros((16, 1024), f32)
    gated_ref[0:16, :] = zeros
    gated_ref[144:160, :] = zeros
    for copy in copies:
        copy.wait()

    first = pl.multiple_of(mine, 128)
    second = pl.multiple_of(mine + SPLIT, 128)
    yrow = pl.multiple_of(y * 64, 64)

    def block_of(colour, level, index, part):
        cols = pl.ds(first, SPLIT) if colour == 0 else pl.ds(second, HALF - SPLIT)
        if level == 0:
            height = 64 if part is None else 32
            offset = 0 if part is None else part * 32
            if colour == 0:
                return out_ref.at[x, pl.ds(pl.multiple_of(index * 64 + offset, 32), height), cols]
            return out_ref.at[index, pl.ds(pl.multiple_of(yrow + offset, 32), height), cols]
        if colour == 0:
            height = 256 if part is None else 128
            offset = 0 if part is None else part * 128
            return out_ref.at[index, pl.ds(offset, height), cols]
        height = 64 if part is None else 32
        offset = 0 if part is None else part * 32
        return out_ref.at[:, pl.ds(pl.multiple_of(index * 64 + offset, 32), height), cols]

    def whereto(colour, level, step):
        if (colour + level) % 2 == 0:
            return spot(x, (y + step) % 4, z, c)
        return spot((x + step) % 4, y, z, c)

    def position(colour, level):
        return y if (colour + level) % 2 == 0 else x

    def opened(colour, level):
        at = position(colour, level)
        block = block_of(colour, level, at, None)
        base = (colour * 2 + level) * 4
        right = remote(block, block, gring_s.at[base], gring_r.at[base], whereto(colour, level, 1))
        left = remote(block, block, gring_s.at[base + 1], gring_r.at[base + 1], whereto(colour, level, 3))
        right.start()
        left.start()
        return right, left

    def passed(colour, level, pair, tell):
        at = position(colour, level)
        base = (colour * 2 + level) * 4
        right, left = pair
        right.wait_recv()
        block = block_of(colour, level, (at + 3) % 4, 0)
        on_right = remote(block, block, gring_s.at[base + 2], gring_r.at[base + 2], whereto(colour, level, 1))
        on_right.start()
        tell((at + 3) % 4, 1)
        left.wait_recv()
        block = block_of(colour, level, (at + 1) % 4, 1)
        on_left = remote(block, block, gring_s.at[base + 3], gring_r.at[base + 3], whereto(colour, level, 3))
        on_left.start()
        tell((at + 1) % 4, 2)
        return on_right, on_left

    def closed(colour, level, pair, onward, tell):
        at = position(colour, level)
        for copy in onward:
            copy.wait_recv()
        tell((at + 2) % 4, 3)
        for copy in pair + onward:
            copy.wait_send()

    silent = lambda index, slot: None
    low = [opened(colour, 0) for colour in (0, 1)]
    arrive(1, 0)
    low_on = [passed(colour, 0, low[colour], silent) for colour in (0, 1)]
    depart(1, 2)
    for colour in (0, 1):
        closed(colour, 0, low[colour], low_on[colour], silent)
    tails = []

    def teller(colour):
        def tell(index, slot):
            block = block_of(colour, 1, index, None)
            at = colour * 4 + slot
            copy = remote(block, block, tail_s.at[at], tail_r.at[at], partner)
            copy.start()
            tails.append(copy)

        return tell

    high = [opened(colour, 1) for colour in (0, 1)]
    for colour in (0, 1):
        teller(colour)(position(colour, 1), 0)
    depart(1, 3)
    arrive(1, 1)
    high_on = [passed(colour, 1, high[colour], teller(colour)) for colour in (0, 1)]
    forward(1, 0)
    for colour in (0, 1):
        closed(colour, 1, high[colour], high_on[colour], teller(colour))
    arrive(1, 2)
    for copy in tails:
        copy.wait()
    forward(1, 1)
    arrive(1, 3)

    normed = xhat_ref[...].astype(bf)

    def point(n, carry):
        cols = columns_of(n, 256)
        value = jnp.dot(normed, out_ref[:, :, cols].reshape(1024, 256), preferred_element_type=f32)
        gate = jnp.dot(normed, out_ref[:, :, columns_of(n + 4, 256)].reshape(1024, 256), preferred_element_type=f32)
        sig = jax.nn.sigmoid(gate)
        value_ref[:, cols] = value
        sig_ref[:, cols] = sig
        gated_ref[16:144, cols] = value * sig * mask
        return carry

    lax.fori_loop(0, 4, point, 0)
    small = out_ref[:, :, 2048:2176].reshape(1024, 128)
    taps_ref[...] = lax.dot_general(identity(), small, (((1,), (1,)), ((), ())), preferred_element_type=f32)
    forward(1, 2)

    def depth(n, carry):
        cols = columns_of(n, 128)
        total = jnp.zeros((128, 128), f32)
        for k in range(KERNEL):
            total = total + taps_ref[64 + k : 65 + k, cols] * gated_ref[k + 1 : k + 129, cols]
        conv_ref[:, cols] = total
        mixed_ref[:, cols] = (frames_ref[:, cols].astype(f32) + swish_of(total) * mask).astype(bf)
        return carry

    lax.fori_loop(0, 8, depth, 0)
    logits = jnp.dot(mixed_ref[...], small, preferred_element_type=f32)
    scores = [jax.nn.sigmoid(jnp.sum(jnp.where(pick, logits, 0.0), axis=1, keepdims=True)) for pick in picks]
    score_sum = scores[0] + scores[1]
    weights = [score / score_sum for score in scores]
    lane = lax.broadcasted_iota(jnp.int32, shape, 1)
    notes = jnp.zeros(shape, f32)
    for i, column in enumerate(weights + scores + [score_sum] + slot_of + [inv_scale]):
        notes = jnp.where(lane == i, column, notes)
    notes_ref[...] = notes

    def fill(n, carry):
        cols = columns_of(n, 256)
        rows_buf[:, cols] = lax.dot_general(both, mixed_ref[:, cols], down, preferred_element_type=f32).astype(bf)
        return carry

    lax.fori_loop(0, 4, fill, 0)
    total = jnp.zeros((256, 128), f32)
    for k in (0, 1):
        upper = weights[k].astype(bf).astype(f32)
        parts = jnp.where(lane == 0, upper, jnp.where(lane == 1, weights[k] - upper, 0.0)).astype(bf)
        total = total + lax.dot_general(spots[k], parts, down, preferred_element_type=f32)
    rows_buf[:, 1024:TALL] = total.astype(bf)
    for q in range(4):
        depart(0, q)
    forward(1, 3)

    folds = {}

    def push(name, q, source, target, where):
        copy = remote(source, target, fold_s.at[name, q], fold_r.at[name, q], where)
        copy.start()
        folds[name, q] = copy

    def compute(q):
        ys = source_y(q)
        for kind in (1, 0):
            for side in (2, 3):
                rings[kind, side, q].wait_recv()

        def scale(n, carry):
            parts = slots[n, ys, :, 1024:TALL].astype(f32)
            weight = parts[:, 0:1] + parts[:, 1:2]
            scaled[n, ys] = (cots[n, ys].astype(f32) * weight).astype(bf)
            return carry

        lax.fori_loop(0, 4, scale, 0)

        def first(n, carry):
            cols = pl.ds(pl.multiple_of(n * 256, 256), 256)
            hidden = jnp.dot(slots[:, ys, :, 0:1024].reshape(256, 1024), inner[:, cols], preferred_element_type=f32)
            act_grad = lax.dot_general(
                scaled[:, ys].reshape(256, 1024), outer[cols, :], (((1,), (1,)), ((), ())), preferred_element_type=f32
            )
            sig = jax.nn.sigmoid(hidden)
            active[:, ys, :, cols] = (hidden * sig).astype(bf).reshape(4, 64, 256)
            slope = sig * (1.0 + hidden * (1.0 - sig))
            pre[:, ys, :, cols] = (act_grad * slope).astype(bf).reshape(4, 64, 256)
            return carry

        lax.fori_loop(0, 4, first, 0)
        def second(n, carry):
            cols = pl.ds(pl.multiple_of(n * 256, 256), 256)
            out = jnp.dot(active[:, ys].reshape(256, 1024), outer[:, cols], preferred_element_type=f32)
            part_y[q, :, :, cols] = out.astype(bf).reshape(4, 64, 256)
            out = lax.dot_general(
                pre[:, ys].reshape(256, 1024), inner[cols, :], (((1,), (1,)), ((), ())), preferred_element_type=f32
            )
            part_z[q, :, :, cols] = out.astype(bf).reshape(4, 64, 256)
            return carry

        lax.fori_loop(0, 4, second, 0)
        push(2, q, part_y.at[q, far], relay_y.at[q], to_right)
        push(3, q, part_z.at[q, far], relay_z.at[q], to_left)
        push(0, q, part_z.at[q, right], straight_z.at[q], to_right)
        push(1, q, part_y.at[q, left], straight_y.at[q], to_left)

    def relay(q):
        folds[2, q].wait_recv()
        part_y[q, right] = (part_y[q, right].astype(f32) + relay_y[q].astype(f32)).astype(bf)
        push(4, q, part_y.at[q, right], joint_y.at[q], to_right)
        folds[3, q].wait_recv()
        part_z[q, left] = (part_z[q, left].astype(f32) + relay_z[q].astype(f32)).astype(bf)
        push(5, q, part_z.at[q, left], joint_z.at[q], to_left)

    def deliver(q):
        yt = source_y(q)
        for name in (1, 4, 0, 5):
            folds[name, q].wait_recv()
        part_y[q, x] = (part_y[q, x].astype(f32) + straight_y[q].astype(f32) + joint_y[q].astype(f32)).astype(bf)
        part_z[q, x] = (part_z[q, x].astype(f32) + straight_z[q].astype(f32) + joint_z[q].astype(f32)).astype(bf)

        def back(i, carry):
            zt, ct = (z + 4 + i // 2) % 8, (c + i) % 2
            rows = pl.ds(pl.multiple_of(8 * zt + 4 * ct, 4), 4)
            for kind, (source, target) in enumerate(((part_y, y_ref), (part_z, z_ref))):
                remote(
                    source.at[q, x, rows], target.at[pl.ds(own4, 4)], back_s.at[kind], back_r.at[kind], (x, yt * 16 + zt * 2 + ct)
                ).start()
            return carry

        if STEPS[q] == 0:
            lax.fori_loop(0, 8, back, 0)
            lax.fori_loop(9, 16, back, 0)
            for kind, (source, target) in enumerate(((part_y, y_ref), (part_z, z_ref))):
                copy = pltpu.make_async_copy(
                    source.at[q, x, pl.ds(line4, 4)], target.at[pl.ds(own4, 4)], self_s.at[2 + kind]
                )
                copy.start()
                selfs[2 + kind] = copy
        else:
            lax.fori_loop(0, 16, back, 0)

    stores = []

    def weight_grad(which, left_ref, right_ref, target):
        def body(n, carry):
            cols = pl.ds(pl.multiple_of(n * 256, 256), 256)
            out = lax.dot_general(
                left_ref[:, :, :, cols].reshape(1024, 256),
                right_ref[...].reshape(1024, 1024),
                (((0,), (0,)), ((), ())),
                preferred_element_type=f32,
            )
            grad_buf[which, cols, :] = out.astype(bf)
            return carry

        lax.fori_loop(0, 4, body, 0)
        copy = pltpu.make_async_copy(grad_buf.at[which], target, store_sem.at[which])
        copy.start()
        stores.append(copy)

    for load in loads:
        load.wait()
    arrive(0, 0)
    arrive(0, 1)
    forward(0, 0)
    arrive(0, 2)
    forward(0, 1)
    compute(0)
    arrive(0, 3)
    forward(0, 2)
    compute(1)
    relay(0)
    forward(0, 3)
    compute(2)
    relay(1)
    deliver(0)
    compute(3)
    relay(2)
    deliver(1)
    weight_grad(1, active, scaled, outer_grad_hbm)
    relay(3)
    deliver(2)
    weight_grad(0, slots, pre, inner_grad_hbm)
    deliver(3)
    for kind in (0, 1):
        for q in range(4):
            view = bulk(kind, q)
            remote(view, view, there_s.at[kind, q], there_r.at[kind, q], to_right).wait_send()
    for copy in list(rings.values()) + list(folds.values()):
        copy.wait_send()
    for kind in (0, 1):
        view = sized.at[pl.ds(0, 63), :, pl.ds(0, 1024)]
        remote(view, view, back_s.at[kind], back_r.at[kind], to_right).wait()
    for copy in [selfs[2], selfs[3]] + stores:
        copy.wait()


def main_pass(frames, lengths, ids, og, conv_in, router, depthwise, inner, outer):
    dma, bf, f32 = pltpu.SemaphoreType.DMA, jnp.bfloat16, jnp.float32
    block = lambda *lead: pltpu.VMEM(lead + (64, 1024), bf)
    shape = lambda *args: jax.ShapeDtypeStruct(*args)
    vmem, anywhere = pl.BlockSpec(memory_space=pltpu.VMEM), pl.BlockSpec(memory_space=pl.ANY)
    return pl.pallas_call(
        main_kernel,
        out_shape=(
            shape((4, 256, WIDE), bf), shape((128, 1024), bf), shape((128, 1024), f32), shape((128, 1024), f32),
            shape((128, 1024), f32), shape((128, 1024), f32), shape((128, 128), f32), shape((160, 1024), f32),
            shape((128, 1024), f32), shape((256, 1024), bf), shape((256, 1024), bf), shape((1024, 1024), bf),
            shape((1024, 1024), bf),
        ),
        in_specs=[vmem, pl.BlockSpec(memory_space=pltpu.SMEM)] + [vmem] * 5 + [anywhere] * 2,
        out_specs=(vmem,) * 11 + (anywhere,) * 2,
        scratch_shapes=[
            pltpu.VMEM((4, WIDE), bf), pltpu.VMEM((256, TALL), bf), pltpu.VMEM((256, 1024), bf),
            pltpu.VMEM((4, 4, 64, TALL), bf),
        ]
        + [block(4, 4)] * 4
        + [pltpu.VMEM((1024, 1024), bf)] * 2
        + [block(4, 4)] * 2
        + [block(4)] * 6
        + [pltpu.VMEM((2, 1024, 1024), bf), pltpu.VMEM((63, 4, TALL), bf)]
        + [
            dma((2,)), dma, dma, dma, dma((7,)), dma((7,)), dma((16,)), dma((16,)), dma((8,)), dma((8,)),
            dma((4,)), dma((2, 4)), dma((2, 4)), dma((2, 4, 4)), dma((2, 4, 4)), dma((6, 4)), dma((6, 4)), dma((2,)),
            dma((2,)), dma((2,)),
        ],
        compiler_params=pltpu.CompilerParams(
            collective_id=2, has_side_effects=True, vmem_limit_bytes=VMEM_LIMIT
        ),
        name="main_pass",
    )(frames, lengths, ids, og, conv_in, router, depthwise, inner, outer)


def back_kernel(
    y_ref, z_ref, og_ref, mixed_ref, value_ref, sig_ref, conv_ref, xhat_ref, notes_ref, gated_ref, taps_ref, length_ref,
    ids_ref, full_ref, inner_ref, outer_ref, layer_ref, frames_ref, part_ref, inner_out, outer_out, pass_buf, pass_s,
    mg_buf, cg_buf, tg_buf, pc_buf, turned, ng_buf
):
    f32, bf = jnp.float32, jnp.bfloat16
    takes = [pltpu.make_async_copy(src, pass_buf.at[i], pass_s.at[i]) for i, src in enumerate((inner_ref, outer_ref))]
    gives = [pltpu.make_async_copy(pass_buf.at[i], dst, pass_s.at[2 + i]) for i, dst in enumerate((inner_out, outer_out))]
    for take in takes:
        take.start()
    mask = mask_of(length_ref)
    picks = chosen_of(ids_ref)
    notes = notes_ref[...]
    column = lambda i: notes[:, i : i + 1]
    weights, scores, score_sum, inv_scale = (column(0), column(1)), (column(2), column(3)), column(4), column(7)
    wide = lax.broadcasted_iota(jnp.int32, (128, 256), 1).astype(f32)
    spots = [(wide == column(5 + k)).astype(bf) for k in (0, 1)]
    both = spots[0] + spots[1]

    def output(n, carry):
        cols = columns_of(n, 256)
        og = og_ref[:, cols].astype(f32)
        total = jnp.zeros((128, 256), f32)
        sums = []
        for k in (0, 1):
            picked = jnp.dot(spots[k], y_ref[:, cols], preferred_element_type=f32)
            total = total + weights[k] * picked
            sums.append(carry[k] + jnp.sum(og * picked, axis=1, keepdims=True))
        layer_ref[:, cols] = (mixed_ref[:, cols].astype(f32) + total).astype(bf)
        return tuple(sums)

    start = jnp.zeros((128, 1), f32)
    weight_grad = lax.fori_loop(0, 4, output, (start, start))
    mean_term = weight_grad[0] * weights[0] + weight_grad[1] * weights[1]
    logit_grad = jnp.zeros((128, 128), f32)
    for k in (0, 1):
        chosen = (weight_grad[k] - mean_term) / score_sum * scores[k] * (1.0 - scores[k])
        logit_grad = jnp.where(picks[k], chosen, logit_grad)
    logit_grad = logit_grad.astype(bf)
    zeros = jnp.zeros((16, 1024), f32)
    cg_buf[0:16, :] = zeros
    cg_buf[144:160, :] = zeros
    across = (((1,), (1,)), ((), ()))

    def mix(n, carry):
        cols = columns_of(n, 256)
        grad = og_ref[:, cols].astype(f32) + jnp.dot(both, z_ref[:, cols], preferred_element_type=f32)
        grad = grad + lax.dot_general(logit_grad, full_ref[n, :, 2048:2176], across, preferred_element_type=f32)
        mg_buf[:, cols] = grad
        cg_buf[16:144, cols] = grad * mask * swish_slope(conv_ref[:, cols])
        return carry

    lax.fori_loop(0, 4, mix, 0)
    tg_buf[...] = jnp.zeros((128, 1024), f32)

    def depth(n, carry):
        cols = columns_of(n, 128)
        grad = cg_buf[16:144, cols]
        total = jnp.zeros((128, 128), f32)
        for k in range(KERNEL):
            total = total + taps_ref[64 + k : 65 + k, cols] * cg_buf[31 - k : 159 - k, cols]
            tg_buf[64 + k : 65 + k, cols] = jnp.sum(grad * gated_ref[k + 1 : k + 129, cols], axis=0, keepdims=True)
        total = total * mask
        sig = sig_ref[:, cols]
        pc_buf[:, cols] = (total * sig).astype(bf)
        pc_buf[:, columns_of(n + 8, 128)] = (total * value_ref[:, cols] * sig * (1.0 - sig)).astype(bf)
        return carry

    lax.fori_loop(0, 8, depth, 0)
    for take in takes:
        take.wait()
    for give in gives:
        give.start()
    turned[...] = jnp.transpose(xhat_ref[...]).astype(bf)

    def outer_product(n, carry):
        cols = columns_of(n, 256)
        out = jnp.dot(turned[...], pc_buf[:, cols], preferred_element_type=f32)
        part_ref[:, :, cols] = out.astype(bf).reshape(4, 256, 256)
        return carry

    lax.fori_loop(0, 8, outer_product, 0)
    down = (((0,), (0,)), ((), ()))
    out = lax.dot_general(mixed_ref[...], logit_grad, down, preferred_element_type=f32)
    out = out + lax.dot_general(tg_buf[...].astype(bf), identity(), down, preferred_element_type=f32)
    part_ref[:, :, 2048:2176] = out.astype(bf).reshape(4, 256, 128)
    part_ref[:, :, 2176:2304] = jnp.zeros((4, 256, 128), bf)

    def inward(n, carry):
        cols = columns_of(n, 256)
        out = lax.dot_general(pc_buf[...], full_ref[n, :, 0:2048], across, preferred_element_type=f32)
        ng_buf[:, cols] = out
        first = carry[0] + jnp.sum(out, axis=1, keepdims=True)
        second = carry[1] + jnp.sum(out * xhat_ref[:, cols], axis=1, keepdims=True)
        return first, second

    first, second = lax.fori_loop(0, 4, inward, (start, start))
    first, second = first * (1.0 / 1024), second * (1.0 / 1024)

    def finish(n, carry):
        cols = columns_of(n, 256)
        grad = inv_scale * (ng_buf[:, cols] - first - xhat_ref[:, cols] * second)
        frames_ref[:, cols] = (mg_buf[:, cols] + grad).astype(bf)
        return carry

    lax.fori_loop(0, 4, finish, 0)
    for give in gives:
        give.wait()


def backward(y, z, og, saved, lengths, ids, full, inner, outer):
    bf, f32 = jnp.bfloat16, jnp.float32
    vmem, anywhere = pl.BlockSpec(memory_space=pltpu.VMEM), pl.BlockSpec(memory_space=pl.ANY)
    shape = lambda *args: jax.ShapeDtypeStruct(*args)
    whole = shape((1024, 1024), bf)
    return pl.pallas_call(
        back_kernel,
        out_shape=(shape((128, 1024), bf), shape((128, 1024), bf), shape((4, 256, WIDE), bf), whole, whole),
        in_specs=[vmem] * 11 + [pl.BlockSpec(memory_space=pltpu.SMEM), vmem, vmem, anywhere, anywhere],
        out_specs=(vmem, vmem, vmem, anywhere, anywhere),
        scratch_shapes=[
            pltpu.VMEM((2, 1024, 1024), bf),
            pltpu.SemaphoreType.DMA((4,)),
            pltpu.VMEM((128, 1024), f32),
            pltpu.VMEM((160, 1024), f32),
            pltpu.VMEM((128, 1024), f32),
            pltpu.VMEM((128, 2048), bf),
            pltpu.VMEM((1024, 128), bf),
            pltpu.VMEM((128, 1024), f32),
        ],
        compiler_params=pltpu.CompilerParams(vmem_limit_bytes=VMEM_LIMIT),
        name="backward",
    )(y, z, og, *saved, lengths, ids, full, inner, outer)


def per_device(frames, lengths, expert_ids, conv_in, depthwise, router, w_in, w_out, out_grad):
    full, *saved, y, z, inner, outer = main_pass(
        frames, lengths, expert_ids, out_grad, conv_in, router, depthwise, w_in[0], w_out[0]
    )
    layer_out, frames_grad, part, w_in_grad, w_out_grad = backward(
        y, z, out_grad, saved, lengths, expert_ids, full, inner, outer
    )
    conv_in_grad, depthwise_grad, router_grad = reduce_grads(part)
    return (
        layer_out,
        frames_grad,
        conv_in_grad,
        depthwise_grad,
        router_grad,
        w_in_grad[None],
        w_out_grad[None],
    )


def solution(mesh):
    in_specs = (
        P(("dp", "expert"), None),
        P(("dp", "expert")),
        P(("dp", "expert"), None),
        P(("dp", "expert"), None),
        P(("dp", "expert"), None),
        P(("dp", "expert"), None),
        P("expert", None, "dp"),
        P("expert", "dp", None),
        P(("dp", "expert"), None),
    )
    out_specs = (
        P(("dp", "expert"), None),
        P(("dp", "expert"), None),
        P(("dp", "expert"), None),
        P(("dp", "expert"), None),
        P(("dp", "expert"), None),
        P("expert", None, "dp"),
        P("expert", "dp", None),
    )
    return jax.shard_map(
        per_device, mesh=mesh, in_specs=in_specs, out_specs=out_specs, check_vma=False
    )
```

```python
import jax
import jax.numpy as jnp
from jax import lax
from jax.experimental import pallas as pl
from jax.experimental.pallas import tpu as pltpu
from jax.sharding import PartitionSpec as P

KERNEL = 31
EPSILON = 1e-05


def swish_of(values):
    return values * jax.nn.sigmoid(values)


def swish_slope(values):
    sigmoid_v = jax.nn.sigmoid(values)
    return sigmoid_v * (1.0 + values * (1.0 - sigmoid_v))


def normalize(values):
    center = values - jnp.mean(values, axis=-1, keepdims=True)
    inv_scale = lax.rsqrt(jnp.mean(center * center, axis=-1, keepdims=True) + EPSILON)
    return (center * inv_scale, inv_scale)


MESH = pl.DeviceIdType.MESH
HALF = 1152
WIDE = 2 * HALF
SPLIT = 640
VMEM_LIMIT = 60 * 1024 * 1024


def place():
    x = lax.axis_index("dp")
    e = lax.axis_index("expert")
    return x, e // 16, (e // 2) % 8, e % 2


def spot(x, y, z, c):
    return (x, y * 16 + z * 2 + c)


def remote(src, dst, send, recv, where):
    return pltpu.make_async_remote_copy(
        src_ref=src, dst_ref=dst, send_sem=send, recv_sem=recv, device_id=where, device_id_type=MESH
    )


STEPS = (0, 1, 3, 2)
TALL = 1152


def columns_of(n, width):
    return pl.ds(pl.multiple_of(n * width, width), width)


def mask_of(length_ref):
    return (lax.broadcasted_iota(jnp.int32, (128, 1), 0) < length_ref[0]).astype(jnp.float32)


def chosen_of(ids_ref):
    lane = lax.broadcasted_iota(jnp.int32, (128, 128), 1)
    return [lane == ids_ref[:, k : k + 1] for k in (0, 1)]


def identity():
    shape = (128, 128)
    return (lax.broadcasted_iota(jnp.int32, shape, 0) == lax.broadcasted_iota(jnp.int32, shape, 1)).astype(jnp.bfloat16)


def layer_kernel(
    frames_ref, length_ref, ids_ref, og_ref, conv_in_ref, router_ref, depthwise_ref, inner_hbm, outer_hbm,
    layer_ref, frames_grad_ref, out_ref, depth_ref, router_grad_ref, inner_grad_hbm, outer_grad_hbm,
    full_ref, mixed_ref, value_ref, sig_ref, conv_ref, xhat_ref, gated_ref, taps_ref, y_ref, z_ref,
    own_ref, rows_buf, og_rows, slots, cots, scaled, active, pre, inner, outer, part_y, part_z, straight_y, straight_z,
    relay_y, relay_z, joint_y, joint_z, grad_buf, sized, mg_buf, cg_buf, tg_buf, pc_buf, turned, ng_buf,
    part_ref, swap_buf, half_buf, far_buf, near_buf, mid_buf, mid_far, mid_near, z_src, z_buf, last_src, last_buf,
    load_sem, core_s, core_r, own_sem, z_s, z_r, gring_s, gring_r, tail_s, tail_r, self_s, there_s, there_r, ring_s,
    ring_r, fold_s, fold_r, back_s, back_r, store_sem, swap_s, swap_r, rring_s, rring_r, rz_s, rz_r, last_s, last_r
):
    x, y, z, c = place()
    f32, bf = jnp.float32, jnp.bfloat16
    here = y * 16 + z * 2 + c
    right, left, far = (x + 1) % 4, (x + 3) % 4, (x + 2) % 4
    to_right, to_left = spot(right, y, z, c), spot(left, y, z, c)
    loads = [
        pltpu.make_async_copy(inner_hbm, inner, load_sem.at[0]),
        pltpu.make_async_copy(outer_hbm, outer, load_sem.at[1]),
    ]
    for load in loads:
        load.start()

    barrier = pltpu.get_barrier_semaphore()

    def hail(i, carry):
        pl.semaphore_signal(barrier, inc=1, device_id=(x, (here + i) % 64), device_id_type=MESH)
        return carry

    lax.fori_loop(1, 64, hail, 0)
    for where in (to_right, to_left):
        pl.semaphore_signal(barrier, inc=1, device_id=where, device_id_type=MESH)

    own_ref[:, 0:2048] = conv_in_ref[...]
    own_ref[:, 2048:WIDE] = jnp.concatenate(
        [router_ref[...].astype(f32), depthwise_ref[...].astype(f32), jnp.zeros((4, WIDE - 2112 - KERNEL), f32)], axis=1
    ).astype(bf)
    mask = mask_of(length_ref)
    picks = chosen_of(ids_ref)
    count = (jnp.where(picks[0] | picks[1], 1.0, 0.0) * mask).astype(bf)
    shape = (128, 128)
    below = (lax.broadcasted_iota(jnp.int32, shape, 1) < lax.broadcasted_iota(jnp.int32, shape, 0)).astype(bf)
    before = jnp.dot(below, count, preferred_element_type=f32)
    wide = lax.broadcasted_iota(jnp.int32, (128, 256), 1).astype(f32)
    slot_of, spots = [], []
    for k, pick in enumerate(picks):
        position = jnp.sum(jnp.where(pick, before, 0.0), axis=1, keepdims=True)
        kept = (position < 4.0) & (mask > 0.0)
        slot = jnp.where(kept, ids_ref[:, k : k + 1].astype(f32) * 4.0 + position, -1.0)
        slot_of.append(slot)
        spots.append((wide == slot).astype(bf))
    both = spots[0] + spots[1]
    down = (((0,), (0,)), ((), ()))

    def fill_og(n, carry):
        cols = columns_of(n, 256)
        og_rows[:, cols] = lax.dot_general(both, og_ref[:, cols], down, preferred_element_type=f32).astype(bf)
        return carry

    lax.fori_loop(0, 4, fill_og, 0)
    pl.semaphore_wait(barrier, 65)

    own4 = pl.multiple_of(4 * here, 4)
    line4 = pl.multiple_of(8 * z + 4 * c, 4)
    kinds = ((rows_buf, slots, TALL), (og_rows, cots, 1024))
    selfs = {}
    rings = {}

    def source_y(q):
        return (y + STEPS[q]) % 4

    def depart(kind, q):
        source, target, _ = kinds[kind]
        dy = STEPS[q]
        yt = (y + 4 - dy) % 4

        def there(i, carry):
            zt, ct = (z + 4 + i // 2) % 8, (c + i) % 2
            et = yt * 16 + zt * 2 + ct
            rows = pl.ds(pl.multiple_of(4 * et, 4), 4)
            remote(
                source.at[rows], target.at[x, y, pl.ds(line4, 4)], there_s.at[kind, q], there_r.at[kind, q], (x, et)
            ).start()
            return carry

        if dy == 0:
            lax.fori_loop(0, 8, there, 0)
            lax.fori_loop(9, 16, there, 0)
            selfs[kind] = pltpu.make_async_copy(
                source.at[pl.ds(own4, 4)], target.at[x, y, pl.ds(line4, 4)], self_s.at[kind]
            )
            selfs[kind].start()
        else:
            lax.fori_loop(0, 16, there, 0)

    def bulk(kind, q):
        return sized.at[pl.ds(0, 15 if STEPS[q] == 0 else 16), :, pl.ds(0, kinds[kind][2])]

    def arrive(kind, q):
        if STEPS[q] == 0:
            selfs[kind].wait()
        view = bulk(kind, q)
        remote(view, view, there_s.at[kind, q], there_r.at[kind, q], to_right).wait_recv()
        block = kinds[kind][1].at[x, source_y(q)]
        for side, where in ((0, to_right), (1, to_left)):
            copy = remote(block, block, ring_s.at[kind, side, q], ring_r.at[kind, side, q], where)
            copy.start()
            rings[kind, side, q] = copy

    def forward(kind, q):
        for side, at, where in ((0, left, to_right), (1, right, to_left)):
            rings[kind, side, q].wait_recv()
            block = kinds[kind][1].at[at, source_y(q), pl.ds(32 * side, 32)]
            copy = remote(block, block, ring_s.at[kind, 2 + side, q], ring_r.at[kind, 2 + side, q], where)
            copy.start()
            rings[kind, 2 + side, q] = copy

    partner = spot(x, y, z, 1 - c)
    mine = pl.multiple_of(c * HALF, 128)
    other = pl.multiple_of((1 - c) * HALF, 128)
    row = pl.multiple_of(y * 64 + z * 8, 8)
    row4 = pl.multiple_of(row + 4 * c, 4)
    swap = remote(
        own_ref.at[:, pl.ds(other, HALF)],
        full_ref.at[x, pl.ds(row4, 4), pl.ds(other, HALF)],
        core_s,
        core_r,
        partner,
    )
    swap.start()
    keep = pltpu.make_async_copy(
        own_ref.at[:, pl.ds(mine, HALF)], full_ref.at[x, pl.ds(row4, 4), pl.ds(mine, HALF)], own_sem
    )
    keep.start()
    depart(1, 0)
    keep.wait()
    swap.wait()
    copies = []
    for dz in (4, 3, 5, 2, 6, 1, 7):
        block = full_ref.at[x, pl.ds(row, 8), pl.ds(mine, HALF)]
        copy = remote(block, block, z_s.at[dz - 1], z_r.at[dz - 1], spot(x, y, (z + dz) % 8, c))
        copy.start()
        copies.append(copy)
    depart(1, 1)
    xhat, inv_scale = normalize(frames_ref[...].astype(f32))
    xhat_ref[...] = xhat
    zeros = jnp.zeros((16, 1024), f32)
    gated_ref[0:16, :] = zeros
    gated_ref[144:160, :] = zeros
    cg_buf[0:16, :] = zeros
    cg_buf[144:160, :] = zeros
    tg_buf[...] = jnp.zeros((128, 1024), f32)
    part_ref[:, :, 2176:2304] = jnp.zeros((4, 256, 128), bf)
    for copy in copies:
        copy.wait()

    first = pl.multiple_of(mine, 128)
    second = pl.multiple_of(mine + SPLIT, 128)
    yrow = pl.multiple_of(y * 64, 64)

    def block_of(colour, level, index, part):
        cols = pl.ds(first, SPLIT) if colour == 0 else pl.ds(second, HALF - SPLIT)
        if level == 0:
            height = 64 if part is None else 32
            offset = 0 if part is None else part * 32
            if colour == 0:
                return full_ref.at[x, pl.ds(pl.multiple_of(index * 64 + offset, 32), height), cols]
            return full_ref.at[index, pl.ds(pl.multiple_of(yrow + offset, 32), height), cols]
        if colour == 0:
            height = 256 if part is None else 128
            offset = 0 if part is None else part * 128
            return full_ref.at[index, pl.ds(offset, height), cols]
        height = 64 if part is None else 32
        offset = 0 if part is None else part * 32
        return full_ref.at[:, pl.ds(pl.multiple_of(index * 64 + offset, 32), height), cols]

    def whereto(colour, level, step):
        if (colour + level) % 2 == 0:
            return spot(x, (y + step) % 4, z, c)
        return spot((x + step) % 4, y, z, c)

    def position(colour, level):
        return y if (colour + level) % 2 == 0 else x

    def opened(colour, level):
        at = position(colour, level)
        block = block_of(colour, level, at, None)
        base = (colour * 2 + level) * 4
        right = remote(block, block, gring_s.at[base], gring_r.at[base], whereto(colour, level, 1))
        left = remote(block, block, gring_s.at[base + 1], gring_r.at[base + 1], whereto(colour, level, 3))
        right.start()
        left.start()
        return right, left

    def passed(colour, level, pair, tell):
        at = position(colour, level)
        base = (colour * 2 + level) * 4
        right, left = pair
        right.wait_recv()
        block = block_of(colour, level, (at + 3) % 4, 0)
        on_right = remote(block, block, gring_s.at[base + 2], gring_r.at[base + 2], whereto(colour, level, 1))
        on_right.start()
        tell((at + 3) % 4, 1)
        left.wait_recv()
        block = block_of(colour, level, (at + 1) % 4, 1)
        on_left = remote(block, block, gring_s.at[base + 3], gring_r.at[base + 3], whereto(colour, level, 3))
        on_left.start()
        tell((at + 1) % 4, 2)
        return on_right, on_left

    def closed(colour, level, pair, onward, tell):
        at = position(colour, level)
        for copy in onward:
            copy.wait_recv()
        tell((at + 2) % 4, 3)
        for copy in pair + onward:
            copy.wait_send()

    silent = lambda index, slot: None
    low = [opened(colour, 0) for colour in (0, 1)]
    arrive(1, 0)
    low_on = [passed(colour, 0, low[colour], silent) for colour in (0, 1)]
    depart(1, 2)
    for colour in (0, 1):
        closed(colour, 0, low[colour], low_on[colour], silent)
    tails = []

    def teller(colour):
        def tell(index, slot):
            block = block_of(colour, 1, index, None)
            at = colour * 4 + slot
            copy = remote(block, block, tail_s.at[at], tail_r.at[at], partner)
            copy.start()
            tails.append(copy)

        return tell

    high = [opened(colour, 1) for colour in (0, 1)]
    for colour in (0, 1):
        teller(colour)(position(colour, 1), 0)
    depart(1, 3)
    arrive(1, 1)
    high_on = [passed(colour, 1, high[colour], teller(colour)) for colour in (0, 1)]
    forward(1, 0)
    for colour in (0, 1):
        closed(colour, 1, high[colour], high_on[colour], teller(colour))
    arrive(1, 2)
    for copy in tails:
        copy.wait()
    forward(1, 1)
    arrive(1, 3)

    normed = xhat_ref[...].astype(bf)

    def point(n, carry):
        cols = columns_of(n, 256)
        value = jnp.dot(normed, full_ref[:, :, cols].reshape(1024, 256), preferred_element_type=f32)
        gate = jnp.dot(normed, full_ref[:, :, columns_of(n + 4, 256)].reshape(1024, 256), preferred_element_type=f32)
        sig = jax.nn.sigmoid(gate)
        value_ref[:, cols] = value
        sig_ref[:, cols] = sig
        gated_ref[16:144, cols] = value * sig * mask
        return carry

    lax.fori_loop(0, 4, point, 0)
    small = full_ref[:, :, 2048:2176].reshape(1024, 128)
    taps_ref[...] = lax.dot_general(identity(), small, (((1,), (1,)), ((), ())), preferred_element_type=f32)
    forward(1, 2)

    def depth(n, carry):
        cols = columns_of(n, 128)
        total = jnp.zeros((128, 128), f32)
        for k in range(KERNEL):
            total = total + taps_ref[64 + k : 65 + k, cols] * gated_ref[k + 1 : k + 129, cols]
        conv_ref[:, cols] = total
        mixed_ref[:, cols] = (frames_ref[:, cols].astype(f32) + swish_of(total) * mask).astype(bf)
        return carry

    lax.fori_loop(0, 8, depth, 0)
    logits = jnp.dot(mixed_ref[...], small, preferred_element_type=f32)
    scores = [jax.nn.sigmoid(jnp.sum(jnp.where(pick, logits, 0.0), axis=1, keepdims=True)) for pick in picks]
    score_sum = scores[0] + scores[1]
    weights = [score / score_sum for score in scores]
    lane = lax.broadcasted_iota(jnp.int32, shape, 1)
    def fill(n, carry):
        cols = columns_of(n, 256)
        rows_buf[:, cols] = lax.dot_general(both, mixed_ref[:, cols], down, preferred_element_type=f32).astype(bf)
        return carry

    lax.fori_loop(0, 4, fill, 0)
    total = jnp.zeros((256, 128), f32)
    for k in (0, 1):
        upper = weights[k].astype(bf).astype(f32)
        parts = jnp.where(lane == 0, upper, jnp.where(lane == 1, weights[k] - upper, 0.0)).astype(bf)
        total = total + lax.dot_general(spots[k], parts, down, preferred_element_type=f32)
    rows_buf[:, 1024:TALL] = total.astype(bf)
    for q in range(4):
        depart(0, q)
    forward(1, 3)

    folds = {}

    def push(name, q, source, target, where):
        copy = remote(source, target, fold_s.at[name, q], fold_r.at[name, q], where)
        copy.start()
        folds[name, q] = copy

    def compute(q):
        ys = source_y(q)
        for kind in (1, 0):
            for side in (2, 3):
                rings[kind, side, q].wait_recv()

        def scale(n, carry):
            parts = slots[n, ys, :, 1024:TALL].astype(f32)
            weight = parts[:, 0:1] + parts[:, 1:2]
            scaled[n, ys] = (cots[n, ys].astype(f32) * weight).astype(bf)
            return carry

        lax.fori_loop(0, 4, scale, 0)

        def first(n, carry):
            cols = pl.ds(pl.multiple_of(n * 256, 256), 256)
            hidden = jnp.dot(slots[:, ys, :, 0:1024].reshape(256, 1024), inner[:, cols], preferred_element_type=f32)
            act_grad = lax.dot_general(
                scaled[:, ys].reshape(256, 1024), outer[cols, :], (((1,), (1,)), ((), ())), preferred_element_type=f32
            )
            sig = jax.nn.sigmoid(hidden)
            active[:, ys, :, cols] = (hidden * sig).astype(bf).reshape(4, 64, 256)
            slope = sig * (1.0 + hidden * (1.0 - sig))
            pre[:, ys, :, cols] = (act_grad * slope).astype(bf).reshape(4, 64, 256)
            return carry

        lax.fori_loop(0, 4, first, 0)
        def second(n, carry):
            cols = pl.ds(pl.multiple_of(n * 256, 256), 256)
            out = jnp.dot(active[:, ys].reshape(256, 1024), outer[:, cols], preferred_element_type=f32)
            part_y[q, :, :, cols] = out.astype(bf).reshape(4, 64, 256)
            out = lax.dot_general(
                pre[:, ys].reshape(256, 1024), inner[cols, :], (((1,), (1,)), ((), ())), preferred_element_type=f32
            )
            part_z[q, :, :, cols] = out.astype(bf).reshape(4, 64, 256)
            return carry

        lax.fori_loop(0, 4, second, 0)
        push(2, q, part_y.at[q, far], relay_y.at[q], to_right)
        push(3, q, part_z.at[q, far], relay_z.at[q], to_left)
        push(0, q, part_z.at[q, right], straight_z.at[q], to_right)
        push(1, q, part_y.at[q, left], straight_y.at[q], to_left)

    def relay(q):
        folds[2, q].wait_recv()
        part_y[q, right] = (part_y[q, right].astype(f32) + relay_y[q].astype(f32)).astype(bf)
        push(4, q, part_y.at[q, right], joint_y.at[q], to_right)
        folds[3, q].wait_recv()
        part_z[q, left] = (part_z[q, left].astype(f32) + relay_z[q].astype(f32)).astype(bf)
        push(5, q, part_z.at[q, left], joint_z.at[q], to_left)

    def deliver(q):
        yt = source_y(q)
        for name in (1, 4, 0, 5):
            folds[name, q].wait_recv()
        part_y[q, x] = (part_y[q, x].astype(f32) + straight_y[q].astype(f32) + joint_y[q].astype(f32)).astype(bf)
        part_z[q, x] = (part_z[q, x].astype(f32) + straight_z[q].astype(f32) + joint_z[q].astype(f32)).astype(bf)

        def back(i, carry):
            zt, ct = (z + 4 + i // 2) % 8, (c + i) % 2
            rows = pl.ds(pl.multiple_of(8 * zt + 4 * ct, 4), 4)
            for kind, (source, target) in enumerate(((part_y, y_ref), (part_z, z_ref))):
                remote(
                    source.at[q, x, rows], target.at[pl.ds(own4, 4)], back_s.at[kind], back_r.at[kind], (x, yt * 16 + zt * 2 + ct)
                ).start()
            return carry

        if STEPS[q] == 0:
            lax.fori_loop(0, 8, back, 0)
            lax.fori_loop(9, 16, back, 0)
            for kind, (source, target) in enumerate(((part_y, y_ref), (part_z, z_ref))):
                copy = pltpu.make_async_copy(
                    source.at[q, x, pl.ds(line4, 4)], target.at[pl.ds(own4, 4)], self_s.at[2 + kind]
                )
                copy.start()
                selfs[2 + kind] = copy
        else:
            lax.fori_loop(0, 16, back, 0)

    stores = []

    def weight_grad(which, left_ref, right_ref, target):
        def body(n, carry):
            cols = pl.ds(pl.multiple_of(n * 256, 256), 256)
            out = lax.dot_general(
                left_ref[:, :, :, cols].reshape(1024, 256),
                right_ref[...].reshape(1024, 1024),
                (((0,), (0,)), ((), ())),
                preferred_element_type=f32,
            )
            grad_buf[which, cols, :] = out.astype(bf)
            return carry

        lax.fori_loop(0, 4, body, 0)
        copy = pltpu.make_async_copy(grad_buf.at[which], target, store_sem.at[which])
        copy.start()
        stores.append(copy)

    for load in loads:
        load.wait()
    arrive(0, 0)
    arrive(0, 1)
    forward(0, 0)
    arrive(0, 2)
    forward(0, 1)
    compute(0)
    arrive(0, 3)
    forward(0, 2)
    compute(1)
    relay(0)
    forward(0, 3)
    compute(2)
    relay(1)
    deliver(0)
    compute(3)
    relay(2)
    turned[...] = jnp.transpose(xhat_ref[...]).astype(bf)
    deliver(1)
    weight_grad(1, active, scaled, outer_grad_hbm)
    relay(3)
    deliver(2)
    weight_grad(0, slots, pre, inner_grad_hbm)
    deliver(3)
    for kind in (0, 1):
        view = sized.at[pl.ds(0, 63), :, pl.ds(0, 1024)]
        remote(view, view, back_s.at[kind], back_r.at[kind], to_right).wait()
    for copy in (selfs[2], selfs[3]):
        copy.wait()

    def output(n, carry):
        cols = columns_of(n, 256)
        og = og_ref[:, cols].astype(f32)
        total = jnp.zeros((128, 256), f32)
        sums = []
        for k in (0, 1):
            picked = jnp.dot(spots[k], y_ref[:, cols], preferred_element_type=f32)
            total = total + weights[k] * picked
            sums.append(carry[k] + jnp.sum(og * picked, axis=1, keepdims=True))
        layer_ref[:, cols] = (mixed_ref[:, cols].astype(f32) + total).astype(bf)
        return tuple(sums)

    start = jnp.zeros((128, 1), f32)
    weight_sums = lax.fori_loop(0, 4, output, (start, start))
    mean_term = weight_sums[0] * weights[0] + weight_sums[1] * weights[1]
    logit_grad = jnp.zeros((128, 128), f32)
    for k in (0, 1):
        chosen = (weight_sums[k] - mean_term) / score_sum * scores[k] * (1.0 - scores[k])
        logit_grad = jnp.where(picks[k], chosen, logit_grad)
    logit_grad = logit_grad.astype(bf)
    across = (((1,), (1,)), ((), ()))

    def mix(n, carry):
        cols = columns_of(n, 256)
        grad = og_ref[:, cols].astype(f32) + jnp.dot(both, z_ref[:, cols], preferred_element_type=f32)
        grad = grad + lax.dot_general(logit_grad, full_ref[n, :, 2048:2176], across, preferred_element_type=f32)
        mg_buf[:, cols] = grad
        cg_buf[16:144, cols] = grad * mask * swish_slope(conv_ref[:, cols])
        return carry

    lax.fori_loop(0, 4, mix, 0)

    def depth_back(n, carry):
        cols = columns_of(n, 128)
        grad = cg_buf[16:144, cols]
        total = jnp.zeros((128, 128), f32)
        for k in range(KERNEL):
            total = total + taps_ref[64 + k : 65 + k, cols] * cg_buf[31 - k : 159 - k, cols]
            tg_buf[64 + k : 65 + k, cols] = jnp.sum(grad * gated_ref[k + 1 : k + 129, cols], axis=0, keepdims=True)
        total = total * mask
        sig = sig_ref[:, cols]
        pc_buf[:, cols] = (total * sig).astype(bf)
        pc_buf[:, columns_of(n + 8, 128)] = (total * value_ref[:, cols] * sig * (1.0 - sig)).astype(bf)
        return carry

    lax.fori_loop(0, 8, depth_back, 0)
    out = lax.dot_general(mixed_ref[...], logit_grad, down, preferred_element_type=f32)
    out = out + lax.dot_general(tg_buf[...].astype(bf), identity(), down, preferred_element_type=f32)
    part_ref[:, :, 2048:2176] = out.astype(bf).reshape(4, 256, 128)

    def outer_product(i, carry):
        cols = columns_of((i + 9 * (1 - c)) % 16, 128)
        out = jnp.dot(turned[...], pc_buf[:, cols], preferred_element_type=f32)
        part_ref[:, :, cols] = out.astype(bf).reshape(4, 256, 128)
        return carry

    lax.fori_loop(0, 9, outer_product, 0)
    colours = ((0, SPLIT), (SPLIT, HALF - SPLIT))
    order = (2, 1, 3, 0)

    def rows_of(colour, index):
        if colour == 0:
            return index, pl.ds(0, 256)
        return slice(None), pl.ds(pl.multiple_of(index * 64, 64), 64)

    swaps = {}
    for step in order:
        for colour, (begin, width) in enumerate(colours):
            at = ((x if colour == 0 else y) + step) % 4
            lead, rows = rows_of(colour, at)
            slot = colour * 4 + step
            copy = remote(
                part_ref.at[lead, rows, pl.ds(pl.multiple_of(other + begin, 128), width)],
                swap_buf.at[lead, rows, pl.ds(begin, width)],
                swap_s.at[slot],
                swap_r.at[slot],
                partner,
            )
            copy.start()
            swaps[colour, step] = copy

    lax.fori_loop(9, 16, outer_product, 0)

    def inward(n, carry):
        cols = columns_of(n, 256)
        out = lax.dot_general(pc_buf[...], full_ref[n, :, 0:2048], across, preferred_element_type=f32)
        ng_buf[:, cols] = out
        first = carry[0] + jnp.sum(out, axis=1, keepdims=True)
        second = carry[1] + jnp.sum(out * xhat_ref[:, cols], axis=1, keepdims=True)
        return first, second

    def finish_frames():
        first, second = lax.fori_loop(0, 4, inward, (start, start))
        first, second = first * (1.0 / 1024), second * (1.0 / 1024)

        def finish(n, carry):
            cols = columns_of(n, 256)
            grad = inv_scale * (ng_buf[:, cols] - first - xhat_ref[:, cols] * second)
            frames_grad_ref[:, cols] = (mg_buf[:, cols] + grad).astype(bf)
            return carry

        lax.fori_loop(0, 4, finish, 0)

    def first_to(colour, step):
        if colour == 0:
            return spot((x + step) % 4, y, z, c)
        return spot(x, (y + step) % 4, z, c)

    def second_to(colour, step):
        return first_to(1 - colour, step)

    def fold(colour, step, extra):
        begin, width = colours[colour]
        at = ((x if colour == 0 else y) + step) % 4
        swaps[colour, step].wait_recv()

        def body(t, carry):
            if colour == 0:
                lead, row = at, pl.multiple_of(t * 32, 32)
            else:
                lead, row = t // 2, pl.multiple_of(at * 64 + (t % 2) * 32, 32)
            value = part_ref[lead, pl.ds(row, 32), pl.ds(pl.multiple_of(mine + begin, 128), width)].astype(jnp.float32)
            value = value + swap_buf[lead, pl.ds(row, 32), pl.ds(begin, width)].astype(jnp.float32)
            value = extra(t, value)
            half_buf[colour, step, pl.ds(pl.multiple_of(t * 32, 32), 32), pl.ds(0, width)] = value.astype(jnp.bfloat16)
            return carry

        return body

    plain = lambda t, value: value
    sent = []
    pend = {}
    for colour, (begin, width) in enumerate(colours):
        lax.fori_loop(0, 8, fold(colour, 2, plain), 0)
        for side, step in ((0, 1), (1, 3)):
            slot = colour * 8 + side
            copy = remote(
                half_buf.at[colour, 2, pl.ds(side * 128, 128), pl.ds(0, width)],
                far_buf.at[colour, side, :, pl.ds(0, width)],
                rring_s.at[slot],
                rring_r.at[slot],
                first_to(colour, step),
            )
            copy.start()
            pend[colour, side] = copy
            sent.append(copy)
    finish_frames()
    for colour, (begin, width) in enumerate(colours):
        for side, step in ((0, 1), (1, 3)):
            lo = side * 4

            lax.fori_loop(4 - lo, 8 - lo, fold(colour, step, plain), 0)
            pend[colour, side].wait_recv()

            def extra(t, value, colour=colour, side=side, lo=lo, width=width):
                row = pl.multiple_of((t - lo) * 32, 32)
                return value + far_buf[colour, side, pl.ds(row, 32), pl.ds(0, width)].astype(jnp.float32)

            def again(t, carry, colour=colour, step=step, extra=extra, begin=begin, width=width):
                at = ((x if colour == 0 else y) + step) % 4
                if colour == 0:
                    lead, row = at, pl.multiple_of(t * 32, 32)
                else:
                    lead, row = t // 2, pl.multiple_of(at * 64 + (t % 2) * 32, 32)
                value = part_ref[lead, pl.ds(row, 32), pl.ds(pl.multiple_of(mine + begin, 128), width)].astype(jnp.float32)
                value = value + swap_buf[lead, pl.ds(row, 32), pl.ds(begin, width)].astype(jnp.float32)
                value = extra(t, value)
                half_buf[colour, step, pl.ds(pl.multiple_of(t * 32, 32), 32), pl.ds(0, width)] = value.astype(jnp.bfloat16)
                return carry

            lax.fori_loop(lo, lo + 4, again, 0)
            slot = colour * 8 + 2 + side
            copy = remote(
                half_buf.at[colour, step, :, pl.ds(0, width)],
                near_buf.at[colour, side, :, pl.ds(0, width)],
                rring_s.at[slot],
                rring_r.at[slot],
                first_to(colour, step),
            )
            copy.start()
            pend[colour, 2 + side] = copy
            sent.append(copy)
    for colour, (begin, width) in enumerate(colours):
        pend[colour, 2].wait_recv()
        pend[colour, 3].wait_recv()

        def extra(t, value, colour=colour, width=width):
            row = pl.multiple_of(t * 32, 32)
            for side in (0, 1):
                value = value + near_buf[colour, side, pl.ds(row, 32), pl.ds(0, width)].astype(jnp.float32)
            return value

        body = fold(colour, 0, extra)
        lax.fori_loop(0, 8, body, 0)
        at = y if colour == 0 else x
        for side, step in ((0, 1), (1, 3)):
            row = pl.multiple_of(((at + 2) % 4) * 64 + side * 32, 32)
            slot = colour * 8 + 4 + side
            copy = remote(
                half_buf.at[colour, 0, pl.ds(row, 32), pl.ds(0, width)],
                mid_far.at[colour, side, :, pl.ds(0, width)],
                rring_s.at[slot],
                rring_r.at[slot],
                second_to(colour, step),
            )
            copy.start()
            pend[colour, 4 + side] = copy
            sent.append(copy)
    for colour, (begin, width) in enumerate(colours):
        at = y if colour == 0 else x
        for side, step in ((0, 1), (1, 3)):
            row = pl.multiple_of(((at + step) % 4) * 64, 32)
            pend[colour, 4 + side].wait_recv()
            for piece in (0, 1):
                value = half_buf[colour, 0, pl.ds(pl.multiple_of(row + piece * 32, 32), 32), pl.ds(0, width)]
                if piece == side:
                    value = value.astype(jnp.float32) + mid_far[colour, side, :, pl.ds(0, width)].astype(jnp.float32)
                    value = value.astype(jnp.bfloat16)
                mid_buf[colour, side, pl.ds(piece * 32, 32), pl.ds(0, width)] = value
            slot = colour * 8 + 6 + side
            copy = remote(
                mid_buf.at[colour, side, :, pl.ds(0, width)],
                mid_near.at[colour, side, :, pl.ds(0, width)],
                rring_s.at[slot],
                rring_r.at[slot],
                second_to(colour, step),
            )
            copy.start()
            pend[colour, 6 + side] = copy
            sent.append(copy)
    for colour, (begin, width) in enumerate(colours):
        at = y if colour == 0 else x
        pend[colour, 6].wait_recv()
        pend[colour, 7].wait_recv()
        for piece in range(2):
            rows = pl.ds(piece * 32, 32)
            value = half_buf[colour, 0, pl.ds(pl.multiple_of(at * 64 + piece * 32, 32), 32), pl.ds(0, width)].astype(jnp.float32)
            for side in (0, 1):
                value = value + mid_near[colour, side, rows, pl.ds(0, width)].astype(jnp.float32)
            z_src[pl.ds(piece * 4, 4), :, pl.ds(begin, width)] = value.astype(jnp.bfloat16).reshape(4, 8, width)
    z_copies = []
    for dz in (4, 3, 5, 2, 6, 1, 7):
        to = (z + dz) % 8
        copy = remote(z_src.at[to], z_buf.at[dz - 1], rz_s.at[dz - 1], rz_r.at[dz - 1], spot(x, y, to, c))
        copy.start()
        z_copies.append(copy)
    total = z_src[z].astype(jnp.float32)
    for copy in z_copies:
        copy.wait_recv()
    for k in range(7):
        total = total + z_buf[k].astype(jnp.float32)
    last_src[...] = total
    last = remote(last_src, last_buf, last_s, last_r, partner)
    last.start()
    for copy in sent + z_copies:
        copy.wait_send()
    for copy in swaps.values():
        copy.wait_send()
    kept = jnp.where(c == 0, last_src[0:4, :], last_src[4:8, :])
    last.wait()
    got = jnp.where(c == 0, last_buf[0:4, :], last_buf[4:8, :])
    low, high = jnp.where(c == 0, kept, got), jnp.where(c == 0, got, kept)
    out_ref[:, 0:HALF] = low
    out_ref[:, HALF:2048] = high[:, 0 : 2048 - HALF]
    router_grad_ref[...] = high[:, 2048 - HALF : 2112 - HALF]
    depth_ref[...] = high[:, 2112 - HALF : 2112 + KERNEL - HALF]
    for kind in (0, 1):
        for q in range(4):
            view = bulk(kind, q)
            remote(view, view, there_s.at[kind, q], there_r.at[kind, q], to_right).wait_send()
    for copy in list(rings.values()) + list(folds.values()):
        copy.wait_send()
    for copy in stores:
        copy.wait()


def layer(frames, lengths, ids, og, conv_in, router, depthwise, inner, outer):
    dma, bf, f32 = pltpu.SemaphoreType.DMA, jnp.bfloat16, jnp.float32
    block = lambda *lead: pltpu.VMEM(lead + (64, 1024), bf)
    shape = lambda *args: jax.ShapeDtypeStruct(*args)
    vmem, anywhere = pl.BlockSpec(memory_space=pltpu.VMEM), pl.BlockSpec(memory_space=pl.ANY)
    wide = pltpu.VMEM((128, 1024), f32)
    long = pltpu.VMEM((160, 1024), f32)
    half = lambda *lead: pltpu.VMEM(lead + (SPLIT,), bf)
    return pl.pallas_call(
        layer_kernel,
        out_shape=(
            shape((128, 1024), bf), shape((128, 1024), bf), shape((4, 2048), f32), shape((4, KERNEL), f32),
            shape((4, 64), f32), shape((1024, 1024), bf), shape((1024, 1024), bf),
        ),
        in_specs=[vmem, pl.BlockSpec(memory_space=pltpu.SMEM)] + [vmem] * 5 + [anywhere] * 2,
        out_specs=(vmem,) * 5 + (anywhere,) * 2,
        scratch_shapes=[
            pltpu.VMEM((4, 256, WIDE), bf), pltpu.VMEM((128, 1024), bf), wide, wide, wide, wide, long, wide,
            pltpu.VMEM((256, 1024), bf), pltpu.VMEM((256, 1024), bf),
            pltpu.VMEM((4, WIDE), bf), pltpu.VMEM((256, TALL), bf), pltpu.VMEM((256, 1024), bf),
            pltpu.VMEM((4, 4, 64, TALL), bf),
        ]
        + [block(4, 4)] * 4
        + [pltpu.VMEM((1024, 1024), bf)] * 2
        + [block(4, 4)] * 2
        + [block(4)] * 6
        + [pltpu.VMEM((2, 1024, 1024), bf), pltpu.VMEM((63, 4, TALL), bf)]
        + [wide, long, wide, pltpu.VMEM((128, 2048), bf), pltpu.VMEM((1024, 128), bf), wide]
        + [
            pltpu.VMEM((4, 256, WIDE), bf), pltpu.VMEM((4, 256, HALF), bf), half(2, 4, 256), half(2, 2, 128),
            half(2, 2, 256), half(2, 2, 64), half(2, 2, 32), half(2, 2, 64), pltpu.VMEM((8, 8, HALF), bf),
            pltpu.VMEM((7, 8, HALF), bf), pltpu.VMEM((8, HALF), f32), pltpu.VMEM((8, HALF), f32),
        ]
        + [
            dma((2,)), dma, dma, dma, dma((7,)), dma((7,)), dma((16,)), dma((16,)), dma((8,)), dma((8,)),
            dma((4,)), dma((2, 4)), dma((2, 4)), dma((2, 4, 4)), dma((2, 4, 4)), dma((6, 4)), dma((6, 4)), dma((2,)),
            dma((2,)), dma((2,)), dma((8,)), dma((8,)), dma((16,)), dma((16,)), dma((7,)), dma((7,)), dma, dma,
        ],
        compiler_params=pltpu.CompilerParams(
            collective_id=2, has_side_effects=True, vmem_limit_bytes=VMEM_LIMIT
        ),
        name="layer",
    )(frames, lengths, ids, og, conv_in, router, depthwise, inner, outer)


def pass_kernel(*refs):
    sources, targets, bufs, sems = refs[:7], refs[7:14], refs[14:21], refs[21]
    loads, stores = [], []
    for i in range(7):
        for part in range(4 if i >= 5 else 1):
            pick = (lambda ref: ref) if i < 5 else (lambda ref: ref.at[pl.ds(part * 256, 256)])
            at = len(loads)
            loads.append(pltpu.make_async_copy(pick(sources[i]), pick(bufs[i]), sems.at[0, at]))
            stores.append(pltpu.make_async_copy(pick(bufs[i]), pick(targets[i]), sems.at[1, at]))
    order = list(range(5, 13)) + list(range(5))
    for at in order:
        loads[at].start()
    for at in order:
        loads[at].wait()
        stores[at].start()
    for at in order:
        stores[at].wait()


def pass_on(values):
    shapes = tuple(jax.ShapeDtypeStruct(value.shape, value.dtype) for value in values)
    anywhere = pl.BlockSpec(memory_space=pl.ANY)
    return pl.pallas_call(
        pass_kernel,
        out_shape=shapes,
        in_specs=[anywhere] * 7,
        out_specs=(anywhere,) * 7,
        scratch_shapes=[pltpu.VMEM(value.shape, value.dtype) for value in values] + [pltpu.SemaphoreType.DMA((2, 13))],
        compiler_params=pltpu.CompilerParams(vmem_limit_bytes=VMEM_LIMIT),
        name="pass_on",
    )(*values)


def per_device(frames, lengths, expert_ids, conv_in, depthwise, router, w_in, w_out, out_grad):
    *outs, w_in_grad, w_out_grad = pass_on(
        layer(frames, lengths, expert_ids, out_grad, conv_in, router, depthwise, w_in[0], w_out[0])
    )
    return (*outs, w_in_grad[None], w_out_grad[None])


def solution(mesh):
    in_specs = (
        P(("dp", "expert"), None),
        P(("dp", "expert")),
        P(("dp", "expert"), None),
        P(("dp", "expert"), None),
        P(("dp", "expert"), None),
        P(("dp", "expert"), None),
        P("expert", None, "dp"),
        P("expert", "dp", None),
        P(("dp", "expert"), None),
    )
    out_specs = (
        P(("dp", "expert"), None),
        P(("dp", "expert"), None),
        P(("dp", "expert"), None),
        P(("dp", "expert"), None),
        P(("dp", "expert"), None),
        P("expert", None, "dp"),
        P("expert", "dp", None),
    )
    return jax.shard_map(
        per_device, mesh=mesh, in_specs=in_specs, out_specs=out_specs, check_vma=False
    )
```

```python
import jax
import jax.numpy as jnp
from jax import lax
from jax.experimental import pallas as pl
from jax.experimental.pallas import tpu as pltpu
from jax.sharding import PartitionSpec as P

KERNEL = 31
EPSILON = 1e-05


def swish_of(values):
    return values * jax.nn.sigmoid(values)


def swish_slope(values):
    sigmoid_v = jax.nn.sigmoid(values)
    return sigmoid_v * (1.0 + values * (1.0 - sigmoid_v))


def normalize(values):
    center = values - jnp.mean(values, axis=-1, keepdims=True)
    inv_scale = lax.rsqrt(jnp.mean(center * center, axis=-1, keepdims=True) + EPSILON)
    return (center * inv_scale, inv_scale)


MESH = pl.DeviceIdType.MESH
HALF = 1152
WIDE = 2 * HALF
SPLIT = 640
VMEM_LIMIT = 60 * 1024 * 1024


def place():
    x = lax.axis_index("dp")
    e = lax.axis_index("expert")
    return x, e // 16, (e // 2) % 8, e % 2


def spot(x, y, z, c):
    return (x, y * 16 + z * 2 + c)


def remote(src, dst, send, recv, where):
    return pltpu.make_async_remote_copy(
        src_ref=src, dst_ref=dst, send_sem=send, recv_sem=recv, device_id=where, device_id_type=MESH
    )


STEPS = (0, 1, 3, 2)
TALL = 1152


def columns_of(n, width):
    return pl.ds(pl.multiple_of(n * width, width), width)


def mask_of(length_ref):
    return (lax.broadcasted_iota(jnp.int32, (128, 1), 0) < length_ref[0]).astype(jnp.float32)


def index_columns(ids_ref):
    shape = (128, 128)
    diagonal = lax.broadcasted_iota(jnp.int32, shape, 0) == lax.broadcasted_iota(jnp.int32, shape, 1)
    rows = ids_ref[...].astype(jnp.float32)
    return [jnp.sum(jnp.where(diagonal, rows[k : k + 1, :], 0.0), axis=1, keepdims=True) for k in (0, 1)]


def identity():
    shape = (128, 128)
    return (lax.broadcasted_iota(jnp.int32, shape, 0) == lax.broadcasted_iota(jnp.int32, shape, 1)).astype(jnp.bfloat16)


def layer_kernel(
    frames_ref, length_ref, ids_ref, og_ref, conv_in_ref, router_ref, depthwise_ref, inner_hbm, outer_hbm,
    layer_ref, frames_grad_ref, out_ref, depth_ref, router_grad_ref, inner_grad_hbm, outer_grad_hbm,
    full_ref, mixed_ref, value_ref, sig_ref, conv_ref, xhat_ref, gated_ref, taps_ref, y_ref, z_ref,
    own_ref, rows_buf, og_rows, slots, cots, scaled, active, pre, inner, outer, part_y, part_z, straight_y, straight_z,
    relay_y, relay_z, joint_y, joint_z, grad_buf, sized, mg_buf, cg_buf, tg_buf, pc_buf, turned, ng_buf,
    part_ref, swap_buf, half_buf, far_buf, near_buf, mid_buf, mid_far, mid_near, z_src, z_buf, last_src, last_buf,
    load_sem, core_s, core_r, own_sem, z_s, z_r, gring_s, gring_r, tail_s, tail_r, self_s, there_s, there_r, ring_s,
    ring_r, fold_s, fold_r, back_s, back_r, store_sem, swap_s, swap_r, rring_s, rring_r, rz_s, rz_r, last_s, last_r
):
    x, y, z, c = place()
    f32, bf = jnp.float32, jnp.bfloat16
    here = y * 16 + z * 2 + c
    right, left, far = (x + 1) % 4, (x + 3) % 4, (x + 2) % 4
    to_right, to_left = spot(right, y, z, c), spot(left, y, z, c)
    loads = [
        pltpu.make_async_copy(inner_hbm, inner, load_sem.at[0]),
        pltpu.make_async_copy(outer_hbm, outer, load_sem.at[1]),
    ]
    for load in loads:
        load.start()

    barrier = pltpu.get_barrier_semaphore()

    def hail(i, carry):
        pl.semaphore_signal(barrier, inc=1, device_id=(x, (here + i) % 64), device_id_type=MESH)
        return carry

    lax.fori_loop(1, 64, hail, 0)
    for where in (to_right, to_left):
        pl.semaphore_signal(barrier, inc=1, device_id=where, device_id_type=MESH)

    own_ref[:, 0:2048] = conv_in_ref[...]
    own_ref[:, 2048:WIDE] = jnp.concatenate(
        [router_ref[...].astype(f32), depthwise_ref[...].astype(f32), jnp.zeros((4, WIDE - 2112 - KERNEL), f32)], axis=1
    ).astype(bf)
    mask = mask_of(length_ref)
    index = index_columns(ids_ref)
    lanes = lax.broadcasted_iota(jnp.int32, (128, 128), 1).astype(f32)
    picks = [lanes == column for column in index]
    count = (jnp.where(picks[0] | picks[1], 1.0, 0.0) * mask).astype(bf)
    shape = (128, 128)
    below = (lax.broadcasted_iota(jnp.int32, shape, 1) < lax.broadcasted_iota(jnp.int32, shape, 0)).astype(bf)
    before = jnp.dot(below, count, preferred_element_type=f32)
    wide = lax.broadcasted_iota(jnp.int32, (128, 256), 1).astype(f32)
    slot_of, spots = [], []
    for k, pick in enumerate(picks):
        position = jnp.sum(jnp.where(pick, before, 0.0), axis=1, keepdims=True)
        kept = (position < 4.0) & (mask > 0.0)
        slot = jnp.where(kept, index[k] * 4.0 + position, -1.0)
        slot_of.append(slot)
        spots.append((wide == slot).astype(bf))
    both = spots[0] + spots[1]
    down = (((0,), (0,)), ((), ()))

    def fill_og(n, carry):
        cols = columns_of(n, 256)
        og_rows[:, cols] = lax.dot_general(both, og_ref[:, cols], down, preferred_element_type=f32).astype(bf)
        return carry

    lax.fori_loop(0, 4, fill_og, 0)
    pl.semaphore_wait(barrier, 65)

    own4 = pl.multiple_of(4 * here, 4)
    line4 = pl.multiple_of(8 * z + 4 * c, 4)
    kinds = ((rows_buf, slots, TALL), (og_rows, cots, 1024))
    selfs = {}
    rings = {}

    def source_y(q):
        return (y + STEPS[q]) % 4

    def depart(kind, q):
        source, target, _ = kinds[kind]
        dy = STEPS[q]
        yt = (y + 4 - dy) % 4

        def there(i, carry):
            zt, ct = (z + 4 + i // 2) % 8, (c + i) % 2
            et = yt * 16 + zt * 2 + ct
            rows = pl.ds(pl.multiple_of(4 * et, 4), 4)
            remote(
                source.at[rows], target.at[x, y, pl.ds(line4, 4)], there_s.at[kind, q], there_r.at[kind, q], (x, et)
            ).start()
            return carry

        if dy == 0:
            lax.fori_loop(0, 8, there, 0)
            lax.fori_loop(9, 16, there, 0)
            selfs[kind] = pltpu.make_async_copy(
                source.at[pl.ds(own4, 4)], target.at[x, y, pl.ds(line4, 4)], self_s.at[kind]
            )
            selfs[kind].start()
        else:
            lax.fori_loop(0, 16, there, 0)

    def bulk(kind, q):
        return sized.at[pl.ds(0, 15 if STEPS[q] == 0 else 16), :, pl.ds(0, kinds[kind][2])]

    def arrive(kind, q):
        if STEPS[q] == 0:
            selfs[kind].wait()
        view = bulk(kind, q)
        remote(view, view, there_s.at[kind, q], there_r.at[kind, q], to_right).wait_recv()
        block = kinds[kind][1].at[x, source_y(q)]
        for side, where in ((0, to_right), (1, to_left)):
            copy = remote(block, block, ring_s.at[kind, side, q], ring_r.at[kind, side, q], where)
            copy.start()
            rings[kind, side, q] = copy

    def forward(kind, q):
        for side, at, where in ((0, left, to_right), (1, right, to_left)):
            rings[kind, side, q].wait_recv()
            block = kinds[kind][1].at[at, source_y(q), pl.ds(32 * side, 32)]
            copy = remote(block, block, ring_s.at[kind, 2 + side, q], ring_r.at[kind, 2 + side, q], where)
            copy.start()
            rings[kind, 2 + side, q] = copy

    partner = spot(x, y, z, 1 - c)
    mine = pl.multiple_of(c * HALF, 128)
    other = pl.multiple_of((1 - c) * HALF, 128)
    row = pl.multiple_of(y * 64 + z * 8, 8)
    row4 = pl.multiple_of(row + 4 * c, 4)
    swap = remote(
        own_ref.at[:, pl.ds(other, HALF)],
        full_ref.at[x, pl.ds(row4, 4), pl.ds(other, HALF)],
        core_s,
        core_r,
        partner,
    )
    swap.start()
    keep = pltpu.make_async_copy(
        own_ref.at[:, pl.ds(mine, HALF)], full_ref.at[x, pl.ds(row4, 4), pl.ds(mine, HALF)], own_sem
    )
    keep.start()
    depart(1, 0)
    keep.wait()
    swap.wait()
    copies = []
    for dz in (4, 3, 5, 2, 6, 1, 7):
        block = full_ref.at[x, pl.ds(row, 8), pl.ds(mine, HALF)]
        copy = remote(block, block, z_s.at[dz - 1], z_r.at[dz - 1], spot(x, y, (z + dz) % 8, c))
        copy.start()
        copies.append(copy)
    depart(1, 1)
    xhat, inv_scale = normalize(frames_ref[...].astype(f32))
    xhat_ref[...] = xhat
    zeros = jnp.zeros((16, 1024), f32)
    gated_ref[0:16, :] = zeros
    gated_ref[144:160, :] = zeros
    cg_buf[0:16, :] = zeros
    cg_buf[144:160, :] = zeros
    tg_buf[...] = jnp.zeros((128, 1024), f32)
    part_ref[:, :, 2176:2304] = jnp.zeros((4, 256, 128), bf)
    for copy in copies:
        copy.wait()

    first = pl.multiple_of(mine, 128)
    second = pl.multiple_of(mine + SPLIT, 128)
    yrow = pl.multiple_of(y * 64, 64)

    def block_of(colour, level, index, part):
        cols = pl.ds(first, SPLIT) if colour == 0 else pl.ds(second, HALF - SPLIT)
        if level == 0:
            height = 64 if part is None else 32
            offset = 0 if part is None else part * 32
            if colour == 0:
                return full_ref.at[x, pl.ds(pl.multiple_of(index * 64 + offset, 32), height), cols]
            return full_ref.at[index, pl.ds(pl.multiple_of(yrow + offset, 32), height), cols]
        if colour == 0:
            height = 256 if part is None else 128
            offset = 0 if part is None else part * 128
            return full_ref.at[index, pl.ds(offset, height), cols]
        height = 64 if part is None else 32
        offset = 0 if part is None else part * 32
        return full_ref.at[:, pl.ds(pl.multiple_of(index * 64 + offset, 32), height), cols]

    def whereto(colour, level, step):
        if (colour + level) % 2 == 0:
            return spot(x, (y + step) % 4, z, c)
        return spot((x + step) % 4, y, z, c)

    def position(colour, level):
        return y if (colour + level) % 2 == 0 else x

    def opened(colour, level):
        at = position(colour, level)
        block = block_of(colour, level, at, None)
        base = (colour * 2 + level) * 4
        right = remote(block, block, gring_s.at[base], gring_r.at[base], whereto(colour, level, 1))
        left = remote(block, block, gring_s.at[base + 1], gring_r.at[base + 1], whereto(colour, level, 3))
        right.start()
        left.start()
        return right, left

    def passed(colour, level, pair, tell):
        at = position(colour, level)
        base = (colour * 2 + level) * 4
        right, left = pair
        right.wait_recv()
        block = block_of(colour, level, (at + 3) % 4, 0)
        on_right = remote(block, block, gring_s.at[base + 2], gring_r.at[base + 2], whereto(colour, level, 1))
        on_right.start()
        tell((at + 3) % 4, 1)
        left.wait_recv()
        block = block_of(colour, level, (at + 1) % 4, 1)
        on_left = remote(block, block, gring_s.at[base + 3], gring_r.at[base + 3], whereto(colour, level, 3))
        on_left.start()
        tell((at + 1) % 4, 2)
        return on_right, on_left

    def closed(colour, level, pair, onward, tell):
        at = position(colour, level)
        for copy in onward:
            copy.wait_recv()
        tell((at + 2) % 4, 3)
        for copy in pair + onward:
            copy.wait_send()

    silent = lambda index, slot: None
    low = [opened(colour, 0) for colour in (0, 1)]
    arrive(1, 0)
    low_on = [passed(colour, 0, low[colour], silent) for colour in (0, 1)]
    depart(1, 2)
    for colour in (0, 1):
        closed(colour, 0, low[colour], low_on[colour], silent)
    tails = []

    def teller(colour):
        def tell(index, slot):
            block = block_of(colour, 1, index, None)
            at = colour * 4 + slot
            copy = remote(block, block, tail_s.at[at], tail_r.at[at], partner)
            copy.start()
            tails.append(copy)

        return tell

    high = [opened(colour, 1) for colour in (0, 1)]
    for colour in (0, 1):
        teller(colour)(position(colour, 1), 0)
    depart(1, 3)
    arrive(1, 1)
    high_on = [passed(colour, 1, high[colour], teller(colour)) for colour in (0, 1)]
    forward(1, 0)
    for colour in (0, 1):
        closed(colour, 1, high[colour], high_on[colour], teller(colour))
    arrive(1, 2)
    for copy in tails:
        copy.wait()
    forward(1, 1)
    arrive(1, 3)

    normed = xhat_ref[...].astype(bf)

    def point(n, carry):
        cols = columns_of(n, 256)
        value = jnp.dot(normed, full_ref[:, :, cols].reshape(1024, 256), preferred_element_type=f32)
        gate = jnp.dot(normed, full_ref[:, :, columns_of(n + 4, 256)].reshape(1024, 256), preferred_element_type=f32)
        sig = jax.nn.sigmoid(gate)
        value_ref[:, cols] = value
        sig_ref[:, cols] = sig
        gated_ref[16:144, cols] = value * sig * mask
        return carry

    lax.fori_loop(0, 4, point, 0)
    small = full_ref[:, :, 2048:2176].reshape(1024, 128)
    taps_ref[...] = lax.dot_general(identity(), small, (((1,), (1,)), ((), ())), preferred_element_type=f32)
    forward(1, 2)

    def depth(n, carry):
        cols = columns_of(n, 128)
        total = jnp.zeros((128, 128), f32)
        for k in range(KERNEL):
            total = total + taps_ref[64 + k : 65 + k, cols] * gated_ref[k + 1 : k + 129, cols]
        conv_ref[:, cols] = total
        mixed_ref[:, cols] = (frames_ref[:, cols].astype(f32) + swish_of(total) * mask).astype(bf)
        return carry

    lax.fori_loop(0, 8, depth, 0)
    logits = jnp.dot(mixed_ref[...], small, preferred_element_type=f32)
    scores = [jax.nn.sigmoid(jnp.sum(jnp.where(pick, logits, 0.0), axis=1, keepdims=True)) for pick in picks]
    score_sum = scores[0] + scores[1]
    weights = [score / score_sum for score in scores]
    lane = lax.broadcasted_iota(jnp.int32, shape, 1)
    def fill(n, carry):
        cols = columns_of(n, 256)
        rows_buf[:, cols] = lax.dot_general(both, mixed_ref[:, cols], down, preferred_element_type=f32).astype(bf)
        return carry

    lax.fori_loop(0, 4, fill, 0)
    total = jnp.zeros((256, 128), f32)
    for k in (0, 1):
        upper = weights[k].astype(bf).astype(f32)
        parts = jnp.where(lane == 0, upper, jnp.where(lane == 1, weights[k] - upper, 0.0)).astype(bf)
        total = total + lax.dot_general(spots[k], parts, down, preferred_element_type=f32)
    rows_buf[:, 1024:TALL] = total.astype(bf)
    for q in range(4):
        depart(0, q)
    forward(1, 3)

    folds = {}

    def push(name, q, source, target, where):
        copy = remote(source, target, fold_s.at[name, q], fold_r.at[name, q], where)
        copy.start()
        folds[name, q] = copy

    def compute(q):
        ys = source_y(q)
        for kind in (1, 0):
            for side in (2, 3):
                rings[kind, side, q].wait_recv()

        def scale(n, carry):
            parts = slots[n, ys, :, 1024:TALL].astype(f32)
            weight = parts[:, 0:1] + parts[:, 1:2]
            scaled[n, ys] = (cots[n, ys].astype(f32) * weight).astype(bf)
            return carry

        lax.fori_loop(0, 4, scale, 0)

        def first(n, carry):
            cols = pl.ds(pl.multiple_of(n * 256, 256), 256)
            hidden = jnp.dot(slots[:, ys, :, 0:1024].reshape(256, 1024), inner[:, cols], preferred_element_type=f32)
            act_grad = lax.dot_general(
                scaled[:, ys].reshape(256, 1024), outer[cols, :], (((1,), (1,)), ((), ())), preferred_element_type=f32
            )
            sig = jax.nn.sigmoid(hidden)
            active[:, ys, :, cols] = (hidden * sig).astype(bf).reshape(4, 64, 256)
            slope = sig * (1.0 + hidden * (1.0 - sig))
            pre[:, ys, :, cols] = (act_grad * slope).astype(bf).reshape(4, 64, 256)
            return carry

        lax.fori_loop(0, 4, first, 0)
        def second(n, carry):
            cols = pl.ds(pl.multiple_of(n * 256, 256), 256)
            out = jnp.dot(active[:, ys].reshape(256, 1024), outer[:, cols], preferred_element_type=f32)
            part_y[q, :, :, cols] = out.astype(bf).reshape(4, 64, 256)
            out = lax.dot_general(
                pre[:, ys].reshape(256, 1024), inner[cols, :], (((1,), (1,)), ((), ())), preferred_element_type=f32
            )
            part_z[q, :, :, cols] = out.astype(bf).reshape(4, 64, 256)
            return carry

        lax.fori_loop(0, 4, second, 0)
        push(2, q, part_y.at[q, far], relay_y.at[q], to_right)
        push(3, q, part_z.at[q, far], relay_z.at[q], to_left)
        push(0, q, part_z.at[q, right], straight_z.at[q], to_right)
        push(1, q, part_y.at[q, left], straight_y.at[q], to_left)

    def relay(q):
        folds[2, q].wait_recv()
        part_y[q, right] = (part_y[q, right].astype(f32) + relay_y[q].astype(f32)).astype(bf)
        push(4, q, part_y.at[q, right], joint_y.at[q], to_right)
        folds[3, q].wait_recv()
        part_z[q, left] = (part_z[q, left].astype(f32) + relay_z[q].astype(f32)).astype(bf)
        push(5, q, part_z.at[q, left], joint_z.at[q], to_left)

    def deliver(q):
        yt = source_y(q)
        for name in (1, 4, 0, 5):
            folds[name, q].wait_recv()
        part_y[q, x] = (part_y[q, x].astype(f32) + straight_y[q].astype(f32) + joint_y[q].astype(f32)).astype(bf)
        part_z[q, x] = (part_z[q, x].astype(f32) + straight_z[q].astype(f32) + joint_z[q].astype(f32)).astype(bf)

        def back(i, carry):
            zt, ct = (z + 4 + i // 2) % 8, (c + i) % 2
            rows = pl.ds(pl.multiple_of(8 * zt + 4 * ct, 4), 4)
            for kind, (source, target) in enumerate(((part_y, y_ref), (part_z, z_ref))):
                remote(
                    source.at[q, x, rows], target.at[pl.ds(own4, 4)], back_s.at[kind], back_r.at[kind], (x, yt * 16 + zt * 2 + ct)
                ).start()
            return carry

        if STEPS[q] == 0:
            lax.fori_loop(0, 8, back, 0)
            lax.fori_loop(9, 16, back, 0)
            for kind, (source, target) in enumerate(((part_y, y_ref), (part_z, z_ref))):
                copy = pltpu.make_async_copy(
                    source.at[q, x, pl.ds(line4, 4)], target.at[pl.ds(own4, 4)], self_s.at[2 + kind]
                )
                copy.start()
                selfs[2 + kind] = copy
        else:
            lax.fori_loop(0, 16, back, 0)

    stores = []

    def weight_grad(which, left_ref, right_ref, target):
        def body(n, carry):
            cols = pl.ds(pl.multiple_of(n * 256, 256), 256)
            out = lax.dot_general(
                left_ref[:, :, :, cols].reshape(1024, 256),
                right_ref[...].reshape(1024, 1024),
                (((0,), (0,)), ((), ())),
                preferred_element_type=f32,
            )
            grad_buf[which, cols, :] = out.astype(bf)
            return carry

        lax.fori_loop(0, 4, body, 0)
        copy = pltpu.make_async_copy(grad_buf.at[which], target, store_sem.at[which])
        copy.start()
        stores.append(copy)

    for load in loads:
        load.wait()
    arrive(0, 0)
    arrive(0, 1)
    forward(0, 0)
    arrive(0, 2)
    forward(0, 1)
    compute(0)
    arrive(0, 3)
    forward(0, 2)
    compute(1)
    relay(0)
    forward(0, 3)
    compute(2)
    relay(1)
    deliver(0)
    compute(3)
    relay(2)
    turned[...] = jnp.transpose(xhat_ref[...]).astype(bf)
    deliver(1)
    weight_grad(1, active, scaled, outer_grad_hbm)
    relay(3)
    deliver(2)
    weight_grad(0, slots, pre, inner_grad_hbm)
    deliver(3)
    def returned(kind):
        view = sized.at[pl.ds(0, 63), :, pl.ds(0, 1024)]
        remote(view, view, back_s.at[kind], back_r.at[kind], to_right).wait()
        selfs[2 + kind].wait()

    returned(0)

    def output(n, carry):
        cols = columns_of(n, 256)
        og = og_ref[:, cols].astype(f32)
        total = jnp.zeros((128, 256), f32)
        sums = []
        for k in (0, 1):
            picked = jnp.dot(spots[k], y_ref[:, cols], preferred_element_type=f32)
            total = total + weights[k] * picked
            sums.append(carry[k] + jnp.sum(og * picked, axis=1, keepdims=True))
        layer_ref[:, cols] = (mixed_ref[:, cols].astype(f32) + total).astype(bf)
        return tuple(sums)

    start = jnp.zeros((128, 1), f32)
    weight_sums = lax.fori_loop(0, 4, output, (start, start))
    mean_term = weight_sums[0] * weights[0] + weight_sums[1] * weights[1]
    logit_grad = jnp.zeros((128, 128), f32)
    for k in (0, 1):
        chosen = (weight_sums[k] - mean_term) / score_sum * scores[k] * (1.0 - scores[k])
        logit_grad = jnp.where(picks[k], chosen, logit_grad)
    logit_grad = logit_grad.astype(bf)
    across = (((1,), (1,)), ((), ()))

    def mix(n, carry):
        cols = columns_of(n, 256)
        grad = og_ref[:, cols].astype(f32) + jnp.dot(both, z_ref[:, cols], preferred_element_type=f32)
        grad = grad + lax.dot_general(logit_grad, full_ref[n, :, 2048:2176], across, preferred_element_type=f32)
        mg_buf[:, cols] = grad
        cg_buf[16:144, cols] = grad * mask * swish_slope(conv_ref[:, cols])
        return carry

    returned(1)
    lax.fori_loop(0, 4, mix, 0)

    def depth_back(n, carry):
        cols = columns_of(n, 128)
        grad = cg_buf[16:144, cols]
        total = jnp.zeros((128, 128), f32)
        for k in range(KERNEL):
            total = total + taps_ref[64 + k : 65 + k, cols] * cg_buf[31 - k : 159 - k, cols]
            tg_buf[64 + k : 65 + k, cols] = jnp.sum(grad * gated_ref[k + 1 : k + 129, cols], axis=0, keepdims=True)
        total = total * mask
        sig = sig_ref[:, cols]
        pc_buf[:, cols] = (total * sig).astype(bf)
        pc_buf[:, columns_of(n + 8, 128)] = (total * value_ref[:, cols] * sig * (1.0 - sig)).astype(bf)
        return carry

    lax.fori_loop(0, 8, depth_back, 0)
    out = lax.dot_general(mixed_ref[...], logit_grad, down, preferred_element_type=f32)
    out = out + lax.dot_general(tg_buf[...].astype(bf), identity(), down, preferred_element_type=f32)
    part_ref[:, :, 2048:2176] = out.astype(bf).reshape(4, 256, 128)

    def outer_product(i, carry):
        cols = columns_of((i + 9 * (1 - c)) % 16, 128)
        out = jnp.dot(turned[...], pc_buf[:, cols], preferred_element_type=f32)
        part_ref[:, :, cols] = out.astype(bf).reshape(4, 256, 128)
        return carry

    lax.fori_loop(0, 9, outer_product, 0)
    colours = ((0, SPLIT), (SPLIT, HALF - SPLIT))
    order = (2, 1, 3, 0)

    def rows_of(colour, index):
        if colour == 0:
            return index, pl.ds(0, 256)
        return slice(None), pl.ds(pl.multiple_of(index * 64, 64), 64)

    swaps = {}
    for step in order:
        for colour, (begin, width) in enumerate(colours):
            at = ((x if colour == 0 else y) + step) % 4
            lead, rows = rows_of(colour, at)
            slot = colour * 4 + step
            copy = remote(
                part_ref.at[lead, rows, pl.ds(pl.multiple_of(other + begin, 128), width)],
                swap_buf.at[lead, rows, pl.ds(begin, width)],
                swap_s.at[slot],
                swap_r.at[slot],
                partner,
            )
            copy.start()
            swaps[colour, step] = copy

    lax.fori_loop(9, 16, outer_product, 0)

    def inward(n, carry):
        cols = columns_of(n, 256)
        out = lax.dot_general(pc_buf[...], full_ref[n, :, 0:2048], across, preferred_element_type=f32)
        ng_buf[:, cols] = out
        first = carry[0] + jnp.sum(out, axis=1, keepdims=True)
        second = carry[1] + jnp.sum(out * xhat_ref[:, cols], axis=1, keepdims=True)
        return first, second

    def finish_frames():
        first, second = lax.fori_loop(0, 4, inward, (start, start))
        first, second = first * (1.0 / 1024), second * (1.0 / 1024)

        def finish(n, carry):
            cols = columns_of(n, 256)
            grad = inv_scale * (ng_buf[:, cols] - first - xhat_ref[:, cols] * second)
            frames_grad_ref[:, cols] = (mg_buf[:, cols] + grad).astype(bf)
            return carry

        lax.fori_loop(0, 4, finish, 0)

    def first_to(colour, step):
        if colour == 0:
            return spot((x + step) % 4, y, z, c)
        return spot(x, (y + step) % 4, z, c)

    def second_to(colour, step):
        return first_to(1 - colour, step)

    def fold(colour, step, extra):
        begin, width = colours[colour]
        at = ((x if colour == 0 else y) + step) % 4
        swaps[colour, step].wait_recv()

        def body(t, carry):
            if colour == 0:
                lead, row = at, pl.multiple_of(t * 32, 32)
            else:
                lead, row = t // 2, pl.multiple_of(at * 64 + (t % 2) * 32, 32)
            value = part_ref[lead, pl.ds(row, 32), pl.ds(pl.multiple_of(mine + begin, 128), width)].astype(jnp.float32)
            value = value + swap_buf[lead, pl.ds(row, 32), pl.ds(begin, width)].astype(jnp.float32)
            value = extra(t, value)
            half_buf[colour, step, pl.ds(pl.multiple_of(t * 32, 32), 32), pl.ds(0, width)] = value.astype(jnp.bfloat16)
            return carry

        return body

    plain = lambda t, value: value
    sent = []
    pend = {}
    for colour, (begin, width) in enumerate(colours):
        lax.fori_loop(0, 8, fold(colour, 2, plain), 0)
        for side, step in ((0, 1), (1, 3)):
            slot = colour * 12 + side
            copy = remote(
                half_buf.at[colour, 2, pl.ds(side * 128, 128), pl.ds(0, width)],
                far_buf.at[colour, side, :, pl.ds(0, width)],
                rring_s.at[slot],
                rring_r.at[slot],
                first_to(colour, step),
            )
            copy.start()
            pend[colour, side] = copy
            sent.append(copy)
    for colour, (begin, width) in enumerate(colours):
        for side, step in ((0, 1), (1, 3)):
            lax.fori_loop(4 - 4 * side, 8 - 4 * side, fold(colour, step, plain), 0)
            slot = colour * 12 + 8 + side
            rows = pl.ds(128 - 128 * side, 128)
            copy = remote(
                half_buf.at[colour, step, rows, pl.ds(0, width)],
                near_buf.at[colour, side, rows, pl.ds(0, width)],
                rring_s.at[slot],
                rring_r.at[slot],
                first_to(colour, step),
            )
            copy.start()
            pend[colour, 8 + side] = copy
            sent.append(copy)
    finish_frames()
    for colour, (begin, width) in enumerate(colours):
        for side, step in ((0, 1), (1, 3)):
            lo = side * 4
            pend[colour, side].wait_recv()

            def extra(t, value, colour=colour, side=side, lo=lo, width=width):
                row = pl.multiple_of((t - lo) * 32, 32)
                return value + far_buf[colour, side, pl.ds(row, 32), pl.ds(0, width)].astype(jnp.float32)

            def again(t, carry, colour=colour, step=step, extra=extra, begin=begin, width=width):
                at = ((x if colour == 0 else y) + step) % 4
                if colour == 0:
                    lead, row = at, pl.multiple_of(t * 32, 32)
                else:
                    lead, row = t // 2, pl.multiple_of(at * 64 + (t % 2) * 32, 32)
                value = part_ref[lead, pl.ds(row, 32), pl.ds(pl.multiple_of(mine + begin, 128), width)].astype(jnp.float32)
                value = value + swap_buf[lead, pl.ds(row, 32), pl.ds(begin, width)].astype(jnp.float32)
                value = extra(t, value)
                half_buf[colour, step, pl.ds(pl.multiple_of(t * 32, 32), 32), pl.ds(0, width)] = value.astype(jnp.bfloat16)
                return carry

            lax.fori_loop(lo, lo + 4, again, 0)
            slot = colour * 12 + 2 + side
            copy = remote(
                half_buf.at[colour, step, pl.ds(128 * side, 128), pl.ds(0, width)],
                near_buf.at[colour, side, pl.ds(128 * side, 128), pl.ds(0, width)],
                rring_s.at[slot],
                rring_r.at[slot],
                first_to(colour, step),
            )
            copy.start()
            pend[colour, 2 + side] = copy
            sent.append(copy)
    for colour, (begin, width) in enumerate(colours):
        for name in (8, 9, 2, 3):
            pend[colour, name].wait_recv()

        def extra(t, value, colour=colour, width=width):
            row = pl.multiple_of(t * 32, 32)
            for side in (0, 1):
                value = value + near_buf[colour, side, pl.ds(row, 32), pl.ds(0, width)].astype(jnp.float32)
            return value

        body = fold(colour, 0, extra)
        lax.fori_loop(0, 8, body, 0)
        at = y if colour == 0 else x
        for side, step in ((0, 1), (1, 3)):
            row = pl.multiple_of(((at + 2) % 4) * 64 + side * 32, 32)
            slot = colour * 12 + 4 + side
            copy = remote(
                half_buf.at[colour, 0, pl.ds(row, 32), pl.ds(0, width)],
                mid_far.at[colour, side, :, pl.ds(0, width)],
                rring_s.at[slot],
                rring_r.at[slot],
                second_to(colour, step),
            )
            copy.start()
            pend[colour, 4 + side] = copy
            sent.append(copy)
        for side, step in ((0, 1), (1, 3)):
            row = pl.multiple_of(((at + step) % 4) * 64 + 32 - 32 * side, 32)
            slot = colour * 12 + 10 + side
            copy = remote(
                half_buf.at[colour, 0, pl.ds(row, 32), pl.ds(0, width)],
                mid_near.at[colour, side, pl.ds(32 - 32 * side, 32), pl.ds(0, width)],
                rring_s.at[slot],
                rring_r.at[slot],
                second_to(colour, step),
            )
            copy.start()
            pend[colour, 10 + side] = copy
            sent.append(copy)
    for colour, (begin, width) in enumerate(colours):
        at = y if colour == 0 else x
        for side, step in ((0, 1), (1, 3)):
            row = pl.multiple_of(((at + step) % 4) * 64 + 32 * side, 32)
            pend[colour, 4 + side].wait_recv()
            value = half_buf[colour, 0, pl.ds(row, 32), pl.ds(0, width)].astype(f32)
            value = value + mid_far[colour, side, :, pl.ds(0, width)].astype(f32)
            mid_buf[colour, side, pl.ds(32 * side, 32), pl.ds(0, width)] = value.astype(bf)
            slot = colour * 12 + 6 + side
            copy = remote(
                mid_buf.at[colour, side, pl.ds(32 * side, 32), pl.ds(0, width)],
                mid_near.at[colour, side, pl.ds(32 * side, 32), pl.ds(0, width)],
                rring_s.at[slot],
                rring_r.at[slot],
                second_to(colour, step),
            )
            copy.start()
            pend[colour, 6 + side] = copy
            sent.append(copy)
    for colour, (begin, width) in enumerate(colours):
        at = y if colour == 0 else x
        for name in (10, 11, 6, 7):
            pend[colour, name].wait_recv()
        for piece in range(2):
            rows = pl.ds(piece * 32, 32)
            value = half_buf[colour, 0, pl.ds(pl.multiple_of(at * 64 + piece * 32, 32), 32), pl.ds(0, width)].astype(jnp.float32)
            for side in (0, 1):
                value = value + mid_near[colour, side, rows, pl.ds(0, width)].astype(jnp.float32)
            z_src[pl.ds(piece * 4, 4), :, pl.ds(begin, width)] = value.astype(jnp.bfloat16).reshape(4, 8, width)
    z_copies = []
    for dz in (4, 3, 5, 2, 6, 1, 7):
        to = (z + dz) % 8
        copy = remote(z_src.at[to], z_buf.at[dz - 1], rz_s.at[dz - 1], rz_r.at[dz - 1], spot(x, y, to, c))
        copy.start()
        z_copies.append(copy)
    total = z_src[z].astype(jnp.float32)
    for copy in z_copies:
        copy.wait_recv()
    for k in range(7):
        total = total + z_buf[k].astype(jnp.float32)
    last_src[...] = total
    last = remote(last_src, last_buf, last_s, last_r, partner)
    last.start()
    for copy in sent + z_copies:
        copy.wait_send()
    for copy in swaps.values():
        copy.wait_send()
    kept = jnp.where(c == 0, last_src[0:4, :], last_src[4:8, :])
    last.wait()
    got = jnp.where(c == 0, last_buf[0:4, :], last_buf[4:8, :])
    low, high = jnp.where(c == 0, kept, got), jnp.where(c == 0, got, kept)
    out_ref[:, 0:HALF] = low
    out_ref[:, HALF:2048] = high[:, 0 : 2048 - HALF]
    router_grad_ref[...] = high[:, 2048 - HALF : 2112 - HALF]
    depth_ref[...] = high[:, 2112 - HALF : 2112 + KERNEL - HALF]
    for kind in (0, 1):
        for q in range(4):
            view = bulk(kind, q)
            remote(view, view, there_s.at[kind, q], there_r.at[kind, q], to_right).wait_send()
    for copy in list(rings.values()) + list(folds.values()):
        copy.wait_send()
    for copy in stores:
        copy.wait()


def layer(frames, lengths, ids, og, conv_in, router, depthwise, inner, outer):
    dma, bf, f32 = pltpu.SemaphoreType.DMA, jnp.bfloat16, jnp.float32
    block = lambda *lead: pltpu.VMEM(lead + (64, 1024), bf)
    shape = lambda *args: jax.ShapeDtypeStruct(*args)
    vmem, anywhere = pl.BlockSpec(memory_space=pltpu.VMEM), pl.BlockSpec(memory_space=pl.ANY)
    wide = pltpu.VMEM((128, 1024), f32)
    long = pltpu.VMEM((160, 1024), f32)
    half = lambda *lead: pltpu.VMEM(lead + (SPLIT,), bf)
    return pl.pallas_call(
        layer_kernel,
        out_shape=(
            shape((128, 1024), bf), shape((128, 1024), bf), shape((4, 2048), f32), shape((4, KERNEL), f32),
            shape((4, 64), f32), shape((1024, 1024), bf), shape((1024, 1024), bf),
        ),
        in_specs=[vmem, pl.BlockSpec(memory_space=pltpu.SMEM)] + [vmem] * 5 + [anywhere] * 2,
        out_specs=(vmem,) * 5 + (anywhere,) * 2,
        scratch_shapes=[
            pltpu.VMEM((4, 256, WIDE), bf), pltpu.VMEM((128, 1024), bf), wide, wide, wide, wide, long, wide,
            pltpu.VMEM((256, 1024), bf), pltpu.VMEM((256, 1024), bf),
            pltpu.VMEM((4, WIDE), bf), pltpu.VMEM((256, TALL), bf), pltpu.VMEM((256, 1024), bf),
            pltpu.VMEM((4, 4, 64, TALL), bf),
        ]
        + [block(4, 4)] * 4
        + [pltpu.VMEM((1024, 1024), bf)] * 2
        + [block(4, 4)] * 2
        + [block(4)] * 6
        + [pltpu.VMEM((2, 1024, 1024), bf), pltpu.VMEM((63, 4, TALL), bf)]
        + [wide, long, wide, pltpu.VMEM((128, 2048), bf), pltpu.VMEM((1024, 128), bf), wide]
        + [
            pltpu.VMEM((4, 256, WIDE), bf), pltpu.VMEM((4, 256, HALF), bf), half(2, 4, 256), half(2, 2, 128),
            half(2, 2, 256), half(2, 2, 64), half(2, 2, 32), half(2, 2, 64), pltpu.VMEM((8, 8, HALF), bf),
            pltpu.VMEM((7, 8, HALF), bf), pltpu.VMEM((8, HALF), f32), pltpu.VMEM((8, HALF), f32),
        ]
        + [
            dma((2,)), dma, dma, dma, dma((7,)), dma((7,)), dma((16,)), dma((16,)), dma((8,)), dma((8,)),
            dma((4,)), dma((2, 4)), dma((2, 4)), dma((2, 4, 4)), dma((2, 4, 4)), dma((6, 4)), dma((6, 4)), dma((2,)),
            dma((2,)), dma((2,)), dma((8,)), dma((8,)), dma((24,)), dma((24,)), dma((7,)), dma((7,)), dma, dma,
        ],
        compiler_params=pltpu.CompilerParams(
            collective_id=2, has_side_effects=True, vmem_limit_bytes=VMEM_LIMIT
        ),
        name="layer",
    )(frames, lengths, ids, og, conv_in, router, depthwise, inner, outer)


def pass_kernel(*refs):
    sources, targets, bufs, sems = refs[:7], refs[7:14], refs[14:21], refs[21]
    loads, stores = [], []
    for i in range(7):
        for part in range(4 if i >= 5 else 1):
            pick = (lambda ref: ref) if i < 5 else (lambda ref: ref.at[pl.ds(part * 256, 256)])
            at = len(loads)
            loads.append(pltpu.make_async_copy(pick(sources[i]), pick(bufs[i]), sems.at[0, at]))
            stores.append(pltpu.make_async_copy(pick(bufs[i]), pick(targets[i]), sems.at[1, at]))
    order = list(range(5, 13)) + list(range(5))
    for at in order:
        loads[at].start()
    for at in order:
        loads[at].wait()
        stores[at].start()
    for at in order:
        stores[at].wait()


def pass_on(values):
    shapes = tuple(jax.ShapeDtypeStruct(value.shape, value.dtype) for value in values)
    anywhere = pl.BlockSpec(memory_space=pl.ANY)
    return pl.pallas_call(
        pass_kernel,
        out_shape=shapes,
        in_specs=[anywhere] * 7,
        out_specs=(anywhere,) * 7,
        scratch_shapes=[pltpu.VMEM(value.shape, value.dtype) for value in values] + [pltpu.SemaphoreType.DMA((2, 13))],
        compiler_params=pltpu.CompilerParams(vmem_limit_bytes=VMEM_LIMIT),
        name="pass_on",
    )(*values)


def per_device(frames, lengths, expert_ids, conv_in, depthwise, router, w_in, w_out, out_grad):
    *outs, w_in_grad, w_out_grad = pass_on(
        layer(frames, lengths, expert_ids.T, out_grad, conv_in, router, depthwise, w_in[0], w_out[0])
    )
    return (*outs, w_in_grad[None], w_out_grad[None])


def solution(mesh):
    in_specs = (
        P(("dp", "expert"), None),
        P(("dp", "expert")),
        P(("dp", "expert"), None),
        P(("dp", "expert"), None),
        P(("dp", "expert"), None),
        P(("dp", "expert"), None),
        P("expert", None, "dp"),
        P("expert", "dp", None),
        P(("dp", "expert"), None),
    )
    out_specs = (
        P(("dp", "expert"), None),
        P(("dp", "expert"), None),
        P(("dp", "expert"), None),
        P(("dp", "expert"), None),
        P(("dp", "expert"), None),
        P("expert", None, "dp"),
        P("expert", "dp", None),
    )
    return jax.shard_map(
        per_device, mesh=mesh, in_specs=in_specs, out_specs=out_specs, check_vma=False
    )
```

```python
import jax
import jax.numpy as jnp
from jax import lax
from jax.experimental import pallas as pl
from jax.experimental.pallas import tpu as pltpu
from jax.sharding import PartitionSpec as P

KERNEL = 31
EPSILON = 1e-05


def swish_of(values):
    return values * jax.nn.sigmoid(values)


def swish_slope(values):
    sigmoid_v = jax.nn.sigmoid(values)
    return sigmoid_v * (1.0 + values * (1.0 - sigmoid_v))


def normalize(values):
    center = values - jnp.mean(values, axis=-1, keepdims=True)
    inv_scale = lax.rsqrt(jnp.mean(center * center, axis=-1, keepdims=True) + EPSILON)
    return (center * inv_scale, inv_scale)


MESH = pl.DeviceIdType.MESH
HALF = 1152
WIDE = 2 * HALF
SPLIT = 640
VMEM_LIMIT = 60 * 1024 * 1024


def place():
    x = lax.axis_index("dp")
    e = lax.axis_index("expert")
    return x, e // 16, (e // 2) % 8, e % 2


def spot(x, y, z, c):
    return (x, y * 16 + z * 2 + c)


def remote(src, dst, send, recv, where):
    return pltpu.make_async_remote_copy(
        src_ref=src, dst_ref=dst, send_sem=send, recv_sem=recv, device_id=where, device_id_type=MESH
    )


STEPS = (0, 1, 3, 2)
TALL = 1152


def columns_of(n, width):
    return pl.ds(pl.multiple_of(n * width, width), width)


def mask_of(length_ref):
    return (lax.broadcasted_iota(jnp.int32, (128, 1), 0) < length_ref[0]).astype(jnp.float32)


def index_columns(ids_ref):
    shape = (128, 128)
    diagonal = lax.broadcasted_iota(jnp.int32, shape, 0) == lax.broadcasted_iota(jnp.int32, shape, 1)
    rows = ids_ref[...].astype(jnp.float32)
    return [jnp.sum(jnp.where(diagonal, rows[k : k + 1, :], 0.0), axis=1, keepdims=True) for k in (0, 1)]


def identity():
    shape = (128, 128)
    return (lax.broadcasted_iota(jnp.int32, shape, 0) == lax.broadcasted_iota(jnp.int32, shape, 1)).astype(jnp.bfloat16)


def layer_kernel(
    frames_ref, length_ref, ids_ref, og_ref, conv_in_ref, router_ref, depthwise_ref, inner_hbm, outer_hbm,
    layer_ref, frames_grad_ref, out_ref, depth_ref, router_grad_ref, inner_grad_hbm, outer_grad_hbm,
    full_ref, mixed_ref, value_ref, sig_ref, conv_ref, xhat_ref, gated_ref, taps_ref, y_ref, z_ref,
    own_ref, rows_buf, og_rows, slots, cots, scaled, active, pre, inner, outer, part_y, part_z, straight_y, straight_z,
    relay_y, relay_z, joint_y, joint_z, grad_buf, sized, mg_buf, cg_buf, tg_buf, pc_buf, turned, ng_buf,
    part_ref, swap_buf, half_buf, far_buf, near_buf, mid_buf, mid_far, mid_near, z_src, z_buf,
    slope_buf, load_sem, own_sem, z_s, z_r, gring_s, gring_r, tail_s, tail_r, self_s, there_s, there_r, ring_s,
    ring_r, fold_s, fold_r, back_s, back_r, store_sem, swap_s, swap_r, rring_s, rring_r, rz_s, rz_r
):
    x, y, z, c = place()
    f32, bf = jnp.float32, jnp.bfloat16
    here = y * 16 + z * 2 + c
    right, left, far = (x + 1) % 4, (x + 3) % 4, (x + 2) % 4
    to_right, to_left = spot(right, y, z, c), spot(left, y, z, c)
    loads = [
        pltpu.make_async_copy(inner_hbm, inner, load_sem.at[0]),
        pltpu.make_async_copy(outer_hbm, outer, load_sem.at[1]),
    ]
    for load in loads:
        load.start()

    barrier = pltpu.get_barrier_semaphore()

    def hail(i, carry):
        pl.semaphore_signal(barrier, inc=1, device_id=(x, (here + i) % 64), device_id_type=MESH)
        return carry

    lax.fori_loop(1, 64, hail, 0)
    for where in (to_right, to_left):
        pl.semaphore_signal(barrier, inc=1, device_id=where, device_id_type=MESH)

    own_ref[:, 0:2048] = conv_in_ref[...]
    own_ref[:, 2048:WIDE] = jnp.concatenate(
        [router_ref[...].astype(f32), depthwise_ref[...].astype(f32), jnp.zeros((4, WIDE - 2112 - KERNEL), f32)], axis=1
    ).astype(bf)
    mask = mask_of(length_ref)
    index = index_columns(ids_ref)
    lanes = lax.broadcasted_iota(jnp.int32, (128, 128), 1).astype(f32)
    picks = [lanes == column for column in index]
    count = (jnp.where(picks[0] | picks[1], 1.0, 0.0) * mask).astype(bf)
    shape = (128, 128)
    below = (lax.broadcasted_iota(jnp.int32, shape, 1) < lax.broadcasted_iota(jnp.int32, shape, 0)).astype(bf)
    before = jnp.dot(below, count, preferred_element_type=f32)
    wide = lax.broadcasted_iota(jnp.int32, (128, 256), 1).astype(f32)
    slot_of, spots = [], []
    for k, pick in enumerate(picks):
        position = jnp.sum(jnp.where(pick, before, 0.0), axis=1, keepdims=True)
        kept = (position < 4.0) & (mask > 0.0)
        slot = jnp.where(kept, index[k] * 4.0 + position, -1.0)
        slot_of.append(slot)
        spots.append((wide == slot).astype(bf))
    both = spots[0] + spots[1]
    down = (((0,), (0,)), ((), ()))

    def fill_og(n, carry):
        cols = columns_of(n, 256)
        og_rows[:, cols] = lax.dot_general(both, og_ref[:, cols], down, preferred_element_type=f32).astype(bf)
        return carry

    lax.fori_loop(0, 4, fill_og, 0)
    pl.semaphore_wait(barrier, 65)

    own4 = pl.multiple_of(4 * here, 4)
    line4 = pl.multiple_of(8 * z + 4 * c, 4)
    kinds = ((rows_buf, slots, TALL), (og_rows, cots, 1024))
    selfs = {}
    rings = {}

    def source_y(q):
        return (y + STEPS[q]) % 4

    def depart(kind, q):
        source, target, _ = kinds[kind]
        dy = STEPS[q]
        yt = (y + 4 - dy) % 4

        def there(i, carry):
            zt, ct = (z + 4 + i // 2) % 8, (c + i) % 2
            et = yt * 16 + zt * 2 + ct
            rows = pl.ds(pl.multiple_of(4 * et, 4), 4)
            remote(
                source.at[rows], target.at[x, y, pl.ds(line4, 4)], there_s.at[kind, q], there_r.at[kind, q], (x, et)
            ).start()
            return carry

        if dy == 0:
            lax.fori_loop(0, 8, there, 0)
            lax.fori_loop(9, 16, there, 0)
            selfs[kind] = pltpu.make_async_copy(
                source.at[pl.ds(own4, 4)], target.at[x, y, pl.ds(line4, 4)], self_s.at[kind]
            )
            selfs[kind].start()
        else:
            lax.fori_loop(0, 16, there, 0)

    def bulk(kind, q):
        return sized.at[pl.ds(0, 15 if STEPS[q] == 0 else 16), :, pl.ds(0, kinds[kind][2])]

    def arrive(kind, q):
        if STEPS[q] == 0:
            selfs[kind].wait()
        view = bulk(kind, q)
        remote(view, view, there_s.at[kind, q], there_r.at[kind, q], to_right).wait_recv()
        block = kinds[kind][1].at[x, source_y(q)]
        for side, where in ((0, to_right), (1, to_left)):
            copy = remote(block, block, ring_s.at[kind, side, q], ring_r.at[kind, side, q], where)
            copy.start()
            rings[kind, side, q] = copy

    def forward(kind, q):
        for side, at, where in ((0, left, to_right), (1, right, to_left)):
            rings[kind, side, q].wait_recv()
            block = kinds[kind][1].at[at, source_y(q), pl.ds(32 * side, 32)]
            copy = remote(block, block, ring_s.at[kind, 2 + side, q], ring_r.at[kind, 2 + side, q], where)
            copy.start()
            rings[kind, 2 + side, q] = copy

    partner = spot(x, y, z, 1 - c)
    mine = pl.multiple_of(c * HALF, 128)
    other = pl.multiple_of((1 - c) * HALF, 128)
    row = pl.multiple_of(y * 64 + z * 8, 8)
    row4 = pl.multiple_of(row + 4 * c, 4)
    keep = pltpu.make_async_copy(
        own_ref.at[:, pl.ds(mine, HALF)], full_ref.at[x, pl.ds(row4, 4), pl.ds(mine, HALF)], own_sem
    )
    keep.start()
    copies = []
    for dz in (4, 3, 5, 2, 6, 1, 7, 0):
        for dc, begin in ((0, mine), (1, other)):
            if dz or dc:
                at = 2 * dz + dc
                copy = remote(
                    own_ref.at[:, pl.ds(begin, HALF)],
                    full_ref.at[x, pl.ds(row4, 4), pl.ds(begin, HALF)],
                    z_s.at[at],
                    z_r.at[at],
                    spot(x, y, (z + dz) % 8, (c + dc) % 2),
                )
                copy.start()
                copies.append(copy)
    depart(1, 0)
    keep.wait()
    depart(1, 1)
    xhat, inv_scale = normalize(frames_ref[...].astype(f32))
    xhat_ref[...] = xhat
    zeros = jnp.zeros((16, 1024), f32)
    gated_ref[0:16, :] = zeros
    gated_ref[144:160, :] = zeros
    cg_buf[0:16, :] = zeros
    cg_buf[144:160, :] = zeros
    tg_buf[...] = jnp.zeros((128, 1024), f32)
    part_ref[:, :, 2176:2304] = jnp.zeros((4, 256, 128), bf)
    for copy in copies:
        copy.wait()

    first = pl.multiple_of(mine, 128)
    second = pl.multiple_of(mine + SPLIT, 128)
    yrow = pl.multiple_of(y * 64, 64)

    def block_of(colour, level, index, part):
        cols = pl.ds(first, SPLIT) if colour == 0 else pl.ds(second, HALF - SPLIT)
        if level == 0:
            height = 64 if part is None else 32
            offset = 0 if part is None else part * 32
            if colour == 0:
                return full_ref.at[x, pl.ds(pl.multiple_of(index * 64 + offset, 32), height), cols]
            return full_ref.at[index, pl.ds(pl.multiple_of(yrow + offset, 32), height), cols]
        if colour == 0:
            height = 256 if part is None else 128
            offset = 0 if part is None else part * 128
            return full_ref.at[index, pl.ds(offset, height), cols]
        height = 64 if part is None else 32
        offset = 0 if part is None else part * 32
        return full_ref.at[:, pl.ds(pl.multiple_of(index * 64 + offset, 32), height), cols]

    def whereto(colour, level, step):
        if (colour + level) % 2 == 0:
            return spot(x, (y + step) % 4, z, c)
        return spot((x + step) % 4, y, z, c)

    def position(colour, level):
        return y if (colour + level) % 2 == 0 else x

    def opened(colour, level):
        at = position(colour, level)
        block = block_of(colour, level, at, None)
        base = (colour * 2 + level) * 4
        right = remote(block, block, gring_s.at[base], gring_r.at[base], whereto(colour, level, 1))
        left = remote(block, block, gring_s.at[base + 1], gring_r.at[base + 1], whereto(colour, level, 3))
        right.start()
        left.start()
        return right, left

    def passed(colour, level, pair, tell):
        at = position(colour, level)
        base = (colour * 2 + level) * 4
        right, left = pair
        right.wait_recv()
        block = block_of(colour, level, (at + 3) % 4, 0)
        on_right = remote(block, block, gring_s.at[base + 2], gring_r.at[base + 2], whereto(colour, level, 1))
        on_right.start()
        tell((at + 3) % 4, 1)
        left.wait_recv()
        block = block_of(colour, level, (at + 1) % 4, 1)
        on_left = remote(block, block, gring_s.at[base + 3], gring_r.at[base + 3], whereto(colour, level, 3))
        on_left.start()
        tell((at + 1) % 4, 2)
        return on_right, on_left

    def closed(colour, level, pair, onward, tell):
        at = position(colour, level)
        for copy in onward:
            copy.wait_recv()
        tell((at + 2) % 4, 3)
        for copy in pair + onward:
            copy.wait_send()

    silent = lambda index, slot: None
    low = [opened(colour, 0) for colour in (0, 1)]
    arrive(1, 0)
    low_on = [passed(colour, 0, low[colour], silent) for colour in (0, 1)]
    depart(1, 2)
    for colour in (0, 1):
        closed(colour, 0, low[colour], low_on[colour], silent)
    tails = []

    def teller(colour):
        def tell(index, slot):
            block = block_of(colour, 1, index, None)
            at = colour * 4 + slot
            copy = remote(block, block, tail_s.at[at], tail_r.at[at], partner)
            copy.start()
            tails.append(copy)

        return tell

    high = [opened(colour, 1) for colour in (0, 1)]
    for colour in (0, 1):
        teller(colour)(position(colour, 1), 0)
    depart(1, 3)
    arrive(1, 1)
    high_on = [passed(colour, 1, high[colour], teller(colour)) for colour in (0, 1)]
    forward(1, 0)
    for colour in (0, 1):
        closed(colour, 1, high[colour], high_on[colour], teller(colour))
    arrive(1, 2)
    for copy in tails:
        copy.wait()
    forward(1, 1)
    arrive(1, 3)

    normed = xhat_ref[...].astype(bf)

    def point(n, carry):
        cols = columns_of(n, 256)
        value = jnp.dot(normed, full_ref[:, :, cols].reshape(1024, 256), preferred_element_type=f32)
        gate = jnp.dot(normed, full_ref[:, :, columns_of(n + 4, 256)].reshape(1024, 256), preferred_element_type=f32)
        sig = jax.nn.sigmoid(gate)
        value_ref[:, cols] = value
        sig_ref[:, cols] = sig
        gated_ref[16:144, cols] = value * sig * mask
        return carry

    lax.fori_loop(0, 4, point, 0)
    small = full_ref[:, :, 2048:2176].reshape(1024, 128)
    taps_ref[...] = lax.dot_general(identity(), small, (((1,), (1,)), ((), ())), preferred_element_type=f32)
    forward(1, 2)

    def depth(n, carry):
        cols = columns_of(n, 128)
        total = jnp.zeros((128, 128), f32)
        for k in range(KERNEL):
            total = total + taps_ref[64 + k : 65 + k, cols] * gated_ref[k + 1 : k + 129, cols]
        conv_ref[:, cols] = total
        mixed_ref[:, cols] = (frames_ref[:, cols].astype(f32) + swish_of(total) * mask).astype(bf)
        return carry

    lax.fori_loop(0, 8, depth, 0)
    logits = jnp.dot(mixed_ref[...], small, preferred_element_type=f32)
    scores = [jax.nn.sigmoid(jnp.sum(jnp.where(pick, logits, 0.0), axis=1, keepdims=True)) for pick in picks]
    score_sum = scores[0] + scores[1]
    weights = [score / score_sum for score in scores]
    lane = lax.broadcasted_iota(jnp.int32, shape, 1)
    def fill(n, carry):
        cols = columns_of(n, 256)
        rows_buf[:, cols] = lax.dot_general(both, mixed_ref[:, cols], down, preferred_element_type=f32).astype(bf)
        return carry

    lax.fori_loop(0, 4, fill, 0)
    total = jnp.zeros((256, 128), f32)
    for k in (0, 1):
        upper = weights[k].astype(bf).astype(f32)
        parts = jnp.where(lane == 0, upper, jnp.where(lane == 1, weights[k] - upper, 0.0)).astype(bf)
        total = total + lax.dot_general(spots[k], parts, down, preferred_element_type=f32)
    rows_buf[:, 1024:TALL] = total.astype(bf)
    for q in range(4):
        depart(0, q)
    forward(1, 3)

    folds = {}

    def push(name, q, source, target, where):
        copy = remote(source, target, fold_s.at[name, q], fold_r.at[name, q], where)
        copy.start()
        folds[name, q] = copy

    def compute(q):
        ys = source_y(q)
        for kind in (1, 0):
            for side in (2, 3):
                rings[kind, side, q].wait_recv()

        def scale(n, carry):
            parts = slots[n, ys, :, 1024:TALL].astype(f32)
            weight = parts[:, 0:1] + parts[:, 1:2]
            scaled[n, ys] = (cots[n, ys].astype(f32) * weight).astype(bf)
            return carry

        def hide(n, carry):
            cols = columns_of(n, 256)
            hidden = jnp.dot(slots[:, ys, :, 0:1024].reshape(256, 1024), inner[:, cols], preferred_element_type=f32)
            sig = jax.nn.sigmoid(hidden)
            active[:, ys, :, cols] = (hidden * sig).astype(bf).reshape(4, 64, 256)
            slope_buf[:, cols] = sig * (1.0 + hidden * (1.0 - sig))
            return carry

        lax.fori_loop(0, 4, hide, 0)

        def outward(n, carry):
            cols = columns_of(n, 256)
            out = jnp.dot(active[:, ys].reshape(256, 1024), outer[:, cols], preferred_element_type=f32)
            part_y[q, :, :, cols] = out.astype(bf).reshape(4, 64, 256)
            return carry

        lax.fori_loop(0, 4, outward, 0)
        push(2, q, part_y.at[q, far], relay_y.at[q], to_right)
        push(1, q, part_y.at[q, left], straight_y.at[q], to_left)
        lax.fori_loop(0, 4, scale, 0)

        def hide_back(n, carry):
            cols = columns_of(n, 256)
            act_grad = lax.dot_general(
                scaled[:, ys].reshape(256, 1024), outer[cols, :], (((1,), (1,)), ((), ())), preferred_element_type=f32
            )
            pre[:, ys, :, cols] = (act_grad * slope_buf[:, cols]).astype(bf).reshape(4, 64, 256)
            return carry

        lax.fori_loop(0, 4, hide_back, 0)

        def outward_back(n, carry):
            cols = columns_of(n, 256)
            out = lax.dot_general(
                pre[:, ys].reshape(256, 1024), inner[cols, :], (((1,), (1,)), ((), ())), preferred_element_type=f32
            )
            part_z[q, :, :, cols] = out.astype(bf).reshape(4, 64, 256)
            return carry

        lax.fori_loop(0, 4, outward_back, 0)
        push(3, q, part_z.at[q, far], relay_z.at[q], to_left)
        push(0, q, part_z.at[q, right], straight_z.at[q], to_right)

    def relay(q):
        folds[2, q].wait_recv()
        part_y[q, right] = (part_y[q, right].astype(f32) + relay_y[q].astype(f32)).astype(bf)
        push(4, q, part_y.at[q, right], joint_y.at[q], to_right)
        folds[3, q].wait_recv()
        part_z[q, left] = (part_z[q, left].astype(f32) + relay_z[q].astype(f32)).astype(bf)
        push(5, q, part_z.at[q, left], joint_z.at[q], to_left)

    def deliver(q):
        yt = source_y(q)
        for kind, (source, target, straight, joint, names) in enumerate(
            ((part_y, y_ref, straight_y, joint_y, (1, 4)), (part_z, z_ref, straight_z, joint_z, (0, 5)))
        ):
            for name in names:
                folds[name, q].wait_recv()
            source[q, x] = (source[q, x].astype(f32) + straight[q].astype(f32) + joint[q].astype(f32)).astype(bf)

            def back(i, carry, kind=kind, source=source, target=target):
                zt, ct = (z + 4 + i // 2) % 8, (c + i) % 2
                rows = pl.ds(pl.multiple_of(8 * zt + 4 * ct, 4), 4)
                remote(
                    source.at[q, x, rows], target.at[pl.ds(own4, 4)], back_s.at[kind], back_r.at[kind], (x, yt * 16 + zt * 2 + ct)
                ).start()
                return carry

            if STEPS[q] == 0:
                lax.fori_loop(0, 8, back, 0)
                lax.fori_loop(9, 16, back, 0)
                copy = pltpu.make_async_copy(
                    source.at[q, x, pl.ds(line4, 4)], target.at[pl.ds(own4, 4)], self_s.at[2 + kind]
                )
                copy.start()
                selfs[2 + kind] = copy
            else:
                lax.fori_loop(0, 16, back, 0)

    stores = []

    def weight_grad(which, left_ref, right_ref, target):
        def body(n, carry):
            cols = pl.ds(pl.multiple_of(n * 256, 256), 256)
            out = lax.dot_general(
                left_ref[:, :, :, cols].reshape(1024, 256),
                right_ref[...].reshape(1024, 1024),
                (((0,), (0,)), ((), ())),
                preferred_element_type=f32,
            )
            grad_buf[which, cols, :] = out.astype(bf)
            return carry

        lax.fori_loop(0, 4, body, 0)
        copy = pltpu.make_async_copy(grad_buf.at[which], target, store_sem.at[which])
        copy.start()
        stores.append(copy)

    for load in loads:
        load.wait()
    arrive(0, 0)
    arrive(0, 1)
    forward(0, 0)
    arrive(0, 2)
    forward(0, 1)
    compute(0)
    arrive(0, 3)
    forward(0, 2)
    compute(1)
    relay(0)
    forward(0, 3)
    compute(2)
    relay(1)
    deliver(0)
    compute(3)
    relay(2)
    turned[...] = jnp.transpose(xhat_ref[...]).astype(bf)
    deliver(1)
    weight_grad(1, active, scaled, outer_grad_hbm)
    relay(3)
    deliver(2)
    weight_grad(0, slots, pre, inner_grad_hbm)
    deliver(3)
    def returned(kind):
        view = sized.at[pl.ds(0, 63), :, pl.ds(0, 1024)]
        remote(view, view, back_s.at[kind], back_r.at[kind], to_right).wait()
        selfs[2 + kind].wait()

    returned(0)

    def output(n, carry):
        cols = columns_of(n, 256)
        og = og_ref[:, cols].astype(f32)
        total = jnp.zeros((128, 256), f32)
        sums = []
        for k in (0, 1):
            picked = jnp.dot(spots[k], y_ref[:, cols], preferred_element_type=f32)
            total = total + weights[k] * picked
            sums.append(carry[k] + jnp.sum(og * picked, axis=1, keepdims=True))
        layer_ref[:, cols] = (mixed_ref[:, cols].astype(f32) + total).astype(bf)
        return tuple(sums)

    start = jnp.zeros((128, 1), f32)
    weight_sums = lax.fori_loop(0, 4, output, (start, start))
    mean_term = weight_sums[0] * weights[0] + weight_sums[1] * weights[1]
    logit_grad = jnp.zeros((128, 128), f32)
    for k in (0, 1):
        chosen = (weight_sums[k] - mean_term) / score_sum * scores[k] * (1.0 - scores[k])
        logit_grad = jnp.where(picks[k], chosen, logit_grad)
    logit_grad = logit_grad.astype(bf)
    across = (((1,), (1,)), ((), ()))

    def mix(n, carry):
        cols = columns_of(n, 256)
        grad = og_ref[:, cols].astype(f32) + jnp.dot(both, z_ref[:, cols], preferred_element_type=f32)
        grad = grad + lax.dot_general(logit_grad, full_ref[n, :, 2048:2176], across, preferred_element_type=f32)
        mg_buf[:, cols] = grad
        cg_buf[16:144, cols] = grad * mask * swish_slope(conv_ref[:, cols])
        return carry

    returned(1)
    lax.fori_loop(0, 4, mix, 0)

    def depth_back(n, carry):
        cols = columns_of(n, 128)
        total = jnp.zeros((128, 128), f32)
        for k in range(KERNEL):
            total = total + taps_ref[64 + k : 65 + k, cols] * cg_buf[31 - k : 159 - k, cols]
        total = total * mask
        sig = sig_ref[:, cols]
        pc_buf[:, cols] = (total * sig).astype(bf)
        pc_buf[:, columns_of(n + 8, 128)] = (total * value_ref[:, cols] * sig * (1.0 - sig)).astype(bf)
        return carry

    lax.fori_loop(0, 8, depth_back, 0)

    def depth_taps(n, carry):
        cols = columns_of(n, 128)
        grad = cg_buf[16:144, cols]
        for k in range(KERNEL):
            tg_buf[64 + k : 65 + k, cols] = jnp.sum(grad * gated_ref[k + 1 : k + 129, cols], axis=0, keepdims=True)
        return carry

    def outer_product(i, carry):
        cols = columns_of((i + 9 * (1 - c)) % 16, 128)
        out = jnp.dot(turned[...], pc_buf[:, cols], preferred_element_type=f32)
        part_ref[:, :, cols] = out.astype(bf).reshape(4, 256, 128)
        return carry

    lax.fori_loop(0, 9, outer_product, 0)
    colours = ((0, SPLIT), (SPLIT, HALF - SPLIT))
    order = (2, 1, 3, 0)

    def rows_of(colour, index):
        if colour == 0:
            return index, pl.ds(0, 256)
        return slice(None), pl.ds(pl.multiple_of(index * 64, 64), 64)

    swaps = {}

    def swap_out(colour):
        begin, width = colours[colour]
        for step in order:
            at = ((x if colour == 0 else y) + step) % 4
            lead, rows = rows_of(colour, at)
            slot = colour * 4 + step
            copy = remote(
                part_ref.at[lead, rows, pl.ds(pl.multiple_of(other + begin, 128), width)],
                swap_buf.at[lead, rows, pl.ds(begin, width)],
                swap_s.at[slot],
                swap_r.at[slot],
                partner,
            )
            copy.start()
            swaps[colour, step] = copy

    swap_out(0)
    lax.fori_loop(0, 8, depth_taps, 0)
    out = lax.dot_general(mixed_ref[...], logit_grad, down, preferred_element_type=f32)
    out = out + lax.dot_general(tg_buf[...].astype(bf), identity(), down, preferred_element_type=f32)
    part_ref[:, :, 2048:2176] = out.astype(bf).reshape(4, 256, 128)
    swap_out(1)
    lax.fori_loop(9, 16, outer_product, 0)

    def inward(n, carry):
        cols = columns_of(n, 256)
        out = lax.dot_general(pc_buf[...], full_ref[n, :, 0:2048], across, preferred_element_type=f32)
        ng_buf[:, cols] = out
        first = carry[0] + jnp.sum(out, axis=1, keepdims=True)
        second = carry[1] + jnp.sum(out * xhat_ref[:, cols], axis=1, keepdims=True)
        return first, second

    def finish_frames():
        first, second = lax.fori_loop(0, 4, inward, (start, start))
        first, second = first * (1.0 / 1024), second * (1.0 / 1024)

        def finish(n, carry):
            cols = columns_of(n, 256)
            grad = inv_scale * (ng_buf[:, cols] - first - xhat_ref[:, cols] * second)
            frames_grad_ref[:, cols] = (mg_buf[:, cols] + grad).astype(bf)
            return carry

        lax.fori_loop(0, 4, finish, 0)

    def first_to(colour, step):
        if colour == 0:
            return spot((x + step) % 4, y, z, c)
        return spot(x, (y + step) % 4, z, c)

    def second_to(colour, step):
        return first_to(1 - colour, step)

    def fold(colour, step, extra):
        begin, width = colours[colour]
        at = ((x if colour == 0 else y) + step) % 4
        swaps[colour, step].wait_recv()

        def body(t, carry):
            if colour == 0:
                lead, row = at, pl.multiple_of(t * 32, 32)
            else:
                lead, row = t // 2, pl.multiple_of(at * 64 + (t % 2) * 32, 32)
            value = part_ref[lead, pl.ds(row, 32), pl.ds(pl.multiple_of(mine + begin, 128), width)].astype(jnp.float32)
            value = value + swap_buf[lead, pl.ds(row, 32), pl.ds(begin, width)].astype(jnp.float32)
            value = extra(t, value)
            half_buf[colour, step, pl.ds(pl.multiple_of(t * 32, 32), 32), pl.ds(0, width)] = value.astype(jnp.bfloat16)
            return carry

        return body

    plain = lambda t, value: value
    sent = []
    pend = {}
    for colour, (begin, width) in enumerate(colours):
        lax.fori_loop(0, 8, fold(colour, 2, plain), 0)
        for side, step in ((0, 1), (1, 3)):
            slot = colour * 12 + side
            copy = remote(
                half_buf.at[colour, 2, pl.ds(side * 128, 128), pl.ds(0, width)],
                far_buf.at[colour, side, :, pl.ds(0, width)],
                rring_s.at[slot],
                rring_r.at[slot],
                first_to(colour, step),
            )
            copy.start()
            pend[colour, side] = copy
            sent.append(copy)
    for colour, (begin, width) in enumerate(colours):
        for side, step in ((0, 1), (1, 3)):
            lax.fori_loop(4 - 4 * side, 8 - 4 * side, fold(colour, step, plain), 0)
            slot = colour * 12 + 8 + side
            rows = pl.ds(128 - 128 * side, 128)
            copy = remote(
                half_buf.at[colour, step, rows, pl.ds(0, width)],
                near_buf.at[colour, side, rows, pl.ds(0, width)],
                rring_s.at[slot],
                rring_r.at[slot],
                first_to(colour, step),
            )
            copy.start()
            pend[colour, 8 + side] = copy
            sent.append(copy)
    finish_frames()
    for colour, (begin, width) in enumerate(colours):
        for side, step in ((0, 1), (1, 3)):
            lo = side * 4
            pend[colour, side].wait_recv()

            def extra(t, value, colour=colour, side=side, lo=lo, width=width):
                row = pl.multiple_of((t - lo) * 32, 32)
                return value + far_buf[colour, side, pl.ds(row, 32), pl.ds(0, width)].astype(jnp.float32)

            def again(t, carry, colour=colour, step=step, extra=extra, begin=begin, width=width):
                at = ((x if colour == 0 else y) + step) % 4
                if colour == 0:
                    lead, row = at, pl.multiple_of(t * 32, 32)
                else:
                    lead, row = t // 2, pl.multiple_of(at * 64 + (t % 2) * 32, 32)
                value = part_ref[lead, pl.ds(row, 32), pl.ds(pl.multiple_of(mine + begin, 128), width)].astype(jnp.float32)
                value = value + swap_buf[lead, pl.ds(row, 32), pl.ds(begin, width)].astype(jnp.float32)
                value = extra(t, value)
                half_buf[colour, step, pl.ds(pl.multiple_of(t * 32, 32), 32), pl.ds(0, width)] = value.astype(jnp.bfloat16)
                return carry

            lax.fori_loop(lo, lo + 4, again, 0)
            slot = colour * 12 + 2 + side
            copy = remote(
                half_buf.at[colour, step, pl.ds(128 * side, 128), pl.ds(0, width)],
                near_buf.at[colour, side, pl.ds(128 * side, 128), pl.ds(0, width)],
                rring_s.at[slot],
                rring_r.at[slot],
                first_to(colour, step),
            )
            copy.start()
            pend[colour, 2 + side] = copy
            sent.append(copy)
    for colour, (begin, width) in enumerate(colours):
        for name in (8, 9, 2, 3):
            pend[colour, name].wait_recv()

        def extra(t, value, colour=colour, width=width):
            row = pl.multiple_of(t * 32, 32)
            for side in (0, 1):
                value = value + near_buf[colour, side, pl.ds(row, 32), pl.ds(0, width)].astype(jnp.float32)
            return value

        body = fold(colour, 0, extra)
        lax.fori_loop(0, 8, body, 0)
        at = y if colour == 0 else x
        for side, step in ((0, 1), (1, 3)):
            row = pl.multiple_of(((at + 2) % 4) * 64 + side * 32, 32)
            slot = colour * 12 + 4 + side
            copy = remote(
                half_buf.at[colour, 0, pl.ds(row, 32), pl.ds(0, width)],
                mid_far.at[colour, side, :, pl.ds(0, width)],
                rring_s.at[slot],
                rring_r.at[slot],
                second_to(colour, step),
            )
            copy.start()
            pend[colour, 4 + side] = copy
            sent.append(copy)
        for side, step in ((0, 1), (1, 3)):
            row = pl.multiple_of(((at + step) % 4) * 64 + 32 - 32 * side, 32)
            slot = colour * 12 + 10 + side
            copy = remote(
                half_buf.at[colour, 0, pl.ds(row, 32), pl.ds(0, width)],
                mid_near.at[colour, side, pl.ds(32 - 32 * side, 32), pl.ds(0, width)],
                rring_s.at[slot],
                rring_r.at[slot],
                second_to(colour, step),
            )
            copy.start()
            pend[colour, 10 + side] = copy
            sent.append(copy)
    for colour, (begin, width) in enumerate(colours):
        at = y if colour == 0 else x
        for side, step in ((0, 1), (1, 3)):
            row = pl.multiple_of(((at + step) % 4) * 64 + 32 * side, 32)
            pend[colour, 4 + side].wait_recv()
            value = half_buf[colour, 0, pl.ds(row, 32), pl.ds(0, width)].astype(f32)
            value = value + mid_far[colour, side, :, pl.ds(0, width)].astype(f32)
            mid_buf[colour, side, pl.ds(32 * side, 32), pl.ds(0, width)] = value.astype(bf)
            slot = colour * 12 + 6 + side
            copy = remote(
                mid_buf.at[colour, side, pl.ds(32 * side, 32), pl.ds(0, width)],
                mid_near.at[colour, side, pl.ds(32 * side, 32), pl.ds(0, width)],
                rring_s.at[slot],
                rring_r.at[slot],
                second_to(colour, step),
            )
            copy.start()
            pend[colour, 6 + side] = copy
            sent.append(copy)
    for colour, (begin, width) in enumerate(colours):
        at = y if colour == 0 else x
        for name in (10, 11, 6, 7):
            pend[colour, name].wait_recv()
        for piece in range(2):
            rows = pl.ds(piece * 32, 32)
            value = half_buf[colour, 0, pl.ds(pl.multiple_of(at * 64 + piece * 32, 32), 32), pl.ds(0, width)].astype(jnp.float32)
            for side in (0, 1):
                value = value + mid_near[colour, side, rows, pl.ds(0, width)].astype(jnp.float32)
            z_src[pl.ds(piece * 4, 4), :, pl.ds(begin, width)] = value.astype(jnp.bfloat16).reshape(4, 8, width)
    z_copies = []
    for dz in (4, 3, 5, 2, 6, 1, 7, 0):
        for dc in (0, 1):
            if dz or dc:
                to, core = (z + dz) % 8, (c + dc) % 2
                at = 2 * dz + dc
                copy = remote(
                    z_src.at[to, pl.ds(pl.multiple_of(4 * core, 4), 4)], z_buf.at[at], rz_s.at[at], rz_r.at[at], spot(x, y, to, core)
                )
                copy.start()
                z_copies.append(copy)
    own8 = z_src[z].astype(f32)
    kept = jnp.where(c == 0, own8[0:4, :], own8[4:8, :])
    for copy in z_copies:
        copy.wait_recv()
    got = jnp.zeros((4, HALF), f32)
    for dz in range(8):
        if dz:
            kept = kept + z_buf[2 * dz].astype(f32)
        got = got + z_buf[2 * dz + 1].astype(f32)
    for copy in sent + z_copies:
        copy.wait_send()
    for copy in swaps.values():
        copy.wait_send()
    low, high = jnp.where(c == 0, kept, got), jnp.where(c == 0, got, kept)
    out_ref[:, 0:HALF] = low
    out_ref[:, HALF:2048] = high[:, 0 : 2048 - HALF]
    router_grad_ref[...] = high[:, 2048 - HALF : 2112 - HALF]
    depth_ref[...] = high[:, 2112 - HALF : 2112 + KERNEL - HALF]
    for kind in (0, 1):
        for q in range(4):
            view = bulk(kind, q)
            remote(view, view, there_s.at[kind, q], there_r.at[kind, q], to_right).wait_send()
    for copy in list(rings.values()) + list(folds.values()):
        copy.wait_send()
    for copy in stores:
        copy.wait()


def layer(frames, lengths, ids, og, conv_in, router, depthwise, inner, outer):
    dma, bf, f32 = pltpu.SemaphoreType.DMA, jnp.bfloat16, jnp.float32
    block = lambda *lead: pltpu.VMEM(lead + (64, 1024), bf)
    shape = lambda *args: jax.ShapeDtypeStruct(*args)
    vmem, anywhere = pl.BlockSpec(memory_space=pltpu.VMEM), pl.BlockSpec(memory_space=pl.ANY)
    wide = pltpu.VMEM((128, 1024), f32)
    long = pltpu.VMEM((160, 1024), f32)
    half = lambda *lead: pltpu.VMEM(lead + (SPLIT,), bf)
    return pl.pallas_call(
        layer_kernel,
        out_shape=(
            shape((128, 1024), bf), shape((128, 1024), bf), shape((4, 2048), f32), shape((4, KERNEL), f32),
            shape((4, 64), f32), shape((1024, 1024), bf), shape((1024, 1024), bf),
        ),
        in_specs=[vmem, pl.BlockSpec(memory_space=pltpu.SMEM)] + [vmem] * 5 + [anywhere] * 2,
        out_specs=(vmem,) * 5 + (anywhere,) * 2,
        scratch_shapes=[
            pltpu.VMEM((4, 256, WIDE), bf), pltpu.VMEM((128, 1024), bf), wide, wide, wide, wide, long, wide,
            pltpu.VMEM((256, 1024), bf), pltpu.VMEM((256, 1024), bf),
            pltpu.VMEM((4, WIDE), bf), pltpu.VMEM((256, TALL), bf), pltpu.VMEM((256, 1024), bf),
            pltpu.VMEM((4, 4, 64, TALL), bf),
        ]
        + [block(4, 4)] * 4
        + [pltpu.VMEM((1024, 1024), bf)] * 2
        + [block(4, 4)] * 2
        + [block(4)] * 6
        + [pltpu.VMEM((2, 1024, 1024), bf), pltpu.VMEM((63, 4, TALL), bf)]
        + [wide, long, wide, pltpu.VMEM((128, 2048), bf), pltpu.VMEM((1024, 128), bf), wide]
        + [
            pltpu.VMEM((4, 256, WIDE), bf), pltpu.VMEM((4, 256, HALF), bf), half(2, 4, 256), half(2, 2, 128),
            half(2, 2, 256), half(2, 2, 64), half(2, 2, 32), half(2, 2, 64), pltpu.VMEM((8, 8, HALF), bf),
            pltpu.VMEM((16, 4, HALF), bf),
            pltpu.VMEM((256, 1024), f32),
        ]
        + [
            dma((2,)), dma, dma((16,)), dma((16,)), dma((16,)), dma((16,)), dma((8,)), dma((8,)),
            dma((4,)), dma((2, 4)), dma((2, 4)), dma((2, 4, 4)), dma((2, 4, 4)), dma((6, 4)), dma((6, 4)), dma((2,)),
            dma((2,)), dma((2,)), dma((8,)), dma((8,)), dma((24,)), dma((24,)), dma((16,)), dma((16,)),
        ],
        compiler_params=pltpu.CompilerParams(
            collective_id=2, has_side_effects=True, vmem_limit_bytes=VMEM_LIMIT
        ),
        name="layer",
    )(frames, lengths, ids, og, conv_in, router, depthwise, inner, outer)


def pass_kernel(*refs):
    sources, targets, bufs, sems = refs[:7], refs[7:14], refs[14:21], refs[21]
    loads, stores = [], []
    for i in range(7):
        for part in range(4 if i >= 5 else 1):
            pick = (lambda ref: ref) if i < 5 else (lambda ref: ref.at[pl.ds(part * 256, 256)])
            at = len(loads)
            loads.append(pltpu.make_async_copy(pick(sources[i]), pick(bufs[i]), sems.at[0, at]))
            stores.append(pltpu.make_async_copy(pick(bufs[i]), pick(targets[i]), sems.at[1, at]))
    order = list(range(5, 13)) + list(range(5))
    for at in order:
        loads[at].start()
    for at in order:
        loads[at].wait()
        stores[at].start()
    for at in order:
        stores[at].wait()


def pass_on(values):
    shapes = tuple(jax.ShapeDtypeStruct(value.shape, value.dtype) for value in values)
    anywhere = pl.BlockSpec(memory_space=pl.ANY)
    return pl.pallas_call(
        pass_kernel,
        out_shape=shapes,
        in_specs=[anywhere] * 7,
        out_specs=(anywhere,) * 7,
        scratch_shapes=[pltpu.VMEM(value.shape, value.dtype) for value in values] + [pltpu.SemaphoreType.DMA((2, 13))],
        compiler_params=pltpu.CompilerParams(vmem_limit_bytes=VMEM_LIMIT),
        name="pass_on",
    )(*values)


def per_device(frames, lengths, expert_ids, conv_in, depthwise, router, w_in, w_out, out_grad):
    *outs, w_in_grad, w_out_grad = pass_on(
        layer(frames, lengths, expert_ids.T, out_grad, conv_in, router, depthwise, w_in[0], w_out[0])
    )
    return (*outs, w_in_grad[None], w_out_grad[None])


def solution(mesh):
    in_specs = (
        P(("dp", "expert"), None),
        P(("dp", "expert")),
        P(("dp", "expert"), None),
        P(("dp", "expert"), None),
        P(("dp", "expert"), None),
        P(("dp", "expert"), None),
        P("expert", None, "dp"),
        P("expert", "dp", None),
        P(("dp", "expert"), None),
    )
    out_specs = (
        P(("dp", "expert"), None),
        P(("dp", "expert"), None),
        P(("dp", "expert"), None),
        P(("dp", "expert"), None),
        P(("dp", "expert"), None),
        P("expert", None, "dp"),
        P("expert", "dp", None),
    )
    return jax.shard_map(
        per_device, mesh=mesh, in_specs=in_specs, out_specs=out_specs, check_vma=False
    )
```

```python
import jax
import jax.numpy as jnp
from jax import lax
from jax.experimental import pallas as pl
from jax.experimental.pallas import tpu as pltpu
from jax.sharding import PartitionSpec as P

KERNEL = 31
EPSILON = 1e-05


def swish_of(values):
    return values * jax.nn.sigmoid(values)


def swish_slope(values):
    sigmoid_v = jax.nn.sigmoid(values)
    return sigmoid_v * (1.0 + values * (1.0 - sigmoid_v))


def normalize(values):
    center = values - jnp.mean(values, axis=-1, keepdims=True)
    inv_scale = lax.rsqrt(jnp.mean(center * center, axis=-1, keepdims=True) + EPSILON)
    return (center * inv_scale, inv_scale)


MESH = pl.DeviceIdType.MESH
HALF = 1152
WIDE = 2 * HALF
SPLIT = 640
VMEM_LIMIT = 60 * 1024 * 1024


def place():
    x = lax.axis_index("dp")
    e = lax.axis_index("expert")
    return x, e // 16, (e // 2) % 8, e % 2


def spot(x, y, z, c):
    return (x, y * 16 + z * 2 + c)


def remote(src, dst, send, recv, where):
    return pltpu.make_async_remote_copy(
        src_ref=src, dst_ref=dst, send_sem=send, recv_sem=recv, device_id=where, device_id_type=MESH
    )


STEPS = (0, 1, 3, 2)
TALL = 1152


def columns_of(n, width):
    return pl.ds(pl.multiple_of(n * width, width), width)


def mask_of(length_ref):
    return (lax.broadcasted_iota(jnp.int32, (128, 1), 0) < length_ref[0]).astype(jnp.float32)


def index_columns(ids_ref):
    shape = (128, 128)
    diagonal = lax.broadcasted_iota(jnp.int32, shape, 0) == lax.broadcasted_iota(jnp.int32, shape, 1)
    rows = ids_ref[...].astype(jnp.float32)
    return [jnp.sum(jnp.where(diagonal, rows[k : k + 1, :], 0.0), axis=1, keepdims=True) for k in (0, 1)]


def identity():
    shape = (128, 128)
    return (lax.broadcasted_iota(jnp.int32, shape, 0) == lax.broadcasted_iota(jnp.int32, shape, 1)).astype(jnp.bfloat16)


def layer_kernel(
    frames_ref, length_ref, ids_ref, og_ref, conv_in_ref, router_ref, depthwise_ref, inner_hbm, outer_hbm,
    layer_ref, frames_grad_ref, out_ref, depth_ref, router_grad_ref, inner_grad_hbm, outer_grad_hbm,
    full_ref, mixed_ref, value_ref, sig_ref, conv_ref, xhat_ref, gated_ref, taps_ref, y_ref, z_ref,
    own_ref, rows_buf, og_rows, slots, cots, scaled, active, pre, inner, outer, part_y, part_z, straight_y, straight_z,
    relay_y, relay_z, joint_y, joint_z, grad_buf, sized, mg_buf, cg_buf, tg_buf, pc_buf, turned, ng_buf,
    part_ref, swap_buf, half_buf, far_buf, near_buf, mid_buf, mid_far, mid_near, z_src, z_buf,
    slope_buf, load_sem, own_sem, z_s, z_r, gring_s, gring_r, tail_s, tail_r, self_s, there_s, there_r, ring_s,
    ring_r, fold_s, fold_r, back_s, back_r, store_sem, swap_s, swap_r, rring_s, rring_r, rz_s, rz_r
):
    x, y, z, c = place()
    f32, bf = jnp.float32, jnp.bfloat16
    here = y * 16 + z * 2 + c
    right, left, far = (x + 1) % 4, (x + 3) % 4, (x + 2) % 4
    to_right, to_left = spot(right, y, z, c), spot(left, y, z, c)
    loads = [
        pltpu.make_async_copy(inner_hbm, inner, load_sem.at[0]),
        pltpu.make_async_copy(outer_hbm, outer, load_sem.at[1]),
    ]
    for load in loads:
        load.start()

    barrier = pltpu.get_barrier_semaphore()

    def hail(i, carry):
        pl.semaphore_signal(barrier, inc=1, device_id=(x, (here + i) % 64), device_id_type=MESH)
        return carry

    lax.fori_loop(1, 64, hail, 0)
    for where in (to_right, to_left):
        pl.semaphore_signal(barrier, inc=1, device_id=where, device_id_type=MESH)

    own_ref[:, 0:2048] = conv_in_ref[...]
    own_ref[:, 2048:WIDE] = jnp.concatenate(
        [router_ref[...].astype(f32), depthwise_ref[...].astype(f32), jnp.zeros((4, WIDE - 2112 - KERNEL), f32)], axis=1
    ).astype(bf)
    mask = mask_of(length_ref)
    index = index_columns(ids_ref)
    lanes = lax.broadcasted_iota(jnp.int32, (128, 128), 1).astype(f32)
    picks = [lanes == column for column in index]
    count = (jnp.where(picks[0] | picks[1], 1.0, 0.0) * mask).astype(bf)
    shape = (128, 128)
    below = (lax.broadcasted_iota(jnp.int32, shape, 1) < lax.broadcasted_iota(jnp.int32, shape, 0)).astype(bf)
    before = jnp.dot(below, count, preferred_element_type=f32)
    wide = lax.broadcasted_iota(jnp.int32, (128, 256), 1).astype(f32)
    slot_of, spots = [], []
    for k, pick in enumerate(picks):
        position = jnp.sum(jnp.where(pick, before, 0.0), axis=1, keepdims=True)
        kept = (position < 4.0) & (mask > 0.0)
        slot = jnp.where(kept, index[k] * 4.0 + position, -1.0)
        slot_of.append(slot)
        spots.append((wide == slot).astype(bf))
    both = spots[0] + spots[1]
    down = (((0,), (0,)), ((), ()))

    def fill_og(n, carry):
        cols = columns_of(n, 256)
        og_rows[:, cols] = lax.dot_general(both, og_ref[:, cols], down, preferred_element_type=f32).astype(bf)
        return carry

    lax.fori_loop(0, 4, fill_og, 0)
    pl.semaphore_wait(barrier, 65)

    own4 = pl.multiple_of(4 * here, 4)
    line4 = pl.multiple_of(8 * z + 4 * c, 4)
    kinds = ((rows_buf, slots, TALL), (og_rows, cots, 1024))
    selfs = {}
    rings = {}

    def source_y(q):
        return (y + STEPS[q]) % 4

    def depart(kind, q):
        source, target, _ = kinds[kind]
        dy = STEPS[q]
        yt = (y + 4 - dy) % 4

        def there(i, carry):
            zt, ct = (z + 4 + i // 2) % 8, (c + i) % 2
            et = yt * 16 + zt * 2 + ct
            rows = pl.ds(pl.multiple_of(4 * et, 4), 4)
            remote(
                source.at[rows], target.at[x, y, pl.ds(line4, 4)], there_s.at[kind, q], there_r.at[kind, q], (x, et)
            ).start()
            return carry

        if dy == 0:
            lax.fori_loop(0, 8, there, 0)
            lax.fori_loop(9, 16, there, 0)
            selfs[kind] = pltpu.make_async_copy(
                source.at[pl.ds(own4, 4)], target.at[x, y, pl.ds(line4, 4)], self_s.at[kind]
            )
            selfs[kind].start()
        else:
            lax.fori_loop(0, 16, there, 0)

    def bulk(kind, q):
        return sized.at[pl.ds(0, 15 if STEPS[q] == 0 else 16), :, pl.ds(0, kinds[kind][2])]

    def arrive(kind, q):
        if STEPS[q] == 0:
            selfs[kind].wait()
        view = bulk(kind, q)
        remote(view, view, there_s.at[kind, q], there_r.at[kind, q], to_right).wait_recv()
        block = kinds[kind][1].at[x, source_y(q)]
        for side, where in ((0, to_right), (1, to_left)):
            copy = remote(block, block, ring_s.at[kind, side, q], ring_r.at[kind, side, q], where)
            copy.start()
            rings[kind, side, q] = copy

    def forward(kind, q):
        for side, at, where in ((0, left, to_right), (1, right, to_left)):
            rings[kind, side, q].wait_recv()
            block = kinds[kind][1].at[at, source_y(q), pl.ds(32 * side, 32)]
            copy = remote(block, block, ring_s.at[kind, 2 + side, q], ring_r.at[kind, 2 + side, q], where)
            copy.start()
            rings[kind, 2 + side, q] = copy

    partner = spot(x, y, z, 1 - c)
    mine = pl.multiple_of(c * HALF, 128)
    other = pl.multiple_of((1 - c) * HALF, 128)
    row = pl.multiple_of(y * 64 + z * 8, 8)
    row4 = pl.multiple_of(row + 4 * c, 4)
    keep = pltpu.make_async_copy(
        own_ref.at[:, pl.ds(mine, HALF)], full_ref.at[x, pl.ds(row4, 4), pl.ds(mine, HALF)], own_sem
    )
    keep.start()
    copies = []
    for dz in (4, 3, 5, 2, 6, 1, 7, 0):
        for dc, begin in ((0, mine), (1, other)):
            if dz or dc:
                at = 2 * dz + dc
                copy = remote(
                    own_ref.at[:, pl.ds(begin, HALF)],
                    full_ref.at[x, pl.ds(row4, 4), pl.ds(begin, HALF)],
                    z_s.at[at],
                    z_r.at[at],
                    spot(x, y, (z + dz) % 8, (c + dc) % 2),
                )
                copy.start()
                copies.append(copy)
    depart(1, 0)
    keep.wait()
    depart(1, 1)
    xhat, inv_scale = normalize(frames_ref[...].astype(f32))
    xhat_ref[...] = xhat
    zeros = jnp.zeros((16, 1024), f32)
    gated_ref[0:16, :] = zeros
    gated_ref[144:160, :] = zeros
    cg_buf[0:16, :] = zeros
    cg_buf[144:160, :] = zeros
    tg_buf[...] = jnp.zeros((128, 1024), f32)
    part_ref[:, :, 2176:2304] = jnp.zeros((4, 256, 128), bf)
    for copy in copies:
        copy.wait()

    first = pl.multiple_of(mine, 128)
    second = pl.multiple_of(mine + SPLIT, 128)
    yrow = pl.multiple_of(y * 64, 64)

    def block_of(colour, level, index, part):
        cols = pl.ds(first, SPLIT) if colour == 0 else pl.ds(second, HALF - SPLIT)
        if level == 0:
            height = 64 if part is None else 32
            offset = 0 if part is None else part * 32
            if colour == 0:
                return full_ref.at[x, pl.ds(pl.multiple_of(index * 64 + offset, 32), height), cols]
            return full_ref.at[index, pl.ds(pl.multiple_of(yrow + offset, 32), height), cols]
        if colour == 0:
            height = 256 if part is None else 128
            offset = 0 if part is None else part * 128
            return full_ref.at[index, pl.ds(offset, height), cols]
        height = 64 if part is None else 32
        offset = 0 if part is None else part * 32
        return full_ref.at[:, pl.ds(pl.multiple_of(index * 64 + offset, 32), height), cols]

    def whereto(colour, level, step):
        if (colour + level) % 2 == 0:
            return spot(x, (y + step) % 4, z, c)
        return spot((x + step) % 4, y, z, c)

    def position(colour, level):
        return y if (colour + level) % 2 == 0 else x

    def opened(colour, level):
        at = position(colour, level)
        block = block_of(colour, level, at, None)
        base = (colour * 2 + level) * 4
        right = remote(block, block, gring_s.at[base], gring_r.at[base], whereto(colour, level, 1))
        left = remote(block, block, gring_s.at[base + 1], gring_r.at[base + 1], whereto(colour, level, 3))
        right.start()
        left.start()
        return right, left

    def passed(colour, level, pair, tell):
        at = position(colour, level)
        base = (colour * 2 + level) * 4
        right, left = pair
        right.wait_recv()
        block = block_of(colour, level, (at + 3) % 4, 0)
        on_right = remote(block, block, gring_s.at[base + 2], gring_r.at[base + 2], whereto(colour, level, 1))
        on_right.start()
        tell((at + 3) % 4, 1)
        left.wait_recv()
        block = block_of(colour, level, (at + 1) % 4, 1)
        on_left = remote(block, block, gring_s.at[base + 3], gring_r.at[base + 3], whereto(colour, level, 3))
        on_left.start()
        tell((at + 1) % 4, 2)
        return on_right, on_left

    def closed(colour, level, pair, onward, tell):
        at = position(colour, level)
        for copy in onward:
            copy.wait_recv()
        tell((at + 2) % 4, 3)
        for copy in pair + onward:
            copy.wait_send()

    silent = lambda index, slot: None
    low = [opened(colour, 0) for colour in (0, 1)]
    arrive(1, 0)
    low_on = [passed(colour, 0, low[colour], silent) for colour in (0, 1)]
    depart(1, 2)
    for colour in (0, 1):
        closed(colour, 0, low[colour], low_on[colour], silent)
    tails = []

    def teller(colour):
        def tell(index, slot):
            block = block_of(colour, 1, index, None)
            at = colour * 4 + slot
            copy = remote(block, block, tail_s.at[at], tail_r.at[at], partner)
            copy.start()
            tails.append(copy)

        return tell

    high = [opened(colour, 1) for colour in (0, 1)]
    for colour in (0, 1):
        teller(colour)(position(colour, 1), 0)
    depart(1, 3)
    arrive(1, 1)
    high_on = [passed(colour, 1, high[colour], teller(colour)) for colour in (0, 1)]
    forward(1, 0)
    for colour in (0, 1):
        closed(colour, 1, high[colour], high_on[colour], teller(colour))
    arrive(1, 2)
    for copy in tails:
        copy.wait()
    forward(1, 1)
    arrive(1, 3)

    normed = xhat_ref[...].astype(bf)

    def point(n, carry):
        cols = columns_of(n, 256)
        value = jnp.dot(normed, full_ref[:, :, cols].reshape(1024, 256), preferred_element_type=f32)
        gate = jnp.dot(normed, full_ref[:, :, columns_of(n + 4, 256)].reshape(1024, 256), preferred_element_type=f32)
        sig = jax.nn.sigmoid(gate)
        value_ref[:, cols] = value
        sig_ref[:, cols] = sig
        gated_ref[16:144, cols] = value * sig * mask
        return carry

    lax.fori_loop(0, 4, point, 0)
    small = full_ref[:, :, 2048:2176].reshape(1024, 128)
    taps_ref[...] = lax.dot_general(identity(), small, (((1,), (1,)), ((), ())), preferred_element_type=f32)
    forward(1, 2)

    def depth(n, carry):
        cols = columns_of(n, 128)
        total = jnp.zeros((128, 128), f32)
        for k in range(KERNEL):
            total = total + taps_ref[64 + k : 65 + k, cols] * gated_ref[k + 1 : k + 129, cols]
        conv_ref[:, cols] = total
        mixed_ref[:, cols] = (frames_ref[:, cols].astype(f32) + swish_of(total) * mask).astype(bf)
        return carry

    lax.fori_loop(0, 8, depth, 0)
    logits = jnp.dot(mixed_ref[...], small, preferred_element_type=f32)
    scores = [jax.nn.sigmoid(jnp.sum(jnp.where(pick, logits, 0.0), axis=1, keepdims=True)) for pick in picks]
    score_sum = scores[0] + scores[1]
    weights = [score / score_sum for score in scores]
    lane = lax.broadcasted_iota(jnp.int32, shape, 1)
    def fill(n, carry):
        cols = columns_of(n, 256)
        rows_buf[:, cols] = lax.dot_general(both, mixed_ref[:, cols], down, preferred_element_type=f32).astype(bf)
        return carry

    lax.fori_loop(0, 4, fill, 0)
    total = jnp.zeros((256, 128), f32)
    for k in (0, 1):
        upper = weights[k].astype(bf).astype(f32)
        parts = jnp.where(lane == 0, upper, jnp.where(lane == 1, weights[k] - upper, 0.0)).astype(bf)
        total = total + lax.dot_general(spots[k], parts, down, preferred_element_type=f32)
    rows_buf[:, 1024:TALL] = total.astype(bf)
    for q in range(4):
        depart(0, q)
    forward(1, 3)

    folds = {}

    def push(name, q, source, target, where):
        copy = remote(source, target, fold_s.at[name, q], fold_r.at[name, q], where)
        copy.start()
        folds[name, q] = copy

    def compute(q):
        ys = source_y(q)
        for kind in (1, 0):
            for side in (2, 3):
                rings[kind, side, q].wait_recv()

        def scale(n, carry):
            parts = slots[n, ys, :, 1024:TALL].astype(f32)
            weight = parts[:, 0:1] + parts[:, 1:2]
            scaled[n, ys] = (cots[n, ys].astype(f32) * weight).astype(bf)
            return carry

        def hide(n, carry):
            cols = columns_of(n, 256)
            hidden = jnp.dot(slots[:, ys, :, 0:1024].reshape(256, 1024), inner[:, cols], preferred_element_type=f32)
            sig = jax.nn.sigmoid(hidden)
            active[:, ys, :, cols] = (hidden * sig).astype(bf).reshape(4, 64, 256)
            slope_buf[:, cols] = sig * (1.0 + hidden * (1.0 - sig))
            return carry

        lax.fori_loop(0, 4, hide, 0)

        def outward(n, carry):
            cols = columns_of(n, 256)
            out = jnp.dot(active[:, ys].reshape(256, 1024), outer[:, cols], preferred_element_type=f32)
            part_y[q, :, :, cols] = out.astype(bf).reshape(4, 64, 256)
            return carry

        lax.fori_loop(0, 4, outward, 0)
        push(2, q, part_y.at[q, far], relay_y.at[q], to_right)
        push(1, q, part_y.at[q, left], straight_y.at[q], to_left)
        lax.fori_loop(0, 4, scale, 0)

        def hide_back(n, carry):
            cols = columns_of(n, 256)
            act_grad = lax.dot_general(
                scaled[:, ys].reshape(256, 1024), outer[cols, :], (((1,), (1,)), ((), ())), preferred_element_type=f32
            )
            pre[:, ys, :, cols] = (act_grad * slope_buf[:, cols]).astype(bf).reshape(4, 64, 256)
            return carry

        lax.fori_loop(0, 4, hide_back, 0)

        def outward_back(n, carry):
            cols = columns_of(n, 256)
            out = lax.dot_general(
                pre[:, ys].reshape(256, 1024), inner[cols, :], (((1,), (1,)), ((), ())), preferred_element_type=f32
            )
            part_z[q, :, :, cols] = out.astype(bf).reshape(4, 64, 256)
            return carry

        lax.fori_loop(0, 4, outward_back, 0)
        push(3, q, part_z.at[q, far], relay_z.at[q], to_left)
        push(0, q, part_z.at[q, right], straight_z.at[q], to_right)

    def relay(q):
        folds[2, q].wait_recv()
        part_y[q, right] = (part_y[q, right].astype(f32) + relay_y[q].astype(f32)).astype(bf)
        push(4, q, part_y.at[q, right], joint_y.at[q], to_right)
        folds[3, q].wait_recv()
        part_z[q, left] = (part_z[q, left].astype(f32) + relay_z[q].astype(f32)).astype(bf)
        push(5, q, part_z.at[q, left], joint_z.at[q], to_left)

    def deliver(q):
        yt = source_y(q)
        for kind, (source, target, straight, joint, names) in enumerate(
            ((part_y, y_ref, straight_y, joint_y, (1, 4)), (part_z, z_ref, straight_z, joint_z, (0, 5)))
        ):
            for name in names:
                folds[name, q].wait_recv()
            source[q, x] = (source[q, x].astype(f32) + straight[q].astype(f32) + joint[q].astype(f32)).astype(bf)

            def back(i, carry, kind=kind, source=source, target=target):
                zt, ct = (z + 4 + i // 2) % 8, (c + i) % 2
                rows = pl.ds(pl.multiple_of(8 * zt + 4 * ct, 4), 4)
                remote(
                    source.at[q, x, rows], target.at[pl.ds(own4, 4)], back_s.at[kind], back_r.at[kind], (x, yt * 16 + zt * 2 + ct)
                ).start()
                return carry

            if STEPS[q] == 0:
                lax.fori_loop(0, 8, back, 0)
                lax.fori_loop(9, 16, back, 0)
                copy = pltpu.make_async_copy(
                    source.at[q, x, pl.ds(line4, 4)], target.at[pl.ds(own4, 4)], self_s.at[2 + kind]
                )
                copy.start()
                selfs[2 + kind] = copy
            else:
                lax.fori_loop(0, 16, back, 0)

    stores = []

    def weight_grad(which, left_ref, right_ref, target):
        def body(n, carry):
            cols = pl.ds(pl.multiple_of(n * 256, 256), 256)
            out = lax.dot_general(
                left_ref[:, :, :, cols].reshape(1024, 256),
                right_ref[...].reshape(1024, 1024),
                (((0,), (0,)), ((), ())),
                preferred_element_type=f32,
            )
            grad_buf[which, cols, :] = out.astype(bf)
            return carry

        lax.fori_loop(0, 4, body, 0)
        copy = pltpu.make_async_copy(grad_buf.at[which], target, store_sem.at[which])
        copy.start()
        stores.append(copy)

    for load in loads:
        load.wait()
    arrive(0, 0)
    arrive(0, 1)
    forward(0, 0)
    arrive(0, 2)
    forward(0, 1)
    arrive(0, 3)
    forward(0, 2)
    compute(0)
    forward(0, 3)
    compute(1)
    relay(0)
    compute(2)
    relay(1)
    deliver(0)
    compute(3)
    relay(2)
    turned[...] = jnp.transpose(xhat_ref[...]).astype(bf)
    deliver(1)
    weight_grad(1, active, scaled, outer_grad_hbm)
    relay(3)
    deliver(2)
    weight_grad(0, slots, pre, inner_grad_hbm)
    deliver(3)
    def returned(kind):
        view = sized.at[pl.ds(0, 63), :, pl.ds(0, 1024)]
        remote(view, view, back_s.at[kind], back_r.at[kind], to_right).wait()
        selfs[2 + kind].wait()

    returned(0)

    def output(n, carry):
        cols = columns_of(n, 256)
        og = og_ref[:, cols].astype(f32)
        total = jnp.zeros((128, 256), f32)
        sums = []
        for k in (0, 1):
            picked = jnp.dot(spots[k], y_ref[:, cols], preferred_element_type=f32)
            total = total + weights[k] * picked
            sums.append(carry[k] + jnp.sum(og * picked, axis=1, keepdims=True))
        layer_ref[:, cols] = (mixed_ref[:, cols].astype(f32) + total).astype(bf)
        return tuple(sums)

    start = jnp.zeros((128, 1), f32)
    weight_sums = lax.fori_loop(0, 4, output, (start, start))
    mean_term = weight_sums[0] * weights[0] + weight_sums[1] * weights[1]
    logit_grad = jnp.zeros((128, 128), f32)
    for k in (0, 1):
        chosen = (weight_sums[k] - mean_term) / score_sum * scores[k] * (1.0 - scores[k])
        logit_grad = jnp.where(picks[k], chosen, logit_grad)
    logit_grad = logit_grad.astype(bf)
    across = (((1,), (1,)), ((), ()))

    def mix(n, carry):
        cols = columns_of(n, 256)
        grad = og_ref[:, cols].astype(f32) + jnp.dot(both, z_ref[:, cols], preferred_element_type=f32)
        grad = grad + lax.dot_general(logit_grad, full_ref[n, :, 2048:2176], across, preferred_element_type=f32)
        mg_buf[:, cols] = grad
        cg_buf[16:144, cols] = grad * mask * swish_slope(conv_ref[:, cols])
        return carry

    returned(1)
    lax.fori_loop(0, 4, mix, 0)

    def depth_back(n, carry):
        cols = columns_of(n, 128)
        total = jnp.zeros((128, 128), f32)
        for k in range(KERNEL):
            total = total + taps_ref[64 + k : 65 + k, cols] * cg_buf[31 - k : 159 - k, cols]
        total = total * mask
        sig = sig_ref[:, cols]
        pc_buf[:, cols] = (total * sig).astype(bf)
        pc_buf[:, columns_of(n + 8, 128)] = (total * value_ref[:, cols] * sig * (1.0 - sig)).astype(bf)
        return carry

    lax.fori_loop(0, 8, depth_back, 0)

    def depth_taps(n, carry):
        cols = columns_of(n, 128)
        grad = cg_buf[16:144, cols]
        for k in range(KERNEL):
            tg_buf[64 + k : 65 + k, cols] = jnp.sum(grad * gated_ref[k + 1 : k + 129, cols], axis=0, keepdims=True)
        return carry

    def outer_product(i, carry):
        cols = columns_of((i + 9 * (1 - c)) % 16, 128)
        out = jnp.dot(turned[...], pc_buf[:, cols], preferred_element_type=f32)
        part_ref[:, :, cols] = out.astype(bf).reshape(4, 256, 128)
        return carry

    lax.fori_loop(0, 9, outer_product, 0)
    colours = ((0, SPLIT), (SPLIT, HALF - SPLIT))
    order = (2, 1, 3, 0)

    def rows_of(colour, index):
        if colour == 0:
            return index, pl.ds(0, 256)
        return slice(None), pl.ds(pl.multiple_of(index * 64, 64), 64)

    swaps = {}

    def swap_out(colour):
        begin, width = colours[colour]
        for step in order:
            at = ((x if colour == 0 else y) + step) % 4
            lead, rows = rows_of(colour, at)
            slot = colour * 4 + step
            copy = remote(
                part_ref.at[lead, rows, pl.ds(pl.multiple_of(other + begin, 128), width)],
                swap_buf.at[lead, rows, pl.ds(begin, width)],
                swap_s.at[slot],
                swap_r.at[slot],
                partner,
            )
            copy.start()
            swaps[colour, step] = copy

    swap_out(0)
    lax.fori_loop(0, 8, depth_taps, 0)
    out = lax.dot_general(mixed_ref[...], logit_grad, down, preferred_element_type=f32)
    out = out + lax.dot_general(tg_buf[...].astype(bf), identity(), down, preferred_element_type=f32)
    part_ref[:, :, 2048:2176] = out.astype(bf).reshape(4, 256, 128)
    swap_out(1)
    lax.fori_loop(9, 16, outer_product, 0)

    def inward(n, carry):
        cols = columns_of(n, 256)
        out = lax.dot_general(pc_buf[...], full_ref[n, :, 0:2048], across, preferred_element_type=f32)
        ng_buf[:, cols] = out
        first = carry[0] + jnp.sum(out, axis=1, keepdims=True)
        second = carry[1] + jnp.sum(out * xhat_ref[:, cols], axis=1, keepdims=True)
        return first, second

    def finish_frames():
        first, second = lax.fori_loop(0, 4, inward, (start, start))
        first, second = first * (1.0 / 1024), second * (1.0 / 1024)

        def finish(n, carry):
            cols = columns_of(n, 256)
            grad = inv_scale * (ng_buf[:, cols] - first - xhat_ref[:, cols] * second)
            frames_grad_ref[:, cols] = (mg_buf[:, cols] + grad).astype(bf)
            return carry

        lax.fori_loop(0, 4, finish, 0)

    def first_to(colour, step):
        if colour == 0:
            return spot((x + step) % 4, y, z, c)
        return spot(x, (y + step) % 4, z, c)

    def second_to(colour, step):
        return first_to(1 - colour, step)

    def fold(colour, step, extra):
        begin, width = colours[colour]
        at = ((x if colour == 0 else y) + step) % 4
        swaps[colour, step].wait_recv()

        def body(t, carry):
            if colour == 0:
                lead, row = at, pl.multiple_of(t * 32, 32)
            else:
                lead, row = t // 2, pl.multiple_of(at * 64 + (t % 2) * 32, 32)
            value = part_ref[lead, pl.ds(row, 32), pl.ds(pl.multiple_of(mine + begin, 128), width)].astype(jnp.float32)
            value = value + swap_buf[lead, pl.ds(row, 32), pl.ds(begin, width)].astype(jnp.float32)
            value = extra(t, value)
            half_buf[colour, step, pl.ds(pl.multiple_of(t * 32, 32), 32), pl.ds(0, width)] = value.astype(jnp.bfloat16)
            return carry

        return body

    plain = lambda t, value: value
    sent = []
    pend = {}
    for colour, (begin, width) in enumerate(colours):
        lax.fori_loop(0, 8, fold(colour, 2, plain), 0)
        for side, step in ((0, 1), (1, 3)):
            slot = colour * 12 + side
            copy = remote(
                half_buf.at[colour, 2, pl.ds(side * 128, 128), pl.ds(0, width)],
                far_buf.at[colour, side, :, pl.ds(0, width)],
                rring_s.at[slot],
                rring_r.at[slot],
                first_to(colour, step),
            )
            copy.start()
            pend[colour, side] = copy
            sent.append(copy)
    for colour, (begin, width) in enumerate(colours):
        for side, step in ((0, 1), (1, 3)):
            lax.fori_loop(4 - 4 * side, 8 - 4 * side, fold(colour, step, plain), 0)
            slot = colour * 12 + 8 + side
            rows = pl.ds(128 - 128 * side, 128)
            copy = remote(
                half_buf.at[colour, step, rows, pl.ds(0, width)],
                near_buf.at[colour, side, rows, pl.ds(0, width)],
                rring_s.at[slot],
                rring_r.at[slot],
                first_to(colour, step),
            )
            copy.start()
            pend[colour, 8 + side] = copy
            sent.append(copy)
    finish_frames()
    for colour, (begin, width) in enumerate(colours):
        for side, step in ((0, 1), (1, 3)):
            lo = side * 4
            pend[colour, side].wait_recv()

            def extra(t, value, colour=colour, side=side, lo=lo, width=width):
                row = pl.multiple_of((t - lo) * 32, 32)
                return value + far_buf[colour, side, pl.ds(row, 32), pl.ds(0, width)].astype(jnp.float32)

            def again(t, carry, colour=colour, step=step, extra=extra, begin=begin, width=width):
                at = ((x if colour == 0 else y) + step) % 4
                if colour == 0:
                    lead, row = at, pl.multiple_of(t * 32, 32)
                else:
                    lead, row = t // 2, pl.multiple_of(at * 64 + (t % 2) * 32, 32)
                value = part_ref[lead, pl.ds(row, 32), pl.ds(pl.multiple_of(mine + begin, 128), width)].astype(jnp.float32)
                value = value + swap_buf[lead, pl.ds(row, 32), pl.ds(begin, width)].astype(jnp.float32)
                value = extra(t, value)
                half_buf[colour, step, pl.ds(pl.multiple_of(t * 32, 32), 32), pl.ds(0, width)] = value.astype(jnp.bfloat16)
                return carry

            lax.fori_loop(lo, lo + 4, again, 0)
            slot = colour * 12 + 2 + side
            copy = remote(
                half_buf.at[colour, step, pl.ds(128 * side, 128), pl.ds(0, width)],
                near_buf.at[colour, side, pl.ds(128 * side, 128), pl.ds(0, width)],
                rring_s.at[slot],
                rring_r.at[slot],
                first_to(colour, step),
            )
            copy.start()
            pend[colour, 2 + side] = copy
            sent.append(copy)
    for colour, (begin, width) in enumerate(colours):
        for name in (8, 9, 2, 3):
            pend[colour, name].wait_recv()

        def extra(t, value, colour=colour, width=width):
            row = pl.multiple_of(t * 32, 32)
            for side in (0, 1):
                value = value + near_buf[colour, side, pl.ds(row, 32), pl.ds(0, width)].astype(jnp.float32)
            return value

        body = fold(colour, 0, extra)
        lax.fori_loop(0, 8, body, 0)
        at = y if colour == 0 else x
        for side, step in ((0, 1), (1, 3)):
            row = pl.multiple_of(((at + 2) % 4) * 64 + side * 32, 32)
            slot = colour * 12 + 4 + side
            copy = remote(
                half_buf.at[colour, 0, pl.ds(row, 32), pl.ds(0, width)],
                mid_far.at[colour, side, :, pl.ds(0, width)],
                rring_s.at[slot],
                rring_r.at[slot],
                second_to(colour, step),
            )
            copy.start()
            pend[colour, 4 + side] = copy
            sent.append(copy)
        for side, step in ((0, 1), (1, 3)):
            row = pl.multiple_of(((at + step) % 4) * 64 + 32 - 32 * side, 32)
            slot = colour * 12 + 10 + side
            copy = remote(
                half_buf.at[colour, 0, pl.ds(row, 32), pl.ds(0, width)],
                mid_near.at[colour, side, pl.ds(32 - 32 * side, 32), pl.ds(0, width)],
                rring_s.at[slot],
                rring_r.at[slot],
                second_to(colour, step),
            )
            copy.start()
            pend[colour, 10 + side] = copy
            sent.append(copy)
    for colour, (begin, width) in enumerate(colours):
        at = y if colour == 0 else x
        for side, step in ((0, 1), (1, 3)):
            row = pl.multiple_of(((at + step) % 4) * 64 + 32 * side, 32)
            pend[colour, 4 + side].wait_recv()
            value = half_buf[colour, 0, pl.ds(row, 32), pl.ds(0, width)].astype(f32)
            value = value + mid_far[colour, side, :, pl.ds(0, width)].astype(f32)
            mid_buf[colour, side, pl.ds(32 * side, 32), pl.ds(0, width)] = value.astype(bf)
            slot = colour * 12 + 6 + side
            copy = remote(
                mid_buf.at[colour, side, pl.ds(32 * side, 32), pl.ds(0, width)],
                mid_near.at[colour, side, pl.ds(32 * side, 32), pl.ds(0, width)],
                rring_s.at[slot],
                rring_r.at[slot],
                second_to(colour, step),
            )
            copy.start()
            pend[colour, 6 + side] = copy
            sent.append(copy)
    for colour, (begin, width) in enumerate(colours):
        at = y if colour == 0 else x
        for name in (10, 11, 6, 7):
            pend[colour, name].wait_recv()
        for piece in range(2):
            rows = pl.ds(piece * 32, 32)
            value = half_buf[colour, 0, pl.ds(pl.multiple_of(at * 64 + piece * 32, 32), 32), pl.ds(0, width)].astype(jnp.float32)
            for side in (0, 1):
                value = value + mid_near[colour, side, rows, pl.ds(0, width)].astype(jnp.float32)
            z_src[pl.ds(piece * 4, 4), :, pl.ds(begin, width)] = value.astype(jnp.bfloat16).reshape(4, 8, width)
    z_copies = []
    for dz in (4, 3, 5, 2, 6, 1, 7, 0):
        for dc in (0, 1):
            if dz or dc:
                to, core = (z + dz) % 8, (c + dc) % 2
                at = 2 * dz + dc
                copy = remote(
                    z_src.at[to, pl.ds(pl.multiple_of(4 * core, 4), 4)], z_buf.at[at], rz_s.at[at], rz_r.at[at], spot(x, y, to, core)
                )
                copy.start()
                z_copies.append(copy)
    own8 = z_src[z].astype(f32)
    kept = jnp.where(c == 0, own8[0:4, :], own8[4:8, :])
    for copy in z_copies:
        copy.wait_recv()
    got = jnp.zeros((4, HALF), f32)
    for dz in range(8):
        if dz:
            kept = kept + z_buf[2 * dz].astype(f32)
        got = got + z_buf[2 * dz + 1].astype(f32)
    for copy in sent + z_copies:
        copy.wait_send()
    for copy in swaps.values():
        copy.wait_send()
    low, high = jnp.where(c == 0, kept, got), jnp.where(c == 0, got, kept)
    out_ref[:, 0:HALF] = low
    out_ref[:, HALF:2048] = high[:, 0 : 2048 - HALF]
    router_grad_ref[...] = high[:, 2048 - HALF : 2112 - HALF]
    depth_ref[...] = high[:, 2112 - HALF : 2112 + KERNEL - HALF]
    for kind in (0, 1):
        for q in range(4):
            view = bulk(kind, q)
            remote(view, view, there_s.at[kind, q], there_r.at[kind, q], to_right).wait_send()
    for copy in list(rings.values()) + list(folds.values()):
        copy.wait_send()
    for copy in stores:
        copy.wait()


def layer(frames, lengths, ids, og, conv_in, router, depthwise, inner, outer):
    dma, bf, f32 = pltpu.SemaphoreType.DMA, jnp.bfloat16, jnp.float32
    block = lambda *lead: pltpu.VMEM(lead + (64, 1024), bf)
    shape = lambda *args: jax.ShapeDtypeStruct(*args)
    vmem, anywhere = pl.BlockSpec(memory_space=pltpu.VMEM), pl.BlockSpec(memory_space=pl.ANY)
    wide = pltpu.VMEM((128, 1024), f32)
    long = pltpu.VMEM((160, 1024), f32)
    half = lambda *lead: pltpu.VMEM(lead + (SPLIT,), bf)
    return pl.pallas_call(
        layer_kernel,
        out_shape=(
            shape((128, 1024), bf), shape((128, 1024), bf), shape((4, 2048), f32), shape((4, KERNEL), f32),
            shape((4, 64), f32), shape((1024, 1024), bf), shape((1024, 1024), bf),
        ),
        in_specs=[vmem, pl.BlockSpec(memory_space=pltpu.SMEM)] + [vmem] * 5 + [anywhere] * 2,
        out_specs=(vmem,) * 5 + (anywhere,) * 2,
        scratch_shapes=[
            pltpu.VMEM((4, 256, WIDE), bf), pltpu.VMEM((128, 1024), bf), wide, wide, wide, wide, long, wide,
            pltpu.VMEM((256, 1024), bf), pltpu.VMEM((256, 1024), bf),
            pltpu.VMEM((4, WIDE), bf), pltpu.VMEM((256, TALL), bf), pltpu.VMEM((256, 1024), bf),
            pltpu.VMEM((4, 4, 64, TALL), bf),
        ]
        + [block(4, 4)] * 4
        + [pltpu.VMEM((1024, 1024), bf)] * 2
        + [block(4, 4)] * 2
        + [block(4)] * 6
        + [pltpu.VMEM((2, 1024, 1024), bf), pltpu.VMEM((63, 4, TALL), bf)]
        + [wide, long, wide, pltpu.VMEM((128, 2048), bf), pltpu.VMEM((1024, 128), bf), wide]
        + [
            pltpu.VMEM((4, 256, WIDE), bf), pltpu.VMEM((4, 256, HALF), bf), half(2, 4, 256), half(2, 2, 128),
            half(2, 2, 256), half(2, 2, 64), half(2, 2, 32), half(2, 2, 64), pltpu.VMEM((8, 8, HALF), bf),
            pltpu.VMEM((16, 4, HALF), bf),
            pltpu.VMEM((256, 1024), f32),
        ]
        + [
            dma((2,)), dma, dma((16,)), dma((16,)), dma((16,)), dma((16,)), dma((8,)), dma((8,)),
            dma((4,)), dma((2, 4)), dma((2, 4)), dma((2, 4, 4)), dma((2, 4, 4)), dma((6, 4)), dma((6, 4)), dma((2,)),
            dma((2,)), dma((2,)), dma((8,)), dma((8,)), dma((24,)), dma((24,)), dma((16,)), dma((16,)),
        ],
        compiler_params=pltpu.CompilerParams(
            collective_id=2, has_side_effects=True, vmem_limit_bytes=VMEM_LIMIT
        ),
        name="layer",
    )(frames, lengths, ids, og, conv_in, router, depthwise, inner, outer)


def pass_kernel(*refs):
    sources, targets, bufs, sems = refs[:7], refs[7:14], refs[14:21], refs[21]
    loads, stores = [], []
    for i in range(7):
        for part in range(4 if i >= 5 else 1):
            pick = (lambda ref: ref) if i < 5 else (lambda ref: ref.at[pl.ds(part * 256, 256)])
            at = len(loads)
            loads.append(pltpu.make_async_copy(pick(sources[i]), pick(bufs[i]), sems.at[0, at]))
            stores.append(pltpu.make_async_copy(pick(bufs[i]), pick(targets[i]), sems.at[1, at]))
    order = list(range(5, 13)) + list(range(5))
    for at in order:
        loads[at].start()
    for at in order:
        loads[at].wait()
        stores[at].start()
    for at in order:
        stores[at].wait()


def pass_on(values):
    shapes = tuple(jax.ShapeDtypeStruct(value.shape, value.dtype) for value in values)
    anywhere = pl.BlockSpec(memory_space=pl.ANY)
    return pl.pallas_call(
        pass_kernel,
        out_shape=shapes,
        in_specs=[anywhere] * 7,
        out_specs=(anywhere,) * 7,
        scratch_shapes=[pltpu.VMEM(value.shape, value.dtype) for value in values] + [pltpu.SemaphoreType.DMA((2, 13))],
        compiler_params=pltpu.CompilerParams(vmem_limit_bytes=VMEM_LIMIT),
        name="pass_on",
    )(*values)


def per_device(frames, lengths, expert_ids, conv_in, depthwise, router, w_in, w_out, out_grad):
    *outs, w_in_grad, w_out_grad = pass_on(
        layer(frames, lengths, expert_ids.T, out_grad, conv_in, router, depthwise, w_in[0], w_out[0])
    )
    return (*outs, w_in_grad[None], w_out_grad[None])


def solution(mesh):
    in_specs = (
        P(("dp", "expert"), None),
        P(("dp", "expert")),
        P(("dp", "expert"), None),
        P(("dp", "expert"), None),
        P(("dp", "expert"), None),
        P(("dp", "expert"), None),
        P("expert", None, "dp"),
        P("expert", "dp", None),
        P(("dp", "expert"), None),
    )
    out_specs = (
        P(("dp", "expert"), None),
        P(("dp", "expert"), None),
        P(("dp", "expert"), None),
        P(("dp", "expert"), None),
        P(("dp", "expert"), None),
        P("expert", None, "dp"),
        P("expert", "dp", None),
    )
    return jax.shard_map(
        per_device, mesh=mesh, in_specs=in_specs, out_specs=out_specs, check_vma=False
    )
```
